256 devices in a mesh: az: 8 (over z), rng: 8 (over y_lo, x), dp: 4 (over y_hi, core).
Axes of the slice: x: 4, y: 4 (y_hi: 2, y_lo: 2; y = y_hi * 2 + y_lo), z: 8, core: 2. Of those that a mesh axis runs over, the one named last changes fastest.
Arguments:
- tokens: bfloat16 [4, 128, 128, 512], P('dp', 'az', 'rng'), may hold values from -6 to 6
- qkv_weight: bfloat16 [512, 1536], replicated, may hold values from -0.25 to 0.25
- out_weight: bfloat16 [512, 512], replicated, may hold values from -0.25 to 0.25
- relative_bias: float32 [8, 17, 17], replicated, may hold values from -4 to 260
- cotangent: bfloat16 [4, 128, 128, 512], P('dp', 'az', 'rng'), may hold values from -6 to 6
Outputs:
- grad_tokens: bfloat16 [4, 128, 128, 512], P('dp', 'az', 'rng')
- grad_qkv_weight: float32 [512, 1536], P(('az', 'rng'))
- grad_out_weight: float32 [512, 512], P(('az', 'rng'))
- grad_bias: float32 [8, 17, 17], replicated
The draws below stay inside these ranges and needn't reach their ends.
All inputs are finite; a program needn't handle non-finite values.
Results may differ from the reference program's by a relative error of at most 0.012.
Values may be sent and summed in bfloat16 or wider, within the bound.
No kernel may reach another device: no remote copies, remote signals or barrier semaphores. Data moves between devices by JAX's collectives and lax.ppermute only.
A program may use at most 128 MiB of HBM per device.

```python
import math
import jax
import jax.numpy as jnp
from jax import lax

D = 512
HEADS = 8
SPAN = 17
NA = 128
NR = 128
BATCH = 4


def draw_relative_bias(key, part):
    shape_key = jax.random.fold_in(key, 0)
    cell_count = SPAN * SPAN
    flat_base = jnp.clip(jax.random.normal(shape_key, (HEADS, cell_count), jnp.float32), -4.0, 4.0)
    return flat_base.reshape(HEADS, SPAN, SPAN)


def level_of(key, shape, cuts, low, top_value):
    level, own = 1.0, jax.random.fold_in(key, 6)
    for axis_at, shards_of in cuts:
        heights = jnp.exp(jax.random.uniform(jax.random.fold_in(own, axis_at), (shards_of,), jnp.float32, low / len(cuts), top_value / len(cuts)))
        level = level * jnp.repeat(heights, shape[axis_at] // shards_of).reshape([-1 if axis == axis_at else 1 for axis in range(len(shape))])
    return level


def centred(rng, shape, spread, reach, cuts=(), kind=jnp.bfloat16):
    loudness = level_of(rng, shape, cuts, -0.22, 0.18) if cuts else 1.0
    drawn = jax.random.normal(rng, shape, jnp.float32) * spread * loudness
    return jnp.minimum(jnp.maximum(drawn, -reach), reach).astype(kind)


def setup_inputs(seed: int = 0) -> dict:
    key_list = jax.random.split(jax.random.key(seed), 6)
    return {
        "tokens": centred(key_list[0], (BATCH, NA, NR, D), 1.0, 6.0, ((0, 4), (1, 8), (2, 8))),
        "qkv_weight": centred(key_list[1], (D, 3 * D), D ** -0.5, 0.25),
        "out_weight": centred(key_list[2], (D, D), D ** -0.5, 0.25),
        "relative_bias": draw_relative_bias(jax.random.fold_in(key_list[5], 71), 0),
        "cotangent": centred(key_list[4], (BATCH, NA, NR, D), 1.0, 6.0, ((0, 4), (1, 8), (2, 8))),
    }


def starts(*values):
    return tuple((jnp.asarray(value).astype(jnp.int32) for value in values))

def selector(length, radius, present):
    span = 2 * radius + 1
    inner = jnp.arange(length)[:, None, None]
    outer = jnp.arange(length + 2 * radius)[None, :, None]
    offset = jnp.arange(span)[None, None, :]
    return ((outer - inner == offset) & present[None, :, None]).astype(jnp.float32)

def window(table, along, across):
    heads = table.shape[0]
    part_bias = jnp.einsum('hxy,jly->hxjl', table, across, precision=lax.Precision.HIGHEST)
    full_bias = jnp.einsum('ikx,hxjl->hijkl', along, part_bias, precision=lax.Precision.HIGHEST)
    row_total = along.shape[0] * across.shape[0]
    col_total = along.shape[1] * across.shape[1]
    inside = lax.optimization_barrier(jnp.sum(along, axis=2))[:, None, :, None] * lax.optimization_barrier(jnp.sum(across, axis=2))[None, :, None, :] > 0.5
    return (full_bias.reshape(heads, row_total, col_total), inside.reshape(row_total, col_total))

def bias_grad(d_score, along, across):
    heads = d_score.shape[0]
    shaped = d_score.reshape(heads, along.shape[0], across.shape[0], along.shape[1], across.shape[1])
    folded = jnp.einsum('hijkl,ikx->hxjl', shaped, along, precision=lax.Precision.HIGHEST)
    return jnp.einsum('hxjl,jly->hxy', folded, across, precision=lax.Precision.HIGHEST)

def query_side(queries, d_attended, key_rows, value_rows, bias, inside, scale):
    score = jnp.einsum('qhc,khc->hqk', queries.astype(jnp.float32), key_rows.astype(jnp.float32)) * scale + bias
    score = jnp.where(inside[None], score, -jnp.inf)
    top = lax.optimization_barrier(jnp.max(score, axis=2, keepdims=True))
    log_total = top + jnp.log(lax.optimization_barrier(jnp.sum(jnp.exp(score - top), axis=2, keepdims=True)))
    soft_prob = jnp.exp(score - log_total)
    prob_low = lax.optimization_barrier(soft_prob.astype(jnp.bfloat16))
    attended = jnp.einsum('hqk,khc->qhc', prob_low.astype(jnp.float32), value_rows.astype(jnp.float32)).astype(jnp.bfloat16)
    attended_wide = lax.optimization_barrier(attended).astype(jnp.float32)
    delta = jnp.einsum('qhc,qhc->hq', d_attended.astype(jnp.float32), attended_wide)
    d_prob = jnp.einsum('qhc,khc->hqk', d_attended.astype(jnp.float32), value_rows.astype(jnp.float32))
    d_score = soft_prob * (d_prob - delta[:, :, None])
    score_low = lax.optimization_barrier(d_score.astype(jnp.bfloat16))
    d_query = (jnp.einsum('hqk,khc->qhc', score_low.astype(jnp.float32), key_rows.astype(jnp.float32)) * scale).astype(jnp.bfloat16)
    return (attended, log_total[:, :, 0], delta, d_query, d_score)

def key_side(key_rows, value_rows, queries, d_attended, log_total, delta, bias, inside, scale):
    score = jnp.einsum('khc,qhc->hkq', key_rows.astype(jnp.float32), queries.astype(jnp.float32)) * scale + bias
    score = jnp.where(inside[None], score, -jnp.inf)
    soft_prob = jnp.exp(score - log_total[:, None, :])
    prob_low = lax.optimization_barrier(soft_prob.astype(jnp.bfloat16))
    d_prob = jnp.einsum('khc,qhc->hkq', value_rows.astype(jnp.float32), d_attended.astype(jnp.float32))
    d_score = soft_prob * (d_prob - delta[:, None, :])
    score_low = lax.optimization_barrier(d_score.astype(jnp.bfloat16))
    d_key = (jnp.einsum('hkq,qhc->khc', score_low.astype(jnp.float32), queries.astype(jnp.float32)) * scale).astype(jnp.bfloat16)
    d_value = jnp.einsum('hkq,qhc->khc', prob_low.astype(jnp.float32), d_attended.astype(jnp.float32)).astype(jnp.bfloat16)
    return (d_key, d_value)

def reference(tokens, qkv_weight, out_weight, relative_bias, cotangent):
    sweeps, azimuth, radial, width = tokens.shape
    heads = relative_bias.shape[0]
    radius = relative_bias.shape[1] // 2
    head_dim = width // heads
    scale = 1.0 / math.sqrt(head_dim)
    tile = 8
    count_all = sweeps * azimuth * radial
    flat_tokens = tokens.reshape(count_all, width)
    flat_cot = cotangent.reshape(count_all, width)
    projected = jnp.dot(flat_tokens, qkv_weight, preferred_element_type=jnp.float32).astype(jnp.bfloat16)
    projected = projected.reshape(sweeps, azimuth, radial, 3 * width)
    queries = projected[..., :width]
    key_value = projected[..., width:]
    d_attended = lax.dot_general(flat_cot, out_weight, (((1,), (1,)), ((), ())), preferred_element_type=jnp.float32)
    d_attended = d_attended.astype(jnp.bfloat16).reshape(sweeps, azimuth, radial, width)

    def extend(field):
        wrapped = jnp.concatenate([field[:, azimuth - radius:], field, field[:, :radius]], axis=1)
        return jnp.pad(wrapped, ((0, 0), (0, 0), (radius, radius), (0, 0)))
    key_ext = extend(key_value)
    tiles_az = azimuth // tile
    tiles_rg = radial // tile
    tile_count = sweeps * tiles_az * tiles_rg
    ext_side = tile + 2 * radius
    along = selector(tile, radius, jnp.ones((ext_side,), dtype=bool))

    def locate(counter):
        sweep_at = counter // (tiles_az * tiles_rg)
        leftover = counter % (tiles_az * tiles_rg)
        return (sweep_at, leftover // tiles_rg * tile, leftover % tiles_rg * tile)

    def across_of(col_at):
        column = col_at - radius + jnp.arange(ext_side)
        return selector(tile, radius, (column >= 0) & (column < radial))

    def query_tile(counter):
        sweep_at, row_at, col_at = locate(counter)
        place = starts(sweep_at, row_at, col_at, 0)
        query_block = lax.dynamic_slice(queries, place, (1, tile, tile, width)).reshape(tile * tile, heads, head_dim)
        cot_block = lax.dynamic_slice(d_attended, place, (1, tile, tile, width)).reshape(tile * tile, heads, head_dim)
        pair_block = lax.dynamic_slice(key_ext, place, (1, ext_side, ext_side, 2 * width)).reshape(ext_side * ext_side, 2, heads, head_dim)
        across = across_of(col_at)
        bias, inside = window(relative_bias, along, across)
        attended, log_total, delta, d_query, d_score = query_side(query_block, cot_block, pair_block[:, 0], pair_block[:, 1], bias, inside, scale)
        return (attended.reshape(tile * tile, width), log_total.T, delta.T, d_query.reshape(tile * tile, width), bias_grad(d_score, along, across))
    group = math.gcd(tile_count, 64)

    def run_tiles(func):
        lanes = jnp.arange(tile_count, dtype=jnp.int32).reshape(tile_count // group, group)
        results = lax.map(jax.vmap(func), lanes)
        return jax.tree.map(lambda leaf: leaf.reshape((tile_count,) + leaf.shape[2:]), results)

    def untile(leaf):
        last = leaf.shape[-1]
        shaped = leaf.reshape(sweeps, tiles_az, tiles_rg, tile, tile, last)
        return shaped.transpose(0, 1, 3, 2, 4, 5).reshape(sweeps, azimuth, radial, last)
    attended_all, log_all, delta_all, dquery_all, bias_terms = run_tiles(query_tile)
    attended_all = untile(attended_all)
    log_all = untile(log_all)
    delta_all = untile(delta_all)
    dquery_all = untile(dquery_all)
    grad_bias = lax.optimization_barrier(jnp.sum(bias_terms, axis=0))
    pair_ext = extend(jnp.concatenate([queries, d_attended], axis=3))
    stats_ext = extend(jnp.concatenate([log_all, delta_all], axis=3))
    flipped = relative_bias[:, ::-1, ::-1]

    def key_tile(counter):
        sweep_at, row_at, col_at = locate(counter)
        place = starts(sweep_at, row_at, col_at, 0)
        own = lax.dynamic_slice(key_value, place, (1, tile, tile, 2 * width)).reshape(tile * tile, 2, heads, head_dim)
        near = lax.dynamic_slice(pair_ext, place, (1, ext_side, ext_side, 2 * width)).reshape(ext_side * ext_side, 2, heads, head_dim)
        near_stats = lax.dynamic_slice(stats_ext, place, (1, ext_side, ext_side, 2 * heads)).reshape(ext_side * ext_side, 2 * heads)
        across = across_of(col_at)
        bias, inside = window(flipped, along, across)
        d_key, d_value = key_side(own[:, 0], own[:, 1], near[:, 0], near[:, 1], near_stats[:, :heads].T, near_stats[:, heads:].T, bias, inside, scale)
        return jnp.stack([d_key, d_value], axis=1).reshape(tile * tile, 2 * width)
    grad_pair = untile(run_tiles(key_tile))
    grad_qkv = jnp.concatenate([dquery_all, grad_pair], axis=3)
    grad_flat = grad_qkv.reshape(count_all, 3 * width)
    grad_tokens = lax.dot_general(grad_flat, qkv_weight, (((1,), (1,)), ((), ())), preferred_element_type=jnp.float32)
    grad_tokens = grad_tokens.astype(jnp.bfloat16).reshape(sweeps, azimuth, radial, width)
    grad_qkv_weight = lax.dot_general(flat_tokens, grad_flat, (((0,), (0,)), ((), ())), preferred_element_type=jnp.float32)
    grad_out_weight = lax.dot_general(attended_all.reshape(count_all, width), flat_cot, (((0,), (0,)), ((), ())), preferred_element_type=jnp.float32)
    return (grad_tokens, grad_qkv_weight, grad_out_weight, grad_bias)
```

```python
import functools
import math

import jax
import jax.numpy as jnp
from jax import lax
from jax.experimental import pallas as pl
from jax.experimental.pallas import tpu as pltpu
from jax.sharding import PartitionSpec as P

F32 = jnp.float32
BF16 = jnp.bfloat16
ABSENT = -1e30
NT = (((1,), (1,)), ((), ()))
VMEM_BYTES = 60 * 1024 * 1024


def dot(a, b, dims=(((1,), (0,)), ((), ()))):
    return lax.dot_general(a, b, dims, preferred_element_type=F32)


def row_slots(row):
    base = row // 8 * 256
    at = row % 8
    return (
        (0, 8, base + at * 8),
        (8, 24, base + 64 + at * 16),
        (24, 32, base + 192 + at * 8),
    )


def before_kernel(edge, x, cot, wt, wo, rows, q, q_t, da, da_t, table):
    xv = x[...]
    cv = cot[...]
    q[...] = (dot(xv, wt[0:512], NT).astype(BF16).astype(F32) * 0.125).astype(BF16)
    q_t[...] = (dot(wt[0:512], xv, NT).astype(BF16).astype(F32) * 0.125).astype(BF16)
    da[...] = dot(cv, wo[...], NT).astype(BF16)
    da_t[...] = dot(wo[...], cv, NT).astype(BF16)
    range_row = lax.broadcasted_iota(jnp.int32, (32, 512), 0)
    lane = lax.broadcasted_iota(jnp.int32, (32, 512), 1)
    gap = range_row - (lane & 15)
    first = jnp.where(edge[0] == 1, 8, 0)
    last = jnp.where(edge[1] == 1, 24, 32)
    present = (range_row >= first) & (range_row < last)

    def pair_step(pair, carry):
        for side in range(2):
            head_rows = rows[pair * 2 + side]
            spread = jnp.full((32, 512), ABSENT, F32)
            for j in range(17):
                spread = jnp.where(gap == j, head_rows[j : j + 1], spread)
            spread = jnp.where(present, spread, ABSENT)
            for v in range(8):
                turned = spread if v == 0 else pltpu.roll(spread, 512 - 16 * v, 1)
                for u in range(3):
                    block = turned[:, 128 * u : 128 * u + 128]
                    for low, high, at in row_slots(23 - 8 * u - v):
                        table[pair, at : at + high - low, side * 128 : side * 128 + 128] = block[
                            low:high
                        ]
        return carry

    lax.fori_loop(0, 4, pair_step, 0)


def main_kernel(
    core, own, top, bottom, left, right, tl, tr, bl, br, q, q_t, da, da_t, table, wt, cot,
    grad_own, g_top, g_bottom, g_left, g_right, g_tl, g_tr, g_bl, g_br, g_keep, g_send, g_bias,
    xs, k, v, k_t, v_t, dkv, att_t, dq_t, dsum, brow,
):
    pieces = (
        (tl, 0, 64, 0), (top, 0, 128, 64), (tr, 0, 64, 192),
        (left, 0, 64, 256), (own, 0, 128, 320), (right, 0, 64, 448),
        (left, 64, 64, 512), (own, 128, 128, 576), (right, 64, 64, 704),
        (bl, 0, 64, 768), (bottom, 0, 128, 832), (br, 0, 64, 960),
    )
    for ref, at, size, to in pieces:
        xs[to : to + size] = ref[at : at + size]

    def project(g, carry):
        at = pl.multiple_of(g * 256, 256)
        block = xs[pl.ds(at, 256)]
        k[pl.ds(at, 256)] = dot(block, wt[512:1024], NT).astype(BF16)
        v[pl.ds(at, 256)] = dot(block, wt[1024:1536], NT).astype(BF16)
        k_t[:, pl.ds(at, 256)] = dot(wt[512:1024], block, NT).astype(BF16)
        v_t[:, pl.ds(at, 256)] = dot(wt[1024:1536], block, NT).astype(BF16)
        return carry

    lax.fori_loop(0, 4, project, 0)

    upper_rows = lax.broadcasted_iota(jnp.int32, (128, 128), 0) < 64
    upper_lanes = lax.broadcasted_iota(jnp.int32, (128, 128), 1) < 64
    gap = lax.broadcasted_iota(jnp.int32, (32, 512), 0) - (
        lax.broadcasted_iota(jnp.int32, (32, 512), 1) & 15
    )

    def split_lanes(block):
        zero = jnp.zeros_like(block)
        return jnp.concatenate(
            [jnp.where(upper_rows, block, zero), jnp.where(upper_rows, zero, block)], axis=1
        )

    def split_rows(block):
        zero = jnp.zeros_like(block)
        return jnp.concatenate(
            [jnp.where(upper_lanes, block, zero), jnp.where(upper_lanes, zero, block)], axis=0
        )

    def pair_step(pair, carry):
        at = pl.multiple_of(pair * 128, 128)
        cols = pl.ds(at, 128)
        tails = []
        for t in range(2):
            keys = slice(t * 256, t * 256 + 768)
            mine = slice(t * 128, t * 128 + 128)
            score = dot(k[keys, cols], split_lanes(q_t[cols, mine])) + table[pair]
            top_score = jnp.max(score, axis=0, keepdims=True)
            weight = jnp.exp(score - top_score)
            prob = weight * (1.0 / jnp.sum(weight, axis=0, keepdims=True))
            prob_low = prob.astype(BF16)
            mixed = dot(v_t[cols, keys], prob_low)
            att = jnp.where(upper_rows, mixed[:, :128], mixed[:, 128:]).astype(BF16)
            att_t[cols, mine] = att
            da_block = da_t[cols, mine]
            product = att.astype(F32) * da_block.astype(F32)
            delta = jnp.concatenate(
                [
                    jnp.sum(product[:64], axis=0, keepdims=True),
                    jnp.sum(product[64:], axis=0, keepdims=True),
                ],
                axis=1,
            )
            d_score = prob * (dot(v[keys, cols], split_lanes(da_block)) - delta)
            if t == 0:
                dsum[...] = d_score
            else:
                dsum[...] += d_score
            score_low = d_score.astype(BF16)
            d_q = dot(k_t[cols, keys], score_low)
            dq_t[cols, mine] = (
                jnp.where(upper_rows, d_q[:, :128], d_q[:, 128:]) * 0.125
            ).astype(BF16)
            tails.append(
                (
                    dot(score_low, split_rows(q[mine, cols])),
                    dot(prob_low, split_rows(da[mine, cols])),
                )
            )
        for which in range(2):
            early, late = tails[0][which], tails[1][which]
            to = pl.ds(pl.multiple_of(which * 512 + at, 128), 128)
            dkv[0:256, to] = early[0:256].astype(BF16)
            dkv[256:768, to] = (early[256:768] + late[0:512]).astype(BF16)
            dkv[768:1024, to] = late[512:768].astype(BF16)
        for side in range(2):
            lanes = slice(side * 128, side * 128 + 128)
            total = None
            for turn in range(8):
                parts = [
                    jnp.concatenate(
                        [
                            dsum[to : to + high - low, lanes]
                            for low, high, to in row_slots(23 - 8 * u - turn)
                        ],
                        axis=0,
                    )
                    for u in range(3)
                ]
                strip = jnp.concatenate(parts + [jnp.zeros((32, 128), F32)], axis=1)
                if turn:
                    strip = pltpu.roll(strip, 16 * turn, 1)
                total = strip if total is None else total + strip
            for j in range(17):
                brow[pair * 2 + side, j : j + 1] = jnp.sum(
                    jnp.where(gap == j, total, 0.0), axis=0, keepdims=True
                )
            brow[pair * 2 + side, 17:24] = jnp.zeros((7, 512), F32)
        return carry

    lax.fori_loop(0, 4, pair_step, 0)

    fold = (
        lax.broadcasted_iota(jnp.int32, (512, 128), 0) // 16
        == lax.broadcasted_iota(jnp.int32, (512, 128), 1)
    ).astype(F32)
    folded = lax.dot_general(
        brow[...].reshape(192, 512), fold, (((1,), (0,)), ((), ())),
        precision=lax.Precision.HIGHEST, preferred_element_type=F32,
    )
    g_bias[...] = folded.reshape(8, 24, 128)

    x_t = xs[...].T
    own_t = jnp.concatenate([x_t[:, 320:448], x_t[:, 576:704]], axis=1)

    def hand_out(start, value):
        half, lanes = start // 1024, slice(start % 1024, start % 1024 + value.shape[1])
        value = value.astype(BF16)

        @pl.when(core[0] == half)
        def _():
            g_keep[:, lanes] = value

        @pl.when(core[0] != half)
        def _():
            g_send[:, lanes] = value

    hand_out(0, dot(own_t, dq_t[...], NT))
    for n in range(4):
        hand_out(512 + n * 256, dot(x_t, dkv[:, n * 256 : n * 256 + 256]))
    hand_out(1536, dot(att_t[...], cot[...]))
    d_q = dq_t[...].T
    homes = (
        ((g_tl, 0, 0, 64), (g_top, 0, 64, 128), (g_tr, 0, 192, 64)),
        ((g_left, 0, 0, 64), (None, 0, 64, 128), (g_right, 0, 192, 64)),
        ((g_left, 64, 0, 64), (None, 128, 64, 128), (g_right, 64, 192, 64)),
        ((g_bl, 0, 0, 64), (g_bottom, 0, 64, 128), (g_br, 0, 192, 64)),
    )
    for g in range(4):
        block = dot(dkv[g * 256 : g * 256 + 256], wt[512:1536])
        for ref, to, at, size in homes[g]:
            part = block[at : at + size]
            if ref is None:
                grad_own[to : to + size] = part + dot(d_q[to : to + size], wt[0:512])
            else:
                ref[to : to + size] = part.astype(BF16)


def after_kernel(own, up, down, west, east, nw, ne, sw, se, out):
    total = own[...]
    low = [up[...].astype(F32), down[...].astype(F32)]
    side = [west[...].astype(F32), east[...].astype(F32)]
    for half in range(2):
        rows = slice(half * 8, half * 8 + 8)
        corner = (nw, ne) if half == 0 else (sw, se)
        for col in range(2):
            cells = slice(col * 8, col * 8 + 8)
            out[rows, cells] = (
                total[rows, cells]
                + low[half][:, cells]
                + side[col][rows]
                + corner[col][...].astype(F32)
            ).astype(BF16)


def reduce_all(core, keep, send, bias):
    az, rng = lax.axis_size("az"), lax.axis_size("rng")

    def among(leaf, flip):
        return lax.ppermute(leaf, "dp", [(i, i ^ flip) for i in range(4)])

    half = (keep.astype(F32) + among(send, 1).astype(F32)).astype(BF16)
    rows = 512 // (az * rng)
    cols = -(-bias.size // (rows * 128)) * 128
    flat = jnp.pad(bias.reshape(-1), (0, rows * cols - bias.size)).astype(BF16)
    flat = jnp.broadcast_to(flat.reshape(1, rows, cols), (az * rng, rows, cols))
    parcel = jnp.concatenate([half.reshape(az * rng, rows, 1024), flat], axis=2)
    parcel = lax.all_to_all(parcel, ("az", "rng"), 0, 0, tiled=True)
    mine = jnp.sum(parcel.astype(F32), axis=0)
    near, other, far = among(mine, 2), among(mine, 1), among(mine, 3)
    here = mine + near
    there = other + far
    total_bias = (here[:, 1024:] + there[:, 1024:]).reshape(-1)[: bias.size].reshape(bias.shape)
    here, there = here[:, :1024], there[:, :1024]
    low = jnp.where(core == 0, here, there)
    high = jnp.where(core == 0, there, here)
    return jnp.concatenate([low, high[:, :512]], axis=1), high[:, 512:], total_bias


def whole(shape, dtype):
    return jax.ShapeDtypeStruct(shape, dtype)


def call(kernel, operands, outs, scratch=(), prefetch=0, flops=0, name=None):
    spec = pl.BlockSpec(memory_space=pltpu.VMEM)
    scalar = pl.BlockSpec(memory_space=pltpu.SMEM)
    size = sum(leaf.size * leaf.dtype.itemsize for leaf in tuple(operands) + tuple(outs))
    return pl.pallas_call(
        kernel,
        out_shape=tuple(outs),
        in_specs=[scalar] * prefetch + [spec] * (len(operands) - prefetch),
        out_specs=tuple([spec] * len(outs)),
        scratch_shapes=list(scratch),
        compiler_params=pltpu.CompilerParams(vmem_limit_bytes=VMEM_BYTES),
        cost_estimate=pl.CostEstimate(flops=flops, bytes_accessed=size, transcendentals=0),
        name=name,
    )(*operands)


def ring(count, step, closed):
    pairs = [(i, i + step) for i in range(count)]
    if closed:
        return [(a, b % count) for a, b in pairs]
    return [(a, b) for a, b in pairs if 0 <= b < count]


def diagonal(rows, cols, down, over):
    return [
        (a * cols + b, (a + down) % rows * cols + b + over)
        for a in range(rows)
        for b in range(cols)
        if 0 <= b + over < cols
    ]


def shards(tokens, qkv_weight, out_weight, relative_bias, cotangent):
    az, rng = lax.axis_size("az"), lax.axis_size("rng")
    width = tokens.shape[3]
    cells = tokens[0]
    own = cells.reshape(256, width)
    cot = cotangent.reshape(256, width)

    def along(leaf, axis, step):
        return lax.ppermute(leaf, axis, ring(az if axis == "az" else rng, step, axis == "az"))

    def across(leaf, down, over):
        return lax.ppermute(leaf, ("az", "rng"), diagonal(az, rng, down, over))

    halo = (
        along(cells[8:], "az", 1),
        along(cells[:8], "az", -1),
        along(cells[:, 8:], "rng", 1),
        along(cells[:, :8], "rng", -1),
        across(cells[8:, 8:], 1, 1),
        across(cells[8:, :8], 1, -1),
        across(cells[:8, 8:], -1, 1),
        across(cells[:8, :8], -1, -1),
    )
    halo = [leaf.reshape(-1, width) for leaf in halo]

    core = (lax.axis_index("dp") % 2).astype(jnp.int32)[None]
    at_range = lax.axis_index("rng")
    edge = jnp.stack([at_range == 0, at_range == rng - 1]).astype(jnp.int32)
    flipped = jnp.transpose(relative_bias[:, ::-1], (0, 2, 1))
    spread = jnp.pad(flipped, ((0, 0), (0, 7), (7, 8)), constant_values=ABSENT)
    bias_rows = jnp.repeat(spread, 16, axis=2)
    turned = qkv_weight.T

    q, q_t, da, da_t, table = call(
        before_kernel,
        (edge, own, cot, turned, out_weight, bias_rows),
        (
            whole((256, 512), BF16), whole((512, 256), BF16),
            whole((256, 512), BF16), whole((512, 256), BF16),
            whole((4, 768, 256), F32),
        ),
        prefetch=1,
        flops=600_000_000,
        name="before",
    )
    outs = call(
        main_kernel,
        (core, own, *halo, q, q_t, da, da_t, table, turned, cot),
        (
            whole((256, 512), F32),
            *[whole((128, 512), BF16)] * 4,
            *[whole((64, 512), BF16)] * 4,
            whole((512, 1024), BF16), whole((512, 1024), BF16),
            whole((8, 24, 128), F32),
        ),
        scratch=(
            pltpu.VMEM((1024, 512), BF16), pltpu.VMEM((1024, 512), BF16),
            pltpu.VMEM((1024, 512), BF16), pltpu.VMEM((512, 1024), BF16),
            pltpu.VMEM((512, 1024), BF16), pltpu.VMEM((1024, 1024), BF16),
            pltpu.VMEM((512, 256), BF16), pltpu.VMEM((512, 256), BF16),
            pltpu.VMEM((768, 256), F32), pltpu.VMEM((8, 24, 512), F32),
        ),
        prefetch=1,
        flops=10_000_000_000,
        name="attention",
    )
    grad_own, g_top, g_bottom, g_left, g_right, g_tl, g_tr, g_bl, g_br = outs[:9]
    g_keep, g_send, g_bias = outs[9:]
    arrived = (
        along(g_bottom.reshape(8, 16, width), "az", 1),
        along(g_top.reshape(8, 16, width), "az", -1),
        along(g_right.reshape(16, 8, width), "rng", 1),
        along(g_left.reshape(16, 8, width), "rng", -1),
        across(g_br.reshape(8, 8, width), 1, 1),
        across(g_bl.reshape(8, 8, width), 1, -1),
        across(g_tr.reshape(8, 8, width), -1, 1),
        across(g_tl.reshape(8, 8, width), -1, -1),
    )
    (grad_tokens,) = call(
        after_kernel,
        (grad_own.reshape(16, 16, width), *arrived),
        (whole((16, 16, width), BF16),),
        flops=1_000_000,
        name="after",
    )
    bias_local = jnp.transpose(g_bias[:, :17, 7:24], (0, 2, 1))[:, ::-1]
    rows_qkv, rows_out, total_bias = reduce_all(core[0], g_keep, g_send, bias_local)
    return (grad_tokens[None], rows_qkv, rows_out, total_bias)


def solution(mesh):
    placed = (P("dp", "az", "rng", None), P(), P(), P(), P("dp", "az", "rng", None))
    return jax.shard_map(
        shards,
        mesh=mesh,
        in_specs=placed,
        out_specs=(P("dp", "az", "rng", None), P(("az", "rng"), None), P(("az", "rng"), None), P()),
        check_vma=False,
    )
```

```python
import jax
import jax.numpy as jnp
from jax import lax
from jax.experimental import pallas as pl
from jax.experimental.pallas import tpu as pltpu
from jax.sharding import PartitionSpec as P

F32 = jnp.float32
BF16 = jnp.bfloat16
ABSENT = -1e30
NT = (((1,), (1,)), ((), ()))
TN = (((0,), (0,)), ((), ()))
MIB = 1024 * 1024


def dot(a, b, dims=(((1,), (0,)), ((), ())), exact=False):
    precision = lax.Precision.HIGHEST if exact else None
    return lax.dot_general(a, b, dims, precision=precision, preferred_element_type=F32)


def iota(shape, axis):
    return lax.broadcasted_iota(jnp.int32, shape, axis)


def row_slots(row):
    base = row // 8 * 256
    at = row % 8
    return (
        (0, 8, base + at * 8),
        (8, 24, base + 64 + at * 16),
        (24, 32, base + 192 + at * 8),
    )


def before_kernel(edge, x, cot, wt, wo, bias, q, q_t, da, da_t, table):
    xv = x[...]
    cv = cot[...]
    q[...] = (dot(xv, wt[0:512], NT).astype(BF16).astype(F32) * 0.125).astype(BF16)
    q_t[...] = (dot(wt[0:512], xv, NT).astype(BF16).astype(F32) * 0.125).astype(BF16)
    da[...] = dot(cv, wo[...], NT).astype(BF16)
    da_t[...] = dot(wo[...], cv, NT).astype(BF16)
    pick = (iota((17, 512), 0) == 23 - (iota((17, 512), 1) >> 4)).astype(F32)
    range_row = iota((32, 512), 0)
    lane = iota((32, 512), 1)
    gap = range_row - (lane & 15)
    first = jnp.where(edge[0] == 1, 8, 0)
    last = jnp.where(edge[1] == 1, 24, 32)
    present = (range_row >= first) & (range_row < last) & (lane >= 112) & (lane < 384)

    def pair_step(pair, carry):
        for side in range(2):
            head_rows = dot(bias[pair * 2 + side], pick, TN, exact=True)
            spread = jnp.full((32, 512), ABSENT, F32)
            for j in range(17):
                spread = jnp.where(gap == j, head_rows[j : j + 1], spread)
            spread = jnp.where(present, spread, ABSENT)
            for v in range(8):
                turned = spread if v == 0 else pltpu.roll(spread, 512 - 16 * v, 1)
                for u in range(3):
                    block = turned[:, 128 * u : 128 * u + 128]
                    for low, high, at in row_slots(23 - 8 * u - v):
                        table[pair, at : at + high - low, side * 128 : side * 128 + 128] = block[
                            low:high
                        ]
        return carry

    lax.fori_loop(0, 4, pair_step, 0)


def project(block, wt, k, v, k_t, v_t, at):
    rows = pl.ds(at, 256)
    keys = dot(block, wt[512:1024], NT).astype(BF16)
    values = dot(block, wt[1024:1536], NT).astype(BF16)
    k[rows] = keys
    v[rows] = values
    k_t[:, rows] = keys.T
    v_t[:, rows] = values.T


def middle_kernel(upper, lower, wt, k, v, k_t, v_t):
    project(upper[...], wt, k, v, k_t, v_t, 0)
    project(lower[...], wt, k, v, k_t, v_t, 256)


def attention_kernel(
    core, above, upper, lower, below, q, q_t, da, da_t, table, k_mid, v_mid, kt_mid, vt_mid, wt, own, cot,
    dkv, dq_t, g_keep, g_send, g_bias,
    k, v, k_t, v_t, xs, att_t, dsum, bsum, lhs, rhs,
):
    project(above[...], wt, k, v, k_t, v_t, 0)
    project(below[...], wt, k, v, k_t, v_t, 768)
    k[256:768] = k_mid[...]
    v[256:768] = v_mid[...]
    k_t[:, 256:768] = kt_mid[...]
    v_t[:, 256:768] = vt_mid[...]
    for g, ref in enumerate((above, upper, lower, below)):
        xs[:, g * 256 : g * 256 + 256] = ref[...].T

    upper_rows = iota((128, 128), 0) < 64
    upper_lanes = iota((128, 128), 1) < 64
    corner = iota((16, 512), 0) == (iota((16, 512), 1) & 15)

    def split_lanes(block):
        zero = jnp.zeros_like(block)
        return jnp.concatenate(
            [jnp.where(upper_rows, block, zero), jnp.where(upper_rows, zero, block)], axis=1
        )

    def split_rows(block):
        zero = jnp.zeros_like(block)
        return jnp.concatenate(
            [jnp.where(upper_lanes, block, zero), jnp.where(upper_lanes, zero, block)], axis=0
        )

    def pair_step(pair, carry):
        at = pl.multiple_of(pair * 128, 128)
        cols = pl.ds(at, 128)
        tails = []
        for t in range(2):
            keys = slice(t * 256, t * 256 + 768)
            mine = slice(t * 128, t * 128 + 128)
            score = dot(k[keys, cols], split_lanes(q_t[cols, mine])) + table[pair]
            top_score = jnp.max(score, axis=0, keepdims=True)
            weight = jnp.exp(score - top_score)
            prob = weight * (1.0 / jnp.sum(weight, axis=0, keepdims=True))
            prob_low = prob.astype(BF16)
            mixed = dot(v_t[cols, keys], prob_low)
            att = jnp.where(upper_rows, mixed[:, :128], mixed[:, 128:]).astype(BF16)
            att_t[cols, mine] = att
            da_block = da_t[cols, mine]
            product = att.astype(F32) * da_block.astype(F32)
            delta = jnp.concatenate(
                [
                    jnp.sum(product[:64], axis=0, keepdims=True),
                    jnp.sum(product[64:], axis=0, keepdims=True),
                ],
                axis=1,
            )
            d_score = prob * (dot(v[keys, cols], split_lanes(da_block)) - delta)
            if t == 0:
                dsum[...] = d_score
            else:
                dsum[...] += d_score
            score_low = d_score.astype(BF16)
            d_q = dot(k_t[cols, keys], score_low)
            dq_t[cols, mine] = (
                jnp.where(upper_rows, d_q[:, :128], d_q[:, 128:]) * 0.125
            ).astype(BF16)
            tails.append(
                (
                    dot(score_low, split_rows(q[mine, cols])),
                    dot(prob_low, split_rows(da[mine, cols])),
                )
            )
        for which in range(2):
            early, late = tails[0][which], tails[1][which]
            to = pl.ds(pl.multiple_of(which * 512 + at, 128), 128)
            dkv[0:256, to] = early[0:256].astype(BF16)
            dkv[256:768, to] = (early[256:768] + late[0:512]).astype(BF16)
            dkv[768:1024, to] = late[512:768].astype(BF16)
        for side in range(2):
            lanes = slice(side * 128, side * 128 + 128)
            total = None
            for turn in range(8):
                parts = [
                    jnp.concatenate(
                        [
                            dsum[to : to + high - low, lanes]
                            for low, high, to in row_slots(23 - 8 * u - turn)
                        ],
                        axis=0,
                    )
                    for u in range(3)
                ]
                strip = jnp.concatenate(parts + [jnp.zeros((32, 128), F32)], axis=1)
                if turn:
                    strip = pltpu.roll(strip, 16 * turn, 1)
                total = strip if total is None else total + strip
            tail = total[16:32]
            last = jnp.where(corner, tail, 0.0)
            rest = jnp.where(corner, 0.0, tail)
            bsum[0, pair * 2 + side] = (
                total[0:8]
                + pltpu.roll(total[8:16], 504, 1)
                + pltpu.roll(rest[0:8], 496, 1)
                + pltpu.roll(rest[8:16], 488, 1)
            )
            bsum[1, pair * 2 + side] = pltpu.roll(last[0:8], 496, 1) + pltpu.roll(
                last[8:16], 488, 1
            )
        return carry

    lax.fori_loop(0, 4, pair_step, 0)

    spot = iota((512, 384), 0)
    place = iota((512, 384), 1)
    i = (place * 241) >> 12
    j = place - i * 17
    inside = place < 289
    flat = None
    for which in range(2):
        lanes = None
        for b in range(8):
            row = bsum[which, :, b, :]
            row = pltpu.roll(row, 512 - b, 1) if b else row
            lanes = row if lanes is None else lanes + row
        from_lane = 368 - 16 * i - j
        choose = inside & (spot == from_lane) & ((j < 16) if which == 0 else (j == 16))
        part = dot(lanes, choose.astype(F32), exact=True)
        flat = part if flat is None else flat + part
    g_bias[...] = flat

    lhs[0, :, 0:128] = xs[:, 320:448]
    lhs[0, :, 128:256] = xs[:, 576:704]
    lhs[1] = att_t[...]
    rhs[0] = dq_t[...].T
    rhs[1] = cot[...]
    for ref, who in ((g_send, 1 - core[0]), (g_keep, core[0])):
        ref[:, 0:512] = dot(lhs[who], rhs[who]).astype(BF16)
        for n in range(2):
            lanes = pl.ds(pl.multiple_of(who * 512 + n * 256, 256), 256)
            ref[:, 512 + n * 256 : 768 + n * 256] = dot(xs[...], dkv[:, lanes]).astype(BF16)


def tokens_kernel(dkv, dq_t, wt, g_above, g_upper, g_lower, g_below):
    d_q = dq_t[...].T
    for g, ref in enumerate((g_above, g_upper, g_lower, g_below)):
        block = dot(dkv[g * 256 : g * 256 + 256], wt[512:1536])
        if g in (0, 3):
            ref[...] = block.astype(BF16)
        else:
            half = (g - 1) * 128
            ref[0:64] = block[0:64]
            ref[64:192] = block[64:192] + dot(d_q[half : half + 128], wt[0:512])
            ref[192:256] = block[192:256]


def fold_kernel(g_upper, g_lower, up, down, west, own, east):
    for half, (ref, term) in enumerate(((g_upper, up), (g_lower, down))):
        total = ref[...] + term[...].astype(F32)
        west[half * 64 : half * 64 + 64] = total[0:64].astype(BF16)
        own[half * 128 : half * 128 + 128] = total[64:192]
        east[half * 64 : half * 64 + 64] = total[192:256].astype(BF16)


def after_kernel(own, west, east, out):
    out[:, 0:8] = (own[:, 0:8] + west[...].astype(F32)).astype(BF16)
    out[:, 8:16] = (own[:, 8:16] + east[...].astype(F32)).astype(BF16)


def pack_kernel(keep, came, bias, _, parcel):
    count, rows, _ = parcel.shape
    cols = bias.shape[1]
    both = keep[...].astype(F32) + came[...].astype(F32)
    parcel[:, :, 0:1024] = both.astype(BF16).reshape(count, rows, 1024)
    parcel[:, :, 1024 : 1024 + cols] = jnp.broadcast_to(
        bias[...].astype(BF16)[None], (count, rows, cols)
    )


def finish_kernel(core, mine, near, other, far, qkv, out, bias):
    here = mine[...] + near[...]
    there = other[...] + far[...]
    is_first = core[0] == 0
    low = jnp.where(is_first, here[:, 0:1024], there[:, 0:1024])
    high = jnp.where(is_first, there[:, 0:1024], here[:, 0:1024])
    qkv[:, 0:1024] = low
    qkv[:, 1024:1536] = high[:, 512:1024]
    out[...] = high[:, 0:512]
    total = here[:, 1024:] + there[:, 1024:]
    for i in range(17):
        bias[i] = total[:, i * 17 : i * 17 + 17]


def whole(shape, dtype):
    return jax.ShapeDtypeStruct(shape, dtype)


def call(kernel, operands, outs, scratch=(), prefetch=0, flops=0, limit=16):
    spec = pl.BlockSpec(memory_space=pltpu.VMEM)
    scalar = pl.BlockSpec(memory_space=pltpu.SMEM)
    size = sum(leaf.size * leaf.dtype.itemsize for leaf in tuple(operands) + tuple(outs))
    return pl.pallas_call(
        kernel,
        out_shape=tuple(outs),
        in_specs=[scalar] * prefetch + [spec] * (len(operands) - prefetch),
        out_specs=tuple([spec] * len(outs)),
        scratch_shapes=list(scratch),
        compiler_params=pltpu.CompilerParams(vmem_limit_bytes=limit * MIB),
        cost_estimate=pl.CostEstimate(flops=flops, bytes_accessed=size, transcendentals=0),
        name=kernel.__name__,
    )(*operands)


def shards(tokens, qkv_weight, out_weight, relative_bias, cotangent):
    az, rng = lax.axis_size("az"), lax.axis_size("rng")
    width = tokens.shape[3]
    cells = tokens[0]
    own = cells.reshape(256, width)
    cot = cotangent.reshape(256, width)

    def turn(leaf, step):
        return lax.ppermute(leaf, "az", [(i, (i + step) % az) for i in range(az)])

    def shift(leaf, step):
        pairs = [(i, i + step) for i in range(rng) if 0 <= i + step < rng]
        return lax.ppermute(leaf, "rng", pairs)

    def among(leaf, flip):
        return lax.ppermute(leaf, "dp", [(i, i ^ flip) for i in range(4)])

    left = shift(cells[:, 8:], 1).reshape(128, width)
    right = shift(cells[:, :8], -1).reshape(128, width)
    upper = jnp.concatenate([left[:64], own[:128], right[:64]], axis=0)
    lower = jnp.concatenate([left[64:], own[128:], right[64:]], axis=0)
    above = turn(lower, 1)
    below = turn(upper, -1)

    core = (lax.axis_index("dp") % 2).astype(jnp.int32)[None]
    at_range = lax.axis_index("rng")
    edge = jnp.stack([at_range == 0, at_range == rng - 1]).astype(jnp.int32)
    turned = qkv_weight.T

    q, q_t, da, da_t, table = call(
        before_kernel,
        (edge, own, cot, turned, out_weight, relative_bias),
        (
            whole((256, 512), BF16), whole((512, 256), BF16),
            whole((256, 512), BF16), whole((512, 256), BF16),
            whole((4, 768, 256), F32),
        ),
        prefetch=1,
        flops=600_000_000,
        limit=12,
    )
    middle = call(
        middle_kernel,
        (upper, lower, turned),
        (
            whole((512, 512), BF16), whole((512, 512), BF16),
            whole((512, 512), BF16), whole((512, 512), BF16),
        ),
        flops=1_000_000_000,
        limit=12,
    )
    dkv, dq_t, g_keep, g_send, g_bias = call(
        attention_kernel,
        (core, above, upper, lower, below, q, q_t, da, da_t, table, *middle, turned, own, cot),
        (
            whole((1024, 1024), BF16), whole((512, 256), BF16),
            whole((512, 1024), BF16), whole((512, 1024), BF16),
            whole((8, 384), F32),
        ),
        scratch=(
            pltpu.VMEM((1024, 512), BF16), pltpu.VMEM((1024, 512), BF16),
            pltpu.VMEM((512, 1024), BF16), pltpu.VMEM((512, 1024), BF16),
            pltpu.VMEM((512, 1024), BF16), pltpu.VMEM((512, 256), BF16),
            pltpu.VMEM((768, 256), F32), pltpu.VMEM((2, 8, 8, 512), F32),
            pltpu.VMEM((2, 512, 256), BF16), pltpu.VMEM((2, 256, 512), BF16),
        ),
        prefetch=1,
        flops=10_000_000_000,
        limit=20,
    )

    g_above, g_upper, g_lower, g_below = call(
        tokens_kernel,
        (dkv, dq_t, turned),
        (
            whole((256, 512), BF16), whole((256, 512), F32),
            whole((256, 512), F32), whole((256, 512), BF16),
        ),
        flops=1_200_000_000,
    )

    came = among(g_send, 1)
    rows = 512 // (az * rng)
    cols = 384
    if rows != 8:
        g_bias = jnp.pad(g_bias, ((0, rows - 8), (0, 0)))
    (parcel,) = call(
        pack_kernel,
        (g_keep, came, g_bias, g_above),
        (whole((az * rng, rows, 1024 + cols), BF16),),
        flops=1_000_000,
    )
    parcel = lax.all_to_all(parcel, ("az", "rng"), 0, 0, tiled=True)

    up = turn(g_below, 1)
    down = turn(g_above, -1)
    to_west, g_own, to_east = call(
        fold_kernel,
        (g_upper, g_lower, up, down),
        (whole((128, 512), BF16), whole((256, 512), F32), whole((128, 512), BF16)),
        flops=1_000_000,
    )
    east = shift(to_west.reshape(16, 8, width), -1)
    west = shift(to_east.reshape(16, 8, width), 1)
    (grad_tokens,) = call(
        after_kernel,
        (g_own.reshape(16, 16, width), west, east),
        (whole((16, 16, width), BF16),),
        flops=1_000_000,
    )

    mine = jnp.sum(parcel.astype(F32), axis=0)
    near, other, far = among(mine, 2), among(mine, 1), among(mine, 3)
    rows_qkv, rows_out, total_bias = call(
        finish_kernel,
        (core, mine, near, other, far),
        (whole((rows, 1536), F32), whole((rows, 512), F32), whole((17, rows, 17), F32)),
        prefetch=1,
        flops=1_000_000,
    )
    total_bias = jnp.transpose(total_bias[:, :8], (1, 0, 2))
    return (grad_tokens[None], rows_qkv, rows_out, total_bias)


def solution(mesh):
    placed = (P("dp", "az", "rng", None), P(), P(), P(), P("dp", "az", "rng", None))
    return jax.shard_map(
        shards,
        mesh=mesh,
        in_specs=placed,
        out_specs=(P("dp", "az", "rng", None), P(("az", "rng"), None), P(("az", "rng"), None), P()),
        check_vma=False,
    )
```

```python
import jax
import jax.numpy as jnp
from jax import lax
from jax.experimental import pallas as pl
from jax.experimental.pallas import tpu as pltpu
from jax.sharding import PartitionSpec as P

F32 = jnp.float32
BF16 = jnp.bfloat16
ABSENT = -1e30
NT = (((1,), (1,)), ((), ()))
TN = (((0,), (0,)), ((), ()))
MIB = 1024 * 1024


def dot(a, b, dims=(((1,), (0,)), ((), ())), exact=False):
    precision = lax.Precision.HIGHEST if exact else None
    return lax.dot_general(a, b, dims, precision=precision, preferred_element_type=F32)


def iota(shape, axis):
    return lax.broadcasted_iota(jnp.int32, shape, axis)


def row_slots(row):
    base = row // 8 * 256
    at = row % 8
    return (
        (0, 8, base + at * 8),
        (8, 24, base + 64 + at * 16),
        (24, 32, base + 192 + at * 8),
    )


def before_kernel(edge, x, cot, wt, wo, bias, q, q_t, da, da_t, table):
    xv = x[...]
    cv = cot[...]
    q[...] = (dot(xv, wt[0:512], NT).astype(BF16).astype(F32) * 0.125).astype(BF16)
    q_t[...] = (dot(wt[0:512], xv, NT).astype(BF16).astype(F32) * 0.125).astype(BF16)
    da[...] = dot(cv, wo[...], NT).astype(BF16)
    da_t[...] = dot(wo[...], cv, NT).astype(BF16)
    pick = (iota((17, 512), 0) == 23 - (iota((17, 512), 1) >> 4)).astype(F32)
    range_row = iota((32, 512), 0)
    lane = iota((32, 512), 1)
    gap = range_row - (lane & 15)
    first = jnp.where(edge[0] == 1, 8, 0)
    last = jnp.where(edge[1] == 1, 24, 32)
    present = (range_row >= first) & (range_row < last) & (lane >= 112) & (lane < 384)

    def pair_step(pair, carry):
        for side in range(2):
            head_rows = dot(bias[pair * 2 + side], pick, TN, exact=True)
            spread = jnp.full((32, 512), ABSENT, F32)
            for j in range(17):
                spread = jnp.where(gap == j, head_rows[j : j + 1], spread)
            spread = jnp.where(present, spread, ABSENT)
            for v in range(8):
                turned = spread if v == 0 else pltpu.roll(spread, 512 - 16 * v, 1)
                for u in range(3):
                    block = turned[:, 128 * u : 128 * u + 128]
                    for low, high, at in row_slots(23 - 8 * u - v):
                        table[pair, at : at + high - low, side * 128 : side * 128 + 128] = block[
                            low:high
                        ]
        return carry

    lax.fori_loop(0, 4, pair_step, 0)


def project(block, wt, k, v, k_t, v_t, at):
    rows = pl.ds(at, 256)
    keys = dot(block, wt[512:1024], NT).astype(BF16)
    values = dot(block, wt[1024:1536], NT).astype(BF16)
    k[rows] = keys
    v[rows] = values
    k_t[:, rows] = keys.T
    v_t[:, rows] = values.T


def middle_kernel(upper, lower, wt, k, v, k_t, v_t):
    project(upper[...], wt, k, v, k_t, v_t, 0)
    project(lower[...], wt, k, v, k_t, v_t, 256)


def attention_kernel(
    core, above, upper, lower, below, q, q_t, da, da_t, table, k_mid, v_mid, kt_mid, vt_mid, wt, own, cot,
    dkv, dq_t, g_keep, g_send, g_bias,
    k, v, k_t, v_t, xs, att_t, dsum, bsum, lhs, rhs,
):
    project(above[...], wt, k, v, k_t, v_t, 0)
    project(below[...], wt, k, v, k_t, v_t, 768)
    k[256:768] = k_mid[...]
    v[256:768] = v_mid[...]
    k_t[:, 256:768] = kt_mid[...]
    v_t[:, 256:768] = vt_mid[...]
    for g, ref in enumerate((above, upper, lower, below)):
        xs[:, g * 256 : g * 256 + 256] = ref[...].T

    upper_rows = iota((128, 128), 0) < 64
    upper_lanes = iota((128, 128), 1) < 64
    corner = iota((16, 512), 0) == (iota((16, 512), 1) & 15)

    def split_lanes(block):
        zero = jnp.zeros_like(block)
        return jnp.concatenate(
            [jnp.where(upper_rows, block, zero), jnp.where(upper_rows, zero, block)], axis=1
        )

    def split_rows(block):
        zero = jnp.zeros_like(block)
        return jnp.concatenate(
            [jnp.where(upper_lanes, block, zero), jnp.where(upper_lanes, zero, block)], axis=0
        )

    def pair_step(pair, carry):
        at = pl.multiple_of(pair * 128, 128)
        cols = pl.ds(at, 128)
        tails = []
        for t in range(2):
            keys = slice(t * 256, t * 256 + 768)
            mine = slice(t * 128, t * 128 + 128)
            score = dot(k[keys, cols], split_lanes(q_t[cols, mine])) + table[pair]
            top_score = jnp.max(score, axis=0, keepdims=True)
            weight = jnp.exp(score - top_score)
            prob = weight * (1.0 / jnp.sum(weight, axis=0, keepdims=True))
            prob_low = prob.astype(BF16)
            mixed = dot(v_t[cols, keys], prob_low)
            att = jnp.where(upper_rows, mixed[:, :128], mixed[:, 128:]).astype(BF16)
            att_t[cols, mine] = att
            da_block = da_t[cols, mine]
            product = att.astype(F32) * da_block.astype(F32)
            delta = jnp.concatenate(
                [
                    jnp.sum(product[:64], axis=0, keepdims=True),
                    jnp.sum(product[64:], axis=0, keepdims=True),
                ],
                axis=1,
            )
            d_score = prob * (dot(v[keys, cols], split_lanes(da_block)) - delta)
            if t == 0:
                dsum[...] = d_score
            else:
                dsum[...] += d_score
            score_low = d_score.astype(BF16)
            d_q = dot(k_t[cols, keys], score_low)
            dq_t[cols, mine] = (
                jnp.where(upper_rows, d_q[:, :128], d_q[:, 128:]) * 0.125
            ).astype(BF16)
            tails.append(
                (
                    dot(score_low, split_rows(q[mine, cols])),
                    dot(prob_low, split_rows(da[mine, cols])),
                )
            )
        for which in range(2):
            early, late = tails[0][which], tails[1][which]
            to = pl.ds(pl.multiple_of(which * 512 + at, 128), 128)
            dkv[0:256, to] = early[0:256].astype(BF16)
            dkv[256:768, to] = (early[256:768] + late[0:512]).astype(BF16)
            dkv[768:1024, to] = late[512:768].astype(BF16)
        for side in range(2):
            lanes = slice(side * 128, side * 128 + 128)
            total = None
            for turn in range(8):
                parts = [
                    jnp.concatenate(
                        [
                            dsum[to : to + high - low, lanes]
                            for low, high, to in row_slots(23 - 8 * u - turn)
                        ],
                        axis=0,
                    )
                    for u in range(3)
                ]
                strip = jnp.concatenate(parts + [jnp.zeros((32, 128), F32)], axis=1)
                if turn:
                    strip = pltpu.roll(strip, 16 * turn, 1)
                total = strip if total is None else total + strip
            tail = total[16:32]
            last = jnp.where(corner, tail, 0.0)
            rest = jnp.where(corner, 0.0, tail)
            bsum[0, pair * 2 + side] = (
                total[0:8]
                + pltpu.roll(total[8:16], 504, 1)
                + pltpu.roll(rest[0:8], 496, 1)
                + pltpu.roll(rest[8:16], 488, 1)
            )
            bsum[1, pair * 2 + side] = pltpu.roll(last[0:8], 496, 1) + pltpu.roll(
                last[8:16], 488, 1
            )
        return carry

    lax.fori_loop(0, 4, pair_step, 0)

    spot = iota((512, 384), 0)
    place = iota((512, 384), 1)
    i = (place * 241) >> 12
    j = place - i * 17
    inside = place < 289
    flat = None
    for which in range(2):
        lanes = None
        for b in range(8):
            row = bsum[which, :, b, :]
            row = pltpu.roll(row, 512 - b, 1) if b else row
            lanes = row if lanes is None else lanes + row
        from_lane = 368 - 16 * i - j
        choose = inside & (spot == from_lane) & ((j < 16) if which == 0 else (j == 16))
        part = dot(lanes, choose.astype(F32), exact=True)
        flat = part if flat is None else flat + part
    g_bias[...] = flat

    lhs[0, :, 0:128] = xs[:, 320:448]
    lhs[0, :, 128:256] = xs[:, 576:704]
    lhs[1] = att_t[...]
    rhs[0] = dq_t[...].T
    rhs[1] = cot[...]
    for ref, who in ((g_send, 1 - core[0]), (g_keep, core[0])):
        ref[:, 0:512] = dot(lhs[who], rhs[who]).astype(BF16)
        for n in range(2):
            lanes = pl.ds(pl.multiple_of(who * 512 + n * 256, 256), 256)
            ref[:, 512 + n * 256 : 768 + n * 256] = dot(xs[...], dkv[:, lanes]).astype(BF16)


def tokens_kernel(dkv, dq_t, wt, g_above, g_upper, g_lower, g_below):
    d_q = dq_t[...].T
    for g, ref in enumerate((g_above, g_upper, g_lower, g_below)):
        block = dot(dkv[g * 256 : g * 256 + 256], wt[512:1536])
        if g in (0, 3):
            ref[...] = block.astype(BF16)
        else:
            half = (g - 1) * 128
            ref[0:64] = block[0:64]
            ref[64:192] = block[64:192] + dot(d_q[half : half + 128], wt[0:512])
            ref[192:256] = block[192:256]


def fold_kernel(g_upper, g_lower, up, down, west, own, east):
    for half, (ref, term) in enumerate(((g_upper, up), (g_lower, down))):
        total = ref[...] + term[...].astype(F32)
        west[half * 64 : half * 64 + 64] = total[0:64].astype(BF16)
        own[half * 128 : half * 128 + 128] = total[64:192]
        east[half * 64 : half * 64 + 64] = total[192:256].astype(BF16)


def after_kernel(own, west, east, out):
    out[:, 0:8] = (own[:, 0:8] + west[...].astype(F32)).astype(BF16)
    out[:, 8:16] = (own[:, 8:16] + east[...].astype(F32)).astype(BF16)


def pack_kernel(keep, came, bias, _, parcel):
    count, rows, _ = parcel.shape
    for a in range(rows // 8):
        for r in range(count):
            at = (a * count + r) * 8
            both = keep[at : at + 8].astype(F32) + came[at : at + 8].astype(F32)
            parcel[r, a * 8 : a * 8 + 8, 0:1024] = both.astype(BF16)
    parcel[:, :, 1024:1152] = jnp.zeros((count, rows, 128), BF16)
    for n in range(3):
        part = bias[:, n * 128 : n * 128 + 128].astype(BF16)
        for r in range(count):
            parcel[r, n * 8 : n * 8 + 8, 1024:1152] = part


def regroup_kernel(came, parcel):
    count = parcel.shape[0]
    for a in range(count):
        rows = slice(a * 8, a * 8 + 8)
        total = came[0, rows, 0:1024].astype(F32)
        for r in range(1, came.shape[0]):
            total += came[r, rows, 0:1024].astype(F32)
        parcel[a, :, 0:1024] = total.astype(BF16)
    for n in range(3):
        rows = slice(n * 8, n * 8 + 8)
        total = came[0, rows, 1024:1152].astype(F32)
        for r in range(1, came.shape[0]):
            total += came[r, rows, 1024:1152].astype(F32)
        part = total.astype(BF16)
        for a in range(count):
            parcel[a, :, 1024 + n * 128 : 1152 + n * 128] = part


def total_kernel(came, mine):
    total = came[0].astype(F32)
    for a in range(1, came.shape[0]):
        total += came[a].astype(F32)
    mine[...] = total


def finish_kernel(core, mine, near, other, far, qkv, out, bias):
    here = mine[...] + near[...]
    there = other[...] + far[...]
    is_first = core[0] == 0
    low = jnp.where(is_first, here[:, 0:1024], there[:, 0:1024])
    high = jnp.where(is_first, there[:, 0:1024], here[:, 0:1024])
    qkv[:, 0:1024] = low
    qkv[:, 1024:1536] = high[:, 512:1024]
    out[...] = high[:, 0:512]
    total = here[:, 1024:] + there[:, 1024:]
    for i in range(17):
        bias[i] = total[:, i * 17 : i * 17 + 17]


def whole(shape, dtype):
    return jax.ShapeDtypeStruct(shape, dtype)


def call(kernel, operands, outs, scratch=(), prefetch=0, flops=0, limit=16):
    spec = pl.BlockSpec(memory_space=pltpu.VMEM)
    scalar = pl.BlockSpec(memory_space=pltpu.SMEM)
    size = sum(leaf.size * leaf.dtype.itemsize for leaf in tuple(operands) + tuple(outs))
    return pl.pallas_call(
        kernel,
        out_shape=tuple(outs),
        in_specs=[scalar] * prefetch + [spec] * (len(operands) - prefetch),
        out_specs=tuple([spec] * len(outs)),
        scratch_shapes=list(scratch),
        compiler_params=pltpu.CompilerParams(vmem_limit_bytes=limit * MIB),
        cost_estimate=pl.CostEstimate(flops=flops, bytes_accessed=size, transcendentals=0),
        name=kernel.__name__,
    )(*operands)


def shards(tokens, qkv_weight, out_weight, relative_bias, cotangent):
    az, rng = lax.axis_size("az"), lax.axis_size("rng")
    width = tokens.shape[3]
    cells = tokens[0]
    own = cells.reshape(256, width)
    cot = cotangent.reshape(256, width)

    def turn(leaf, step):
        return lax.ppermute(leaf, "az", [(i, (i + step) % az) for i in range(az)])

    def shift(leaf, step):
        pairs = [(i, i + step) for i in range(rng) if 0 <= i + step < rng]
        return lax.ppermute(leaf, "rng", pairs)

    def among(leaf, flip):
        return lax.ppermute(leaf, "dp", [(i, i ^ flip) for i in range(4)])

    left = shift(cells[:, 8:], 1).reshape(128, width)
    right = shift(cells[:, :8], -1).reshape(128, width)
    upper = jnp.concatenate([left[:64], own[:128], right[:64]], axis=0)
    lower = jnp.concatenate([left[64:], own[128:], right[64:]], axis=0)
    above = turn(lower, 1)
    below = turn(upper, -1)

    core = (lax.axis_index("dp") % 2).astype(jnp.int32)[None]
    at_range = lax.axis_index("rng")
    edge = jnp.stack([at_range == 0, at_range == rng - 1]).astype(jnp.int32)
    turned = qkv_weight.T

    q, q_t, da, da_t, table = call(
        before_kernel,
        (edge, own, cot, turned, out_weight, relative_bias),
        (
            whole((256, 512), BF16), whole((512, 256), BF16),
            whole((256, 512), BF16), whole((512, 256), BF16),
            whole((4, 768, 256), F32),
        ),
        prefetch=1,
        flops=600_000_000,
        limit=12,
    )
    middle = call(
        middle_kernel,
        (upper, lower, turned),
        (
            whole((512, 512), BF16), whole((512, 512), BF16),
            whole((512, 512), BF16), whole((512, 512), BF16),
        ),
        flops=1_000_000_000,
        limit=12,
    )
    dkv, dq_t, g_keep, g_send, g_bias = call(
        attention_kernel,
        (core, above, upper, lower, below, q, q_t, da, da_t, table, *middle, turned, own, cot),
        (
            whole((1024, 1024), BF16), whole((512, 256), BF16),
            whole((512, 1024), BF16), whole((512, 1024), BF16),
            whole((8, 384), F32),
        ),
        scratch=(
            pltpu.VMEM((1024, 512), BF16), pltpu.VMEM((1024, 512), BF16),
            pltpu.VMEM((512, 1024), BF16), pltpu.VMEM((512, 1024), BF16),
            pltpu.VMEM((512, 1024), BF16), pltpu.VMEM((512, 256), BF16),
            pltpu.VMEM((768, 256), F32), pltpu.VMEM((2, 8, 8, 512), F32),
            pltpu.VMEM((2, 512, 256), BF16), pltpu.VMEM((2, 256, 512), BF16),
        ),
        prefetch=1,
        flops=10_000_000_000,
        limit=20,
    )

    g_above, g_upper, g_lower, g_below = call(
        tokens_kernel,
        (dkv, dq_t, turned),
        (
            whole((256, 512), BF16), whole((256, 512), F32),
            whole((256, 512), F32), whole((256, 512), BF16),
        ),
        flops=1_200_000_000,
    )

    came = among(g_send, 1)
    (parcel,) = call(
        pack_kernel,
        (g_keep, came, g_bias, g_above),
        (whole((rng, 8 * az, 1152), BF16),),
        flops=1_000_000,
    )
    parcel = lax.all_to_all(parcel, "rng", 0, 0, tiled=True)
    (parcel,) = call(
        regroup_kernel, (parcel,), (whole((az, 8, 1408), BF16),), flops=1_000_000
    )
    parcel = lax.all_to_all(parcel, "az", 0, 0, tiled=True)
    (mine,) = call(total_kernel, (parcel,), (whole((8, 1408), F32),), flops=1_000_000)

    up = turn(g_below, 1)
    down = turn(g_above, -1)
    to_west, g_own, to_east = call(
        fold_kernel,
        (g_upper, g_lower, up, down),
        (whole((128, 512), BF16), whole((256, 512), F32), whole((128, 512), BF16)),
        flops=1_000_000,
    )
    east = shift(to_west.reshape(16, 8, width), -1)
    west = shift(to_east.reshape(16, 8, width), 1)
    (grad_tokens,) = call(
        after_kernel,
        (g_own.reshape(16, 16, width), west, east),
        (whole((16, 16, width), BF16),),
        flops=1_000_000,
    )

    near, other, far = among(mine, 2), among(mine, 1), among(mine, 3)
    rows_qkv, rows_out, total_bias = call(
        finish_kernel,
        (core, mine, near, other, far),
        (whole((8, 1536), F32), whole((8, 512), F32), whole((17, 8, 17), F32)),
        prefetch=1,
        flops=1_000_000,
    )
    total_bias = jnp.transpose(total_bias, (1, 0, 2))
    return (grad_tokens[None], rows_qkv, rows_out, total_bias)


def solution(mesh):
    placed = (P("dp", "az", "rng", None), P(), P(), P(), P("dp", "az", "rng", None))
    return jax.shard_map(
        shards,
        mesh=mesh,
        in_specs=placed,
        out_specs=(P("dp", "az", "rng", None), P(("az", "rng"), None), P(("az", "rng"), None), P()),
        check_vma=False,
    )
```

```python
import jax
import jax.numpy as jnp
from jax import lax
from jax.experimental import pallas as pl
from jax.experimental.pallas import tpu as pltpu
from jax.sharding import PartitionSpec as P

F32 = jnp.float32
BF16 = jnp.bfloat16
ABSENT = -1e30
NT = (((1,), (1,)), ((), ()))
TN = (((0,), (0,)), ((), ()))
MIB = 1024 * 1024


def dot(a, b, dims=(((1,), (0,)), ((), ())), exact=False):
    precision = lax.Precision.HIGHEST if exact else None
    return lax.dot_general(a, b, dims, precision=precision, preferred_element_type=F32)


def iota(shape, axis):
    return lax.broadcasted_iota(jnp.int32, shape, axis)


def row_slots(row):
    base = row // 8 * 256
    at = row % 8
    return (
        (0, 8, base + at * 8),
        (8, 24, base + 64 + at * 16),
        (24, 32, base + 192 + at * 8),
    )


def before_kernel(edge, x, cot, wt, wo, bias, q, q_t, da, da_t, table):
    xv = x[...]
    cv = cot[...]
    q[...] = (dot(xv, wt[0:512], NT).astype(BF16).astype(F32) * 0.125).astype(BF16)
    q_t[...] = (dot(wt[0:512], xv, NT).astype(BF16).astype(F32) * 0.125).astype(BF16)
    da[...] = dot(cv, wo[...], NT).astype(BF16)
    da_t[...] = dot(wo[...], cv, NT).astype(BF16)
    pick = (iota((17, 512), 0) == 23 - (iota((17, 512), 1) >> 4)).astype(F32)
    range_row = iota((32, 512), 0)
    lane = iota((32, 512), 1)
    gap = range_row - (lane & 15)
    first = jnp.where(edge[0] == 1, 8, 0)
    last = jnp.where(edge[1] == 1, 24, 32)
    present = (range_row >= first) & (range_row < last) & (lane >= 112) & (lane < 384)

    def pair_step(pair, carry):
        for side in range(2):
            head_rows = dot(bias[pair * 2 + side], pick, TN, exact=True)
            spread = jnp.full((32, 512), ABSENT, F32)
            for j in range(17):
                spread = jnp.where(gap == j, head_rows[j : j + 1], spread)
            spread = jnp.where(present, spread, ABSENT)
            for v in range(8):
                turned = spread if v == 0 else pltpu.roll(spread, 512 - 16 * v, 1)
                for u in range(3):
                    block = turned[:, 128 * u : 128 * u + 128]
                    for low, high, at in row_slots(23 - 8 * u - v):
                        table[pair, at : at + high - low, side * 128 : side * 128 + 128] = block[
                            low:high
                        ]
        return carry

    lax.fori_loop(0, 4, pair_step, 0)


def project(block, wt, k, v, k_t, v_t, at):
    rows = pl.ds(at, 256)
    keys = dot(block, wt[512:1024], NT).astype(BF16)
    values = dot(block, wt[1024:1536], NT).astype(BF16)
    k[rows] = keys
    v[rows] = values
    k_t[:, rows] = keys.T
    v_t[:, rows] = values.T


def middle_kernel(upper, lower, wt, k, v, k_t, v_t, x_t):
    for at, ref in ((0, upper), (256, lower)):
        project(ref[...], wt, k, v, k_t, v_t, at)
        x_t[:, at : at + 256] = ref[...].T


def weight_terms(ref, who, x_t, dkv, lhs, rhs):
    ref[:, 0:512] = dot(lhs[who], rhs[who]).astype(BF16)
    for n in range(2):
        lanes = pl.ds(pl.multiple_of(who * 512 + n * 256, 256), 256)
        ref[:, 512 + n * 256 : 768 + n * 256] = dot(x_t[...], dkv[:, lanes]).astype(BF16)


def attention_kernel(
    core, above, below, q, q_t, da, da_t, table, k_mid, v_mid, kt_mid, vt_mid, xt_mid, wt, cot,
    x_t, dkv, lhs, rhs, bsum, g_send,
    k, v, k_t, v_t, dq_t, dsum,
):
    project(above[...], wt, k, v, k_t, v_t, 0)
    project(below[...], wt, k, v, k_t, v_t, 768)
    k[256:768] = k_mid[...]
    v[256:768] = v_mid[...]
    k_t[:, 256:768] = kt_mid[...]
    v_t[:, 256:768] = vt_mid[...]
    x_t[:, 0:256] = above[...].T
    x_t[:, 256:768] = xt_mid[...]
    x_t[:, 768:1024] = below[...].T
    lhs[0, :, 0:128] = xt_mid[:, 64:192]
    lhs[0, :, 128:256] = xt_mid[:, 320:448]
    rhs[1] = cot[...]

    upper_rows = iota((128, 128), 0) < 64
    upper_lanes = iota((128, 128), 1) < 64
    corner = iota((16, 512), 0) == (iota((16, 512), 1) & 15)

    def split_lanes(block):
        zero = jnp.zeros_like(block)
        return jnp.concatenate(
            [jnp.where(upper_rows, block, zero), jnp.where(upper_rows, zero, block)], axis=1
        )

    def tall(ref, rows, cols, block):
        return dot(ref[rows, cols], block)

    def split_rows(block):
        zero = jnp.zeros_like(block)
        return jnp.concatenate(
            [jnp.where(upper_lanes, block, zero), jnp.where(upper_lanes, zero, block)], axis=0
        )

    def pair_step(pair, carry):
        at = pl.multiple_of(pair * 128, 128)
        cols = pl.ds(at, 128)
        keys = [slice(t * 256, t * 256 + 768) for t in range(2)]
        mine = [slice(t * 128, t * 128 + 128) for t in range(2)]
        da_block = [da_t[cols, mine[t]] for t in range(2)]
        score = [
            tall(k, keys[t], cols, split_lanes(q_t[cols, mine[t]])) + table[pair] for t in range(2)
        ]
        d_prob = [tall(v, keys[t], cols, split_lanes(da_block[t])) for t in range(2)]
        prob, delta, d_value, d_key = [], [], [], []
        for t in range(2):
            top_score = jnp.max(score[t], axis=0, keepdims=True)
            weight = jnp.exp(score[t] - top_score)
            prob.append(weight * (1.0 / jnp.sum(weight, axis=0, keepdims=True)))
        prob_low = [each.astype(BF16) for each in prob]
        for t in range(2):
            mixed = dot(v_t[cols, keys[t]], prob_low[t])
            att = jnp.where(upper_rows, mixed[:, :128], mixed[:, 128:]).astype(BF16)
            lhs[1, cols, mine[t]] = att
            product = att.astype(F32) * da_block[t].astype(F32)
            delta.append(
                jnp.concatenate(
                    [
                        jnp.sum(product[:64], axis=0, keepdims=True),
                        jnp.sum(product[64:], axis=0, keepdims=True),
                    ],
                    axis=1,
                )
            )
            d_value.append(dot(prob_low[t], split_rows(da[mine[t], cols])))
        d_score = [prob[t] * (d_prob[t] - delta[t]) for t in range(2)]
        dsum[...] = d_score[0] + d_score[1]
        for t in range(2):
            score_low = d_score[t].astype(BF16)
            d_q = dot(k_t[cols, keys[t]], score_low)
            dq_t[cols, mine[t]] = (
                jnp.where(upper_rows, d_q[:, :128], d_q[:, 128:]) * 0.125
            ).astype(BF16)
            d_key.append(dot(score_low, split_rows(q[mine[t], cols])))
        tails = ((d_key[0], d_value[0]), (d_key[1], d_value[1]))
        for which in range(2):
            early, late = tails[0][which], tails[1][which]
            to = pl.ds(pl.multiple_of(which * 512 + at, 128), 128)
            dkv[0:256, to] = early[0:256].astype(BF16)
            dkv[256:768, to] = (early[256:768] + late[0:512]).astype(BF16)
            dkv[768:1024, to] = late[512:768].astype(BF16)
        for side in range(2):
            lanes = slice(side * 128, side * 128 + 128)
            total = None
            for turn in range(8):
                parts = [
                    jnp.concatenate(
                        [
                            dsum[to : to + high - low, lanes]
                            for low, high, to in row_slots(23 - 8 * u - turn)
                        ],
                        axis=0,
                    )
                    for u in range(3)
                ]
                strip = jnp.concatenate(parts + [jnp.zeros((32, 128), F32)], axis=1)
                if turn:
                    strip = pltpu.roll(strip, 16 * turn, 1)
                total = strip if total is None else total + strip
            tail = total[16:32]
            last = jnp.where(corner, tail, 0.0)
            rest = jnp.where(corner, 0.0, tail)
            bsum[0, pair * 2 + side] = (
                total[0:8]
                + pltpu.roll(total[8:16], 504, 1)
                + pltpu.roll(rest[0:8], 496, 1)
                + pltpu.roll(rest[8:16], 488, 1)
            )
            bsum[1, pair * 2 + side] = pltpu.roll(last[0:8], 496, 1) + pltpu.roll(
                last[8:16], 488, 1
            )
        return carry

    lax.fori_loop(0, 4, pair_step, 0)

    rhs[0] = dq_t[...].T
    weight_terms(g_send, 1 - core[0], x_t, dkv, lhs, rhs)


def terms_kernel(
    core, x_t, dkv, lhs, rhs, bsum, wt, g_keep, g_bias, g_above, g_upper, g_lower, g_below
):
    weight_terms(g_keep, core[0], x_t, dkv, lhs, rhs)

    spot = iota((512, 384), 0)
    place = iota((512, 384), 1)
    i = (place * 241) >> 12
    j = place - i * 17
    inside = place < 289
    flat = None
    for which in range(2):
        lanes = None
        for b in range(8):
            row = bsum[which, :, b, :]
            row = pltpu.roll(row, 512 - b, 1) if b else row
            lanes = row if lanes is None else lanes + row
        from_lane = 368 - 16 * i - j
        choose = inside & (spot == from_lane) & ((j < 16) if which == 0 else (j == 16))
        part = dot(lanes.astype(BF16), choose.astype(F32).astype(BF16))
        flat = part if flat is None else flat + part
    g_bias[...] = flat

    for g, ref in enumerate((g_above, g_upper, g_lower, g_below)):
        block = dot(dkv[g * 256 : g * 256 + 256], wt[512:1536])
        if g in (0, 3):
            ref[...] = block.astype(BF16)
        else:
            half = (g - 1) * 128
            ref[0:64] = block[0:64]
            ref[64:192] = block[64:192] + dot(rhs[0, half : half + 128], wt[0:512])
            ref[192:256] = block[192:256]


def fold_kernel(g_upper, g_lower, up, down, west, own, east):
    for half, (ref, term) in enumerate(((g_upper, up), (g_lower, down))):
        total = ref[...] + term[...].astype(F32)
        west[half * 64 : half * 64 + 64] = total[0:64].astype(BF16)
        own[half * 128 : half * 128 + 128] = total[64:192]
        east[half * 64 : half * 64 + 64] = total[192:256].astype(BF16)


def after_kernel(own, west, east, out):
    out[:, 0:8] = (own[:, 0:8] + west[...].astype(F32)).astype(BF16)
    out[:, 8:16] = (own[:, 8:16] + east[...].astype(F32)).astype(BF16)


def pack_kernel(keep, came, bias, parcel):
    count, rows, _ = parcel.shape
    for a in range(rows // 8):
        for r in range(count):
            at = (a * count + r) * 8
            both = keep[at : at + 8].astype(F32) + came[at : at + 8].astype(F32)
            parcel[r, a * 8 : a * 8 + 8, 0:1024] = both.astype(BF16)
    parcel[:, :, 1024:1152] = jnp.zeros((count, rows, 128), BF16)
    for n in range(3):
        part = bias[:, n * 128 : n * 128 + 128].astype(BF16)
        for r in range(count):
            parcel[r, n * 8 : n * 8 + 8, 1024:1152] = part


def regroup_kernel(came, _, parcel):
    count = parcel.shape[0]
    for a in range(count):
        rows = slice(a * 8, a * 8 + 8)
        total = came[0, rows, 0:1024].astype(F32)
        for r in range(1, came.shape[0]):
            total += came[r, rows, 0:1024].astype(F32)
        parcel[a, :, 0:1024] = total.astype(BF16)
    for n in range(3):
        rows = slice(n * 8, n * 8 + 8)
        total = came[0, rows, 1024:1152].astype(F32)
        for r in range(1, came.shape[0]):
            total += came[r, rows, 1024:1152].astype(F32)
        part = total.astype(BF16)
        for a in range(count):
            parcel[a, :, 1024 + n * 128 : 1152 + n * 128] = part


def total_kernel(came, mine):
    total = came[0].astype(F32)
    for a in range(1, came.shape[0]):
        total += came[a].astype(F32)
    mine[...] = total


def finish_kernel(core, mine, near, other, far, qkv, out, bias):
    here = mine[...] + near[...]
    there = other[...] + far[...]
    is_first = core[0] == 0
    low = jnp.where(is_first, here[:, 0:1024], there[:, 0:1024])
    high = jnp.where(is_first, there[:, 0:1024], here[:, 0:1024])
    qkv[:, 0:1024] = low
    qkv[:, 1024:1536] = high[:, 512:1024]
    out[...] = high[:, 0:512]
    total = here[:, 1024:] + there[:, 1024:]
    for i in range(17):
        bias[i] = total[:, i * 17 : i * 17 + 17]


def whole(shape, dtype):
    return jax.ShapeDtypeStruct(shape, dtype)


def call(kernel, operands, outs, scratch=(), prefetch=0, flops=0, limit=16, untouched=0):
    spec = pl.BlockSpec(memory_space=pltpu.VMEM)
    scalar = pl.BlockSpec(memory_space=pltpu.SMEM)
    size = sum(leaf.size * leaf.dtype.itemsize for leaf in tuple(operands) + tuple(outs))
    return pl.pallas_call(
        kernel,
        out_shape=tuple(outs),
        in_specs=[scalar] * prefetch
        + [spec] * (len(operands) - prefetch - untouched)
        + [pl.BlockSpec(memory_space=pl.ANY)] * untouched,
        out_specs=tuple([spec] * len(outs)),
        scratch_shapes=list(scratch),
        compiler_params=pltpu.CompilerParams(vmem_limit_bytes=limit * MIB),
        cost_estimate=pl.CostEstimate(flops=flops, bytes_accessed=size, transcendentals=0),
        name=kernel.__name__,
    )(*operands)


def shards(tokens, qkv_weight, out_weight, relative_bias, cotangent):
    az, rng = lax.axis_size("az"), lax.axis_size("rng")
    width = tokens.shape[3]
    cells = tokens[0]
    own = cells.reshape(256, width)
    cot = cotangent.reshape(256, width)

    def turn(leaf, step):
        return lax.ppermute(leaf, "az", [(i, (i + step) % az) for i in range(az)])

    def shift(leaf, step):
        pairs = [(i, i + step) for i in range(rng) if 0 <= i + step < rng]
        return lax.ppermute(leaf, "rng", pairs)

    def among(leaf, flip):
        return lax.ppermute(leaf, "dp", [(i, i ^ flip) for i in range(4)])

    left = shift(cells[:, 8:], 1).reshape(128, width)
    right = shift(cells[:, :8], -1).reshape(128, width)
    upper = jnp.concatenate([left[:64], own[:128], right[:64]], axis=0)
    lower = jnp.concatenate([left[64:], own[128:], right[64:]], axis=0)
    above = turn(lower, 1)
    below = turn(upper, -1)

    core = (lax.axis_index("dp") % 2).astype(jnp.int32)[None]
    at_range = lax.axis_index("rng")
    edge = jnp.stack([at_range == 0, at_range == rng - 1]).astype(jnp.int32)
    turned = qkv_weight.T

    q, q_t, da, da_t, table = call(
        before_kernel,
        (edge, own, cot, turned, out_weight, relative_bias),
        (
            whole((256, 512), BF16), whole((512, 256), BF16),
            whole((256, 512), BF16), whole((512, 256), BF16),
            whole((4, 768, 256), F32),
        ),
        prefetch=1,
        flops=600_000_000,
        limit=12,
    )
    middle = call(
        middle_kernel, (upper, lower, turned), (whole((512, 512), BF16),) * 5, flops=1_000_000_000, limit=12
    )
    x_t, dkv, lhs, rhs, bsum, g_send = call(
        attention_kernel,
        (core, above, below, q, q_t, da, da_t, table, *middle, turned, cot),
        (
            whole((512, 1024), BF16), whole((1024, 1024), BF16),
            whole((2, 512, 256), BF16), whole((2, 256, 512), BF16),
            whole((2, 8, 8, 512), F32), whole((512, 1024), BF16),
        ),
        scratch=(
            pltpu.VMEM((1024, 512), BF16), pltpu.VMEM((1024, 512), BF16),
            pltpu.VMEM((512, 1024), BF16), pltpu.VMEM((512, 1024), BF16),
            pltpu.VMEM((512, 256), BF16), pltpu.VMEM((768, 256), F32),
        ),
        prefetch=1,
        flops=10_000_000_000,
        limit=20,
    )
    came = among(g_send, 1)
    g_keep, g_bias, g_above, g_upper, g_lower, g_below = call(
        terms_kernel,
        (core, x_t, dkv, lhs, rhs, bsum, turned),
        (
            whole((512, 1024), BF16), whole((8, 384), F32),
            whole((256, 512), BF16), whole((256, 512), F32),
            whole((256, 512), F32), whole((256, 512), BF16),
        ),
        prefetch=1,
        flops=2_500_000_000,
        limit=12,
    )
    (parcel,) = call(
        pack_kernel,
        (g_keep, came, g_bias),
        (whole((rng, 8 * az, 1152), BF16),),
        flops=1_000_000,
    )
    parcel = lax.all_to_all(parcel, "rng", 0, 0, tiled=True)

    up = turn(g_below, 1)
    down = turn(g_above, -1)
    to_west, g_own, to_east = call(
        fold_kernel,
        (g_upper, g_lower, up, down),
        (whole((128, 512), BF16), whole((256, 512), F32), whole((128, 512), BF16)),
        flops=1_000_000,
    )
    east = shift(to_west.reshape(16, 8, width), -1)
    west = shift(to_east.reshape(16, 8, width), 1)
    (grad_tokens,) = call(
        after_kernel,
        (g_own.reshape(16, 16, width), west, east),
        (whole((16, 16, width), BF16),),
        flops=1_000_000,
    )

    (parcel,) = call(
        regroup_kernel,
        (parcel, grad_tokens),
        (whole((az, 8, 1408), BF16),),
        flops=1_000_000,
        untouched=1,
    )
    parcel = lax.all_to_all(parcel, "az", 0, 0, tiled=True)
    (mine,) = call(total_kernel, (parcel,), (whole((8, 1408), F32),), flops=1_000_000)
    near, other, far = among(mine, 2), among(mine, 1), among(mine, 3)
    rows_qkv, rows_out, total_bias = call(
        finish_kernel,
        (core, mine, near, other, far),
        (whole((8, 1536), F32), whole((8, 512), F32), whole((17, 8, 17), F32)),
        prefetch=1,
        flops=1_000_000,
    )
    total_bias = jnp.transpose(total_bias, (1, 0, 2))
    return (grad_tokens[None], rows_qkv, rows_out, total_bias)


def solution(mesh):
    placed = (P("dp", "az", "rng", None), P(), P(), P(), P("dp", "az", "rng", None))
    return jax.shard_map(
        shards,
        mesh=mesh,
        in_specs=placed,
        out_specs=(P("dp", "az", "rng", None), P(("az", "rng"), None), P(("az", "rng"), None), P()),
        check_vma=False,
    )
```

```python
import functools

import jax
import jax.numpy as jnp
from jax import lax
from jax.experimental import pallas as pl
from jax.experimental.pallas import tpu as pltpu
from jax.sharding import Mesh, PartitionSpec as P


F32 = jnp.float32
BF16 = jnp.bfloat16
ABSENT = -1e30
NT = (((1,), (1,)), ((), ()))
TN = (((0,), (0,)), ((), ()))
MIB = 1024 * 1024


def dot(a, b, dims=(((1,), (0,)), ((), ())), exact=False):
    precision = lax.Precision.HIGHEST if exact else None
    return lax.dot_general(a, b, dims, precision=precision, preferred_element_type=F32)


def iota(shape, axis):
    return lax.broadcasted_iota(jnp.int32, shape, axis)


def row_slots(row):
    base = row // 8 * 256
    at = row % 8
    return (
        (0, 8, base + at * 8),
        (8, 24, base + 64 + at * 16),
        (24, 32, base + 192 + at * 8),
    )


def before_kernel(edge, x, cot, wt, wo, bias, q, q_t, da, da_t, table):
    xv = x[...]
    cv = cot[...]
    q[...] = (dot(xv, wt[0:512], NT).astype(BF16).astype(F32) * 0.125).astype(BF16)
    q_t[...] = (dot(wt[0:512], xv, NT).astype(BF16).astype(F32) * 0.125).astype(BF16)
    da[...] = dot(cv, wo[...], NT).astype(BF16)
    da_t[...] = dot(wo[...], cv, NT).astype(BF16)
    pick = (iota((17, 512), 0) == 23 - (iota((17, 512), 1) >> 4)).astype(F32)
    range_row = iota((32, 512), 0)
    lane = iota((32, 512), 1)
    gap = range_row - (lane & 15)
    first = jnp.where(edge[0] == 1, 8, 0)
    last = jnp.where(edge[1] == 1, 24, 32)
    present = (range_row >= first) & (range_row < last) & (lane >= 112) & (lane < 384)

    def pair_step(pair, carry):
        for side in range(2):
            head_rows = dot(bias[pair * 2 + side], pick, TN, exact=True)
            spread = jnp.full((32, 512), ABSENT, F32)
            for j in range(17):
                spread = jnp.where(gap == j, head_rows[j : j + 1], spread)
            spread = jnp.where(present, spread, ABSENT)
            for v in range(8):
                turned = spread if v == 0 else pltpu.roll(spread, 512 - 16 * v, 1)
                for u in range(3):
                    block = turned[:, 128 * u : 128 * u + 128]
                    for low, high, at in row_slots(23 - 8 * u - v):
                        table[pair, at : at + high - low, side * 128 : side * 128 + 128] = block[
                            low:high
                        ]
        return carry

    lax.fori_loop(0, 4, pair_step, 0)


def project(block, wt, k, v, k_t, v_t, at):
    rows = pl.ds(at, 256)
    keys = dot(block, wt[512:1024], NT).astype(BF16)
    values = dot(block, wt[1024:1536], NT).astype(BF16)
    k[rows] = keys
    v[rows] = values
    k_t[:, rows] = keys.T
    v_t[:, rows] = values.T


def middle_kernel(upper, lower, wt, k, v, k_t, v_t, x_t):
    for at, ref in ((0, upper), (256, lower)):
        project(ref[...], wt, k, v, k_t, v_t, at)
        x_t[:, at : at + 256] = ref[...].T


def by_range(block, rng):
    rows, cols = block.shape
    turned = jnp.transpose(block.reshape(rows // (rng * 8), rng, 8, cols), (1, 0, 2, 3))
    return turned.reshape(rows, cols)


def weight_terms(ref, who, rng, x_t, dkv, lhs, rhs):
    ref[:, 0:512] = by_range(dot(lhs[who], rhs[who]), rng).astype(BF16)
    for n in range(2):
        lanes = pl.ds(pl.multiple_of(who * 512 + n * 256, 256), 256)
        ref[:, 512 + n * 256 : 768 + n * 256] = by_range(dot(x_t[...], dkv[:, lanes]), rng).astype(
            BF16
        )


def attention_kernel(
    rng, core, above, below, q, q_t, da, da_t, table, k_mid, v_mid, kt_mid, vt_mid, xt_mid, wt, cot,
    x_t, dkv, lhs, rhs, bsum, g_send,
    k, v, k_t, v_t, dq_t, dsum,
):
    project(above[...], wt, k, v, k_t, v_t, 0)
    project(below[...], wt, k, v, k_t, v_t, 768)
    k[256:768] = k_mid[...]
    v[256:768] = v_mid[...]
    k_t[:, 256:768] = kt_mid[...]
    v_t[:, 256:768] = vt_mid[...]
    x_t[:, 0:256] = above[...].T
    x_t[:, 256:768] = xt_mid[...]
    x_t[:, 768:1024] = below[...].T
    lhs[0, :, 0:128] = xt_mid[:, 64:192]
    lhs[0, :, 128:256] = xt_mid[:, 320:448]
    rhs[1] = cot[...]

    upper_rows = iota((128, 128), 0) < 64
    upper_lanes = iota((128, 128), 1) < 64
    corner = iota((16, 512), 0) == (iota((16, 512), 1) & 15)

    def split_lanes(block):
        zero = jnp.zeros_like(block)
        return jnp.concatenate(
            [jnp.where(upper_rows, block, zero), jnp.where(upper_rows, zero, block)], axis=1
        )

    def tall(ref, rows, cols, block):
        return dot(ref[rows, cols], block)

    def split_rows(block):
        zero = jnp.zeros_like(block)
        return jnp.concatenate(
            [jnp.where(upper_lanes, block, zero), jnp.where(upper_lanes, zero, block)], axis=0
        )

    def pair_step(pair, carry):
        at = pl.multiple_of(pair * 128, 128)
        cols = pl.ds(at, 128)
        keys = [slice(t * 256, t * 256 + 768) for t in range(2)]
        mine = [slice(t * 128, t * 128 + 128) for t in range(2)]
        da_block = [da_t[cols, mine[t]] for t in range(2)]
        score = [
            tall(k, keys[t], cols, split_lanes(q_t[cols, mine[t]])) + table[pair] for t in range(2)
        ]
        d_prob = [tall(v, keys[t], cols, split_lanes(da_block[t])) for t in range(2)]
        prob, delta, d_value, d_key = [], [], [], []
        for t in range(2):
            top_score = jnp.max(score[t], axis=0, keepdims=True)
            weight = jnp.exp(score[t] - top_score)
            prob.append(weight * (1.0 / jnp.sum(weight, axis=0, keepdims=True)))
        prob_low = [each.astype(BF16) for each in prob]
        for t in range(2):
            mixed = dot(v_t[cols, keys[t]], prob_low[t])
            att = jnp.where(upper_rows, mixed[:, :128], mixed[:, 128:]).astype(BF16)
            lhs[1, cols, mine[t]] = att
            product = att.astype(F32) * da_block[t].astype(F32)
            delta.append(
                jnp.concatenate(
                    [
                        jnp.sum(product[:64], axis=0, keepdims=True),
                        jnp.sum(product[64:], axis=0, keepdims=True),
                    ],
                    axis=1,
                )
            )
            d_value.append(dot(prob_low[t], split_rows(da[mine[t], cols])))
        d_score = [prob[t] * (d_prob[t] - delta[t]) for t in range(2)]
        dsum[...] = d_score[0] + d_score[1]
        for t in range(2):
            score_low = d_score[t].astype(BF16)
            d_q = dot(k_t[cols, keys[t]], score_low)
            dq_t[cols, mine[t]] = (
                jnp.where(upper_rows, d_q[:, :128], d_q[:, 128:]) * 0.125
            ).astype(BF16)
            d_key.append(dot(score_low, split_rows(q[mine[t], cols])))
        tails = ((d_key[0], d_value[0]), (d_key[1], d_value[1]))
        for which in range(2):
            early, late = tails[0][which], tails[1][which]
            to = pl.ds(pl.multiple_of(which * 512 + at, 128), 128)
            dkv[0:256, to] = early[0:256].astype(BF16)
            dkv[256:768, to] = (early[256:768] + late[0:512]).astype(BF16)
            dkv[768:1024, to] = late[512:768].astype(BF16)
        for side in range(2):
            lanes = slice(side * 128, side * 128 + 128)
            total = None
            for turn in range(8):
                parts = [
                    jnp.concatenate(
                        [
                            dsum[to : to + high - low, lanes]
                            for low, high, to in row_slots(23 - 8 * u - turn)
                        ],
                        axis=0,
                    )
                    for u in range(3)
                ]
                strip = jnp.concatenate(parts + [jnp.zeros((32, 128), F32)], axis=1)
                if turn:
                    strip = pltpu.roll(strip, 16 * turn, 1)
                total = strip if total is None else total + strip
            tail = total[16:32]
            last = jnp.where(corner, tail, 0.0)
            rest = jnp.where(corner, 0.0, tail)
            bsum[0, pair * 2 + side] = (
                total[0:8]
                + pltpu.roll(total[8:16], 504, 1)
                + pltpu.roll(rest[0:8], 496, 1)
                + pltpu.roll(rest[8:16], 488, 1)
            )
            bsum[1, pair * 2 + side] = pltpu.roll(last[0:8], 496, 1) + pltpu.roll(
                last[8:16], 488, 1
            )
        return carry

    lax.fori_loop(0, 4, pair_step, 0)

    rhs[0] = dq_t[...].T
    weight_terms(g_send, 1 - core[0], rng, x_t, dkv, lhs, rhs)


def terms_kernel(
    rng, core, x_t, dkv, lhs, rhs, bsum, wt, g_keep, g_bias, g_above, g_upper, g_lower, g_below
):
    weight_terms(g_keep, core[0], rng, x_t, dkv, lhs, rhs)

    spot = iota((512, 384), 0)
    place = iota((512, 384), 1)
    i = (place * 241) >> 12
    j = place - i * 17
    inside = place < 289
    flat = None
    for which in range(2):
        lanes = None
        for b in range(8):
            row = bsum[which, :, b, :]
            row = pltpu.roll(row, 512 - b, 1) if b else row
            lanes = row if lanes is None else lanes + row
        from_lane = 368 - 16 * i - j
        choose = inside & (spot == from_lane) & ((j < 16) if which == 0 else (j == 16))
        part = dot(lanes.astype(BF16), choose.astype(F32).astype(BF16))
        flat = part if flat is None else flat + part
    g_bias[...] = flat

    for g, ref in enumerate((g_above, g_upper, g_lower, g_below)):
        block = dot(dkv[g * 256 : g * 256 + 256], wt[512:1536])
        if g in (0, 3):
            ref[...] = block.astype(BF16)
        else:
            half = (g - 1) * 128
            ref[0:64] = block[0:64]
            ref[64:192] = block[64:192] + dot(rhs[0, half : half + 128], wt[0:512])
            ref[192:256] = block[192:256]


def fold_kernel(g_upper, g_lower, up, down, west, own, east):
    for half, (ref, term) in enumerate(((g_upper, up), (g_lower, down))):
        total = ref[...] + term[...].astype(F32)
        west[half * 64 : half * 64 + 64] = total[0:64].astype(BF16)
        own[half * 128 : half * 128 + 128] = total[64:192]
        east[half * 64 : half * 64 + 64] = total[192:256].astype(BF16)


def after_kernel(own, west, east, out):
    out[:, 0:8] = (own[:, 0:8] + west[...].astype(F32)).astype(BF16)
    out[:, 8:16] = (own[:, 8:16] + east[...].astype(F32)).astype(BF16)


def pack_kernel(keep, came, bias, parcel):
    rows = parcel.shape[1] - 8
    for r in range(parcel.shape[0] // 2):
        at = slice(r * rows, r * rows + rows)
        both = (keep[at].astype(F32) + came[at].astype(F32)).astype(BF16)
        for side in range(2):
            parcel[r * 2 + side, 0:rows] = both[:, side * 512 : side * 512 + 512]
    low = bias[...].astype(BF16)
    for n in range(parcel.shape[0]):
        parcel[n, rows : rows + 8, 0:384] = low
        parcel[n, rows : rows + 8, 384:512] = jnp.zeros((8, 128), BF16)


def regroup_kernel(came, _, parcel):
    total = came[0].astype(F32)
    for n in range(1, came.shape[0]):
        total += came[n].astype(F32)
    rows = came.shape[1] - 8
    low = total.astype(BF16)
    for a in range(parcel.shape[0] // 2):
        for side in range(2):
            parcel[a * 2 + side, 0:8] = low[a * 8 : a * 8 + 8]
            parcel[a * 2 + side, 8:16] = low[rows : rows + 8]


def total_kernel(came, mine):
    for side in range(2):
        total = came[side].astype(F32)
        for a in range(1, came.shape[0] // 2):
            total += came[a * 2 + side].astype(F32)
        mine[:, side * 512 : side * 512 + 512] = total[0:8]
        if side == 0:
            mine[:, 1024:1408] = total[8:16, 0:384]


def finish_kernel(core, here, there, qkv, out, bias):
    is_first = core[0] == 0
    low = jnp.where(is_first, here[:, 0:1024], there[:, 0:1024])
    high = jnp.where(is_first, there[:, 0:1024], here[:, 0:1024])
    qkv[:, 0:1024] = low
    qkv[:, 1024:1536] = high[:, 512:1024]
    out[...] = high[:, 0:512]
    total = here[:, 1024:] + there[:, 1024:]
    for i in range(17):
        bias[i] = total[:, i * 17 : i * 17 + 17]


def whole(shape, dtype):
    return jax.ShapeDtypeStruct(shape, dtype)


def call(kernel, operands, outs, scratch=(), prefetch=0, flops=0, limit=16, untouched=0):
    spec = pl.BlockSpec(memory_space=pltpu.VMEM)
    scalar = pl.BlockSpec(memory_space=pltpu.SMEM)
    size = sum(leaf.size * leaf.dtype.itemsize for leaf in tuple(operands) + tuple(outs))
    return pl.pallas_call(
        kernel,
        out_shape=tuple(outs),
        in_specs=[scalar] * prefetch
        + [spec] * (len(operands) - prefetch - untouched)
        + [pl.BlockSpec(memory_space=pl.ANY)] * untouched,
        out_specs=tuple([spec] * len(outs)),
        scratch_shapes=list(scratch),
        compiler_params=pltpu.CompilerParams(vmem_limit_bytes=limit * MIB),
        cost_estimate=pl.CostEstimate(flops=flops, bytes_accessed=size, transcendentals=0),
    )(*operands)


def shards(tokens, qkv_weight, out_weight, relative_bias, cotangent):
    az, rng = lax.axis_size("az"), lax.axis_size("rng")
    width = tokens.shape[3]
    cells = tokens[0]
    own = cells.reshape(256, width)
    cot = cotangent.reshape(256, width)

    def turn(leaf, step):
        return lax.ppermute(leaf, "az", [(i, (i + step) % az) for i in range(az)])

    def shift(leaf, step):
        pairs = [(i, i + step) for i in range(rng) if 0 <= i + step < rng]
        return lax.ppermute(leaf, "rng", pairs)

    def swap(leaf):
        return lax.ppermute(leaf, "core", [(0, 1), (1, 0)])

    left = shift(cells[:, 8:], 1).reshape(128, width)
    right = shift(cells[:, :8], -1).reshape(128, width)
    upper = jnp.concatenate([left[:64], own[:128], right[:64]], axis=0)
    lower = jnp.concatenate([left[64:], own[128:], right[64:]], axis=0)
    above = turn(lower, 1)
    below = turn(upper, -1)

    core = lax.axis_index("core").astype(jnp.int32)[None]
    at_range = lax.axis_index("rng")
    edge = jnp.stack([at_range == 0, at_range == rng - 1]).astype(jnp.int32)
    turned = qkv_weight.T

    q, q_t, da, da_t, table = call(
        before_kernel,
        (edge, own, cot, turned, out_weight, relative_bias),
        (
            whole((256, 512), BF16), whole((512, 256), BF16),
            whole((256, 512), BF16), whole((512, 256), BF16),
            whole((4, 768, 256), F32),
        ),
        prefetch=1,
        flops=600_000_000,
        limit=12,
    )
    middle = call(
        middle_kernel, (upper, lower, turned), (whole((512, 512), BF16),) * 5, flops=1_000_000_000, limit=12
    )
    x_t, dkv, lhs, rhs, bsum, g_send = call(
        functools.partial(attention_kernel, rng),
        (core, above, below, q, q_t, da, da_t, table, *middle, turned, cot),
        (
            whole((512, 1024), BF16), whole((1024, 1024), BF16),
            whole((2, 512, 256), BF16), whole((2, 256, 512), BF16),
            whole((2, 8, 8, 512), F32), whole((512, 1024), BF16),
        ),
        scratch=(
            pltpu.VMEM((1024, 512), BF16), pltpu.VMEM((1024, 512), BF16),
            pltpu.VMEM((512, 1024), BF16), pltpu.VMEM((512, 1024), BF16),
            pltpu.VMEM((512, 256), BF16), pltpu.VMEM((768, 256), F32),
        ),
        prefetch=1,
        flops=10_000_000_000,
        limit=20,
    )
    came = swap(g_send)
    g_keep, g_bias, g_above, g_upper, g_lower, g_below = call(
        functools.partial(terms_kernel, rng),
        (core, x_t, dkv, lhs, rhs, bsum, turned),
        (
            whole((512, 1024), BF16), whole((8, 384), F32),
            whole((256, 512), BF16), whole((256, 512), F32),
            whole((256, 512), F32), whole((256, 512), BF16),
        ),
        prefetch=1,
        flops=2_500_000_000,
        limit=12,
    )
    (parcel,) = call(
        pack_kernel,
        (g_keep, came, g_bias),
        (whole((rng * 2, 8 * az + 8, 512), BF16),),
        flops=1_000_000,
    )
    parcel = lax.all_to_all(parcel, ("rng", "half"), 0, 0, tiled=True)

    up = turn(g_below, 1)
    down = turn(g_above, -1)
    to_west, g_own, to_east = call(
        fold_kernel,
        (g_upper, g_lower, up, down),
        (whole((128, 512), BF16), whole((256, 512), F32), whole((128, 512), BF16)),
        flops=1_000_000,
    )
    east = shift(to_west.reshape(16, 8, width), -1)
    west = shift(to_east.reshape(16, 8, width), 1)
    (grad_tokens,) = call(
        after_kernel,
        (g_own.reshape(16, 16, width), west, east),
        (whole((16, 16, width), BF16),),
        flops=1_000_000,
    )

    (parcel,) = call(
        regroup_kernel,
        (parcel, g_own),
        (whole((az * 2, 16, 512), BF16),),
        flops=1_000_000,
        untouched=1,
    )
    parcel = lax.all_to_all(parcel, ("az", "half"), 0, 0, tiled=True)
    (mine,) = call(total_kernel, (parcel,), (whole((8, 1408), F32),), flops=1_000_000)
    rows_qkv, rows_out, total_bias = call(
        finish_kernel,
        (core, mine, swap(mine)),
        (whole((8, 1536), F32), whole((8, 512), F32), whole((17, 8, 17), F32)),
        prefetch=1,
        flops=1_000_000,
    )
    total_bias = jnp.transpose(total_bias, (1, 0, 2))
    return (grad_tokens[None], rows_qkv, rows_out, total_bias)


def solution(mesh):
    az, rng, dp = mesh.devices.shape
    split = Mesh(mesh.devices.reshape(az, rng, dp // 2, 2), ("az", "rng", "half", "core"))
    cells = P(("half", "core"), "az", "rng", None)
    rows = P(("az", "rng"), None)
    return jax.shard_map(
        shards,
        mesh=split,
        in_specs=(cells, P(), P(), P(), cells),
        out_specs=(cells, rows, rows, P()),
        check_vma=False,
    )
```

```python
import functools

import jax
import jax.numpy as jnp
from jax import lax
from jax.experimental import pallas as pl
from jax.experimental.pallas import tpu as pltpu
from jax.sharding import Mesh, PartitionSpec as P

F32 = jnp.float32
BF16 = jnp.bfloat16
ABSENT = -1e30
NT = (((1,), (1,)), ((), ()))
TN = (((0,), (0,)), ((), ()))
MIB = 1024 * 1024


def dot(a, b, dims=(((1,), (0,)), ((), ())), exact=False):
    precision = lax.Precision.HIGHEST if exact else None
    return lax.dot_general(a, b, dims, precision=precision, preferred_element_type=F32)


def iota(shape, axis):
    return lax.broadcasted_iota(jnp.int32, shape, axis)


def row_slots(row):
    base = row // 8 * 256
    at = row % 8
    return (
        (0, 8, base + at * 8),
        (8, 24, base + 64 + at * 16),
        (24, 32, base + 192 + at * 8),
    )


def before_kernel(edge, x, cot, wt, wo, bias, q, q_t, da, da_t, table):
    xv = x[...]
    cv = cot[...]
    q[...] = (dot(xv, wt[0:512], NT).astype(BF16).astype(F32) * 0.125).astype(BF16)
    q_t[...] = (dot(wt[0:512], xv, NT).astype(BF16).astype(F32) * 0.125).astype(BF16)
    da[...] = dot(cv, wo[...], NT).astype(BF16)
    da_t[...] = dot(wo[...], cv, NT).astype(BF16)
    pick = (iota((17, 512), 0) == 23 - (iota((17, 512), 1) >> 4)).astype(F32)
    range_row = iota((32, 512), 0)
    lane = iota((32, 512), 1)
    gap = range_row - (lane & 15)
    first = jnp.where(edge[0] == 1, 8, 0)
    last = jnp.where(edge[1] == 1, 24, 32)
    present = (range_row >= first) & (range_row < last) & (lane >= 112) & (lane < 384)

    def pair_step(pair, carry):
        for side in range(2):
            head_rows = dot(bias[pair * 2 + side], pick, TN, exact=True)
            spread = jnp.full((32, 512), ABSENT, F32)
            for j in range(17):
                spread = jnp.where(gap == j, head_rows[j : j + 1], spread)
            spread = jnp.where(present, spread, ABSENT)
            for v in range(8):
                turned = spread if v == 0 else pltpu.roll(spread, 512 - 16 * v, 1)
                for u in range(3):
                    block = turned[:, 128 * u : 128 * u + 128]
                    for low, high, at in row_slots(23 - 8 * u - v):
                        table[pair, at : at + high - low, side * 128 : side * 128 + 128] = block[
                            low:high
                        ]
        return carry

    lax.fori_loop(0, 4, pair_step, 0)


def project(block, wt, k, v, k_t, v_t, at):
    rows = pl.ds(at, 256)
    keys = dot(block, wt[512:1024], NT).astype(BF16)
    values = dot(block, wt[1024:1536], NT).astype(BF16)
    k[rows] = keys
    v[rows] = values
    k_t[:, rows] = keys.T
    v_t[:, rows] = values.T


def middle_kernel(upper, lower, wt, k, v, k_t, v_t, x_t):
    for at, ref in ((0, upper), (256, lower)):
        project(ref[...], wt, k, v, k_t, v_t, at)
        x_t[:, at : at + 256] = ref[...].T


def by_range(block, rng):
    rows, cols = block.shape
    turned = jnp.transpose(block.reshape(rows // (rng * 8), rng, 8, cols), (1, 0, 2, 3))
    return turned.reshape(rows, cols)


def weight_terms(ref, who, rng, x_t, dkv, lhs, rhs):
    ref[:, 0:512] = by_range(dot(lhs[who], rhs[who]), rng).astype(BF16)
    for n in range(2):
        lanes = pl.ds(pl.multiple_of(who * 512 + n * 256, 256), 256)
        ref[:, 512 + n * 256 : 768 + n * 256] = by_range(dot(x_t[...], dkv[:, lanes]), rng).astype(
            BF16
        )


def attention_kernel(
    rng, core, above, below, q, q_t, da, da_t, table, k_mid, v_mid, kt_mid, vt_mid, xt_mid, wt, cot,
    x_t, dkv, lhs, rhs, bsum, g_send,
    k, v, k_t, v_t, dq_t, dsum,
):
    project(above[...], wt, k, v, k_t, v_t, 0)
    project(below[...], wt, k, v, k_t, v_t, 768)
    k[256:768] = k_mid[...]
    v[256:768] = v_mid[...]
    k_t[:, 256:768] = kt_mid[...]
    v_t[:, 256:768] = vt_mid[...]
    x_t[:, 0:256] = above[...].T
    x_t[:, 256:768] = xt_mid[...]
    x_t[:, 768:1024] = below[...].T
    lhs[0, :, 0:128] = xt_mid[:, 64:192]
    lhs[0, :, 128:256] = xt_mid[:, 320:448]
    rhs[1] = cot[...]

    upper_rows = iota((128, 128), 0) < 64
    upper_lanes = iota((128, 128), 1) < 64
    corner = iota((16, 512), 0) == (iota((16, 512), 1) & 15)

    def split_lanes(block):
        zero = jnp.zeros_like(block)
        return jnp.concatenate(
            [jnp.where(upper_rows, block, zero), jnp.where(upper_rows, zero, block)], axis=1
        )

    def tall(ref, rows, cols, block):
        return dot(ref[rows, cols], block)

    def split_rows(block):
        zero = jnp.zeros_like(block)
        return jnp.concatenate(
            [jnp.where(upper_lanes, block, zero), jnp.where(upper_lanes, zero, block)], axis=0
        )

    def pair_step(pair, carry):
        at = pl.multiple_of(pair * 128, 128)
        cols = pl.ds(at, 128)
        keys = [slice(t * 256, t * 256 + 768) for t in range(2)]
        mine = [slice(t * 128, t * 128 + 128) for t in range(2)]
        da_block = [da_t[cols, mine[t]] for t in range(2)]
        score = [
            tall(k, keys[t], cols, split_lanes(q_t[cols, mine[t]])) + table[pair] for t in range(2)
        ]
        d_prob = [tall(v, keys[t], cols, split_lanes(da_block[t])) for t in range(2)]
        prob, delta, d_value, d_key = [], [], [], []
        for t in range(2):
            top_score = jnp.max(score[t], axis=0, keepdims=True)
            weight = jnp.exp(score[t] - top_score)
            prob.append(weight * (1.0 / jnp.sum(weight, axis=0, keepdims=True)))
        prob_low = [each.astype(BF16) for each in prob]
        for t in range(2):
            mixed = dot(v_t[cols, keys[t]], prob_low[t])
            att = jnp.where(upper_rows, mixed[:, :128], mixed[:, 128:]).astype(BF16)
            lhs[1, cols, mine[t]] = att
            product = att.astype(F32) * da_block[t].astype(F32)
            delta.append(
                jnp.concatenate(
                    [
                        jnp.sum(product[:64], axis=0, keepdims=True),
                        jnp.sum(product[64:], axis=0, keepdims=True),
                    ],
                    axis=1,
                )
            )
            d_value.append(dot(prob_low[t], split_rows(da[mine[t], cols])))
        d_score = [prob[t] * (d_prob[t] - delta[t]) for t in range(2)]
        dsum[...] = d_score[0] + d_score[1]
        for t in range(2):
            score_low = d_score[t].astype(BF16)
            d_q = dot(k_t[cols, keys[t]], score_low)
            dq_t[cols, mine[t]] = (
                jnp.where(upper_rows, d_q[:, :128], d_q[:, 128:]) * 0.125
            ).astype(BF16)
            d_key.append(dot(score_low, split_rows(q[mine[t], cols])))
        tails = ((d_key[0], d_value[0]), (d_key[1], d_value[1]))
        for which in range(2):
            early, late = tails[0][which], tails[1][which]
            to = pl.ds(pl.multiple_of(which * 512 + at, 128), 128)
            dkv[0:256, to] = early[0:256].astype(BF16)
            dkv[256:768, to] = (early[256:768] + late[0:512]).astype(BF16)
            dkv[768:1024, to] = late[512:768].astype(BF16)
        for side in range(2):
            lanes = slice(side * 128, side * 128 + 128)
            total = None
            for turn in range(8):
                parts = [
                    jnp.concatenate(
                        [
                            dsum[to : to + high - low, lanes]
                            for low, high, to in row_slots(23 - 8 * u - turn)
                        ],
                        axis=0,
                    )
                    for u in range(3)
                ]
                strip = jnp.concatenate(parts + [jnp.zeros((32, 128), F32)], axis=1)
                if turn:
                    strip = pltpu.roll(strip, 16 * turn, 1)
                total = strip if total is None else total + strip
            tail = total[16:32]
            last = jnp.where(corner, tail, 0.0)
            rest = jnp.where(corner, 0.0, tail)
            bsum[0, pair * 2 + side] = (
                total[0:8]
                + pltpu.roll(total[8:16], 504, 1)
                + pltpu.roll(rest[0:8], 496, 1)
                + pltpu.roll(rest[8:16], 488, 1)
            )
            bsum[1, pair * 2 + side] = pltpu.roll(last[0:8], 496, 1) + pltpu.roll(
                last[8:16], 488, 1
            )
        return carry

    lax.fori_loop(0, 4, pair_step, 0)

    rhs[0] = dq_t[...].T
    weight_terms(g_send, 1 - core[0], rng, x_t, dkv, lhs, rhs)


def terms_kernel(
    rng, core, x_t, dkv, lhs, rhs, bsum, wt, g_keep, g_bias, g_above, g_upper, g_lower, g_below
):
    weight_terms(g_keep, core[0], rng, x_t, dkv, lhs, rhs)

    spot = iota((512, 384), 0)
    place = iota((512, 384), 1)
    i = (place * 241) >> 12
    j = place - i * 17
    inside = place < 289
    flat = None
    for which in range(2):
        lanes = None
        for b in range(8):
            row = bsum[which, :, b, :]
            row = pltpu.roll(row, 512 - b, 1) if b else row
            lanes = row if lanes is None else lanes + row
        from_lane = 368 - 16 * i - j
        choose = inside & (spot == from_lane) & ((j < 16) if which == 0 else (j == 16))
        part = dot(lanes.astype(BF16), choose.astype(F32).astype(BF16))
        flat = part if flat is None else flat + part
    g_bias[...] = flat

    for g, ref in enumerate((g_above, g_upper, g_lower, g_below)):
        block = dot(dkv[g * 256 : g * 256 + 256], wt[512:1536])
        if g in (0, 3):
            ref[...] = block.astype(BF16)
        else:
            half = (g - 1) * 128
            ref[0:64] = block[0:64]
            ref[64:192] = block[64:192] + dot(rhs[0, half : half + 128], wt[0:512])
            ref[192:256] = block[192:256]


def fold_kernel(g_upper, g_lower, up, down, west, own, east):
    for half, (ref, term) in enumerate(((g_upper, up), (g_lower, down))):
        total = ref[...] + term[...].astype(F32)
        west[half * 64 : half * 64 + 64] = total[0:64].astype(BF16)
        own[half * 128 : half * 128 + 128] = total[64:192]
        east[half * 64 : half * 64 + 64] = total[192:256].astype(BF16)


def after_kernel(own, west, east, out):
    out[:, 0:8] = (own[:, 0:8] + west[...].astype(F32)).astype(BF16)
    out[:, 8:16] = (own[:, 8:16] + east[...].astype(F32)).astype(BF16)


def pack_kernel(keep, came, bias, parcel):
    rows = parcel.shape[1] - 8
    low = bias[...].astype(BF16)
    for r in range(parcel.shape[0]):
        at = slice(r * rows, r * rows + rows)
        parcel[r, 0:rows] = (keep[at].astype(F32) + came[at].astype(F32)).astype(BF16)
        parcel[r, rows : rows + 8, 0:384] = low
        parcel[r, rows : rows + 8, 384:1024] = jnp.zeros((8, 640), BF16)


def regroup_kernel(came, _, parcel):
    total = came[0].astype(F32)
    for n in range(1, came.shape[0]):
        total += came[n].astype(F32)
    rows = came.shape[1] - 8
    low = total.astype(BF16)
    for a in range(parcel.shape[0]):
        parcel[a, :, 0:1024] = low[a * 8 : a * 8 + 8]
        parcel[a, :, 1024:1408] = low[rows : rows + 8, 0:384]


def total_kernel(came, mine):
    total = came[0].astype(F32)
    for a in range(1, came.shape[0]):
        total += came[a].astype(F32)
    mine[...] = total


def add_kernel(mine, came, both):
    both[...] = mine[...] + came[...]


def finish_kernel(core, here, there, qkv, out, bias):
    is_first = core[0] == 0
    low = jnp.where(is_first, here[:, 0:1024], there[:, 0:1024])
    high = jnp.where(is_first, there[:, 0:1024], here[:, 0:1024])
    qkv[:, 0:1024] = low
    qkv[:, 1024:1536] = high[:, 512:1024]
    out[...] = high[:, 0:512]
    total = here[:, 1024:] + there[:, 1024:]
    for i in range(17):
        bias[i] = total[:, i * 17 : i * 17 + 17]


def whole(shape, dtype):
    return jax.ShapeDtypeStruct(shape, dtype)


def call(kernel, operands, outs, scratch=(), prefetch=0, flops=0, limit=16, untouched=0):
    spec = pl.BlockSpec(memory_space=pltpu.VMEM)
    scalar = pl.BlockSpec(memory_space=pltpu.SMEM)
    size = sum(leaf.size * leaf.dtype.itemsize for leaf in tuple(operands) + tuple(outs))
    return pl.pallas_call(
        kernel,
        out_shape=tuple(outs),
        in_specs=[scalar] * prefetch
        + [spec] * (len(operands) - prefetch - untouched)
        + [pl.BlockSpec(memory_space=pl.ANY)] * untouched,
        out_specs=tuple([spec] * len(outs)),
        scratch_shapes=list(scratch),
        compiler_params=pltpu.CompilerParams(vmem_limit_bytes=limit * MIB),
        cost_estimate=pl.CostEstimate(flops=flops, bytes_accessed=size, transcendentals=0),
        name=getattr(kernel, "func", kernel).__name__,
    )(*operands)


def shards(tokens, qkv_weight, out_weight, relative_bias, cotangent):
    az, rng = lax.axis_size("az"), lax.axis_size("rng")
    width = tokens.shape[3]
    cells = tokens[0]
    own = cells.reshape(256, width)
    cot = cotangent.reshape(256, width)

    def turn(leaf, step):
        return lax.ppermute(leaf, "az", [(i, (i + step) % az) for i in range(az)])

    def shift(leaf, step):
        pairs = [(i, i + step) for i in range(rng) if 0 <= i + step < rng]
        return lax.ppermute(leaf, "rng", pairs)

    def swap(leaf, axis="core"):
        return lax.ppermute(leaf, axis, [(0, 1), (1, 0)])

    left = shift(cells[:, 8:], 1).reshape(128, width)
    right = shift(cells[:, :8], -1).reshape(128, width)
    upper = jnp.concatenate([left[:64], own[:128], right[:64]], axis=0)
    lower = jnp.concatenate([left[64:], own[128:], right[64:]], axis=0)
    above = turn(lower, 1)
    below = turn(upper, -1)

    core = lax.axis_index("core").astype(jnp.int32)[None]
    at_range = lax.axis_index("rng")
    edge = jnp.stack([at_range == 0, at_range == rng - 1]).astype(jnp.int32)
    turned = qkv_weight.T

    q, q_t, da, da_t, table = call(
        before_kernel,
        (edge, own, cot, turned, out_weight, relative_bias),
        (
            whole((256, 512), BF16), whole((512, 256), BF16),
            whole((256, 512), BF16), whole((512, 256), BF16),
            whole((4, 768, 256), F32),
        ),
        prefetch=1,
        flops=600_000_000,
        limit=12,
    )
    middle = call(
        middle_kernel, (upper, lower, turned), (whole((512, 512), BF16),) * 5, flops=1_000_000_000, limit=12
    )
    x_t, dkv, lhs, rhs, bsum, g_send = call(
        functools.partial(attention_kernel, rng),
        (core, above, below, q, q_t, da, da_t, table, *middle, turned, cot),
        (
            whole((512, 1024), BF16), whole((1024, 1024), BF16),
            whole((2, 512, 256), BF16), whole((2, 256, 512), BF16),
            whole((2, 8, 8, 512), F32), whole((512, 1024), BF16),
        ),
        scratch=(
            pltpu.VMEM((1024, 512), BF16), pltpu.VMEM((1024, 512), BF16),
            pltpu.VMEM((512, 1024), BF16), pltpu.VMEM((512, 1024), BF16),
            pltpu.VMEM((512, 256), BF16), pltpu.VMEM((768, 256), F32),
        ),
        prefetch=1,
        flops=10_000_000_000,
        limit=20,
    )
    came = swap(g_send)
    g_keep, g_bias, g_above, g_upper, g_lower, g_below = call(
        functools.partial(terms_kernel, rng),
        (core, x_t, dkv, lhs, rhs, bsum, turned),
        (
            whole((512, 1024), BF16), whole((8, 384), F32),
            whole((256, 512), BF16), whole((256, 512), F32),
            whole((256, 512), F32), whole((256, 512), BF16),
        ),
        prefetch=1,
        flops=2_500_000_000,
        limit=12,
    )
    (parcel,) = call(
        pack_kernel,
        (g_keep, came, g_bias),
        (whole((rng, 8 * az + 8, 1024), BF16),),
        flops=1_000_000,
    )
    parcel = lax.all_to_all(parcel, "rng", 0, 0, tiled=True)

    up = turn(g_below, 1)
    down = turn(g_above, -1)
    to_west, g_own, to_east = call(
        fold_kernel,
        (g_upper, g_lower, up, down),
        (whole((128, 512), BF16), whole((256, 512), F32), whole((128, 512), BF16)),
        flops=1_000_000,
    )
    east = shift(to_west.reshape(16, 8, width), -1)
    west = shift(to_east.reshape(16, 8, width), 1)
    (grad_tokens,) = call(
        after_kernel,
        (g_own.reshape(16, 16, width), west, east),
        (whole((16, 16, width), BF16),),
        flops=1_000_000,
    )

    (parcel,) = call(
        regroup_kernel,
        (parcel, g_own),
        (whole((az, 8, 1408), BF16),),
        flops=1_000_000,
        untouched=1,
    )
    parcel = lax.all_to_all(parcel, "az", 0, 0, tiled=True)
    (mine,) = call(total_kernel, (parcel,), (whole((8, 1408), F32),), flops=1_000_000)
    (mine,) = call(
        add_kernel, (mine, swap(mine, "half")), (whole((8, 1408), F32),), flops=1_000_000
    )
    rows_qkv, rows_out, total_bias = call(
        finish_kernel,
        (core, mine, swap(mine)),
        (whole((8, 1536), F32), whole((8, 512), F32), whole((17, 8, 17), F32)),
        prefetch=1,
        flops=1_000_000,
    )
    total_bias = jnp.transpose(total_bias, (1, 0, 2))
    return (grad_tokens[None], rows_qkv, rows_out, total_bias)


def solution(mesh):
    az, rng, dp = mesh.devices.shape
    split = Mesh(mesh.devices.reshape(az, rng, dp // 2, 2), ("az", "rng", "half", "core"))
    cells = P(("half", "core"), "az", "rng", None)
    rows = P(("az", "rng"), None)
    return jax.shard_map(
        shards,
        mesh=split,
        in_specs=(cells, P(), P(), P(), cells),
        out_specs=(cells, rows, rows, P()),
        check_vma=False,
    )
```

```python
import functools

import jax
import jax.numpy as jnp
from jax import lax
from jax.experimental import pallas as pl
from jax.experimental.pallas import tpu as pltpu
from jax.sharding import Mesh, PartitionSpec as P

F32 = jnp.float32
BF16 = jnp.bfloat16
ABSENT = -1e30
NT = (((1,), (1,)), ((), ()))
TN = (((0,), (0,)), ((), ()))
MIB = 1024 * 1024


def dot(a, b, dims=(((1,), (0,)), ((), ())), exact=False):
    precision = lax.Precision.HIGHEST if exact else None
    return lax.dot_general(a, b, dims, precision=precision, preferred_element_type=F32)


def iota(shape, axis):
    return lax.broadcasted_iota(jnp.int32, shape, axis)


def row_slots(row):
    base = row // 8 * 256
    at = row % 8
    return (
        (0, 8, base + at * 8),
        (8, 24, base + 64 + at * 16),
        (24, 32, base + 192 + at * 8),
    )


def before_kernel(edge, x, cot, w, wo, bias, q, q_t, da, da_t, table):
    queries = (dot(x[...], w[:, 0:512]).astype(BF16).astype(F32) * 0.125).astype(BF16)
    q[...] = queries
    q_t[...] = queries.T
    d_attended = dot(cot[...], wo[...], NT).astype(BF16)
    da[...] = d_attended
    da_t[...] = d_attended.T
    pick = (iota((17, 512), 0) == 23 - (iota((17, 512), 1) >> 4)).astype(F32)
    range_row = iota((32, 512), 0)
    lane = iota((32, 512), 1)
    gap = range_row - (lane & 15)
    first = jnp.where(edge[0] == 1, 8, 0)
    last = jnp.where(edge[1] == 1, 24, 32)
    present = (range_row >= first) & (range_row < last) & (lane >= 112) & (lane < 384)

    def pair_step(pair, carry):
        for side in range(2):
            head_rows = dot(bias[pair * 2 + side], pick, TN, exact=True)
            spread = jnp.full((32, 512), ABSENT, F32)
            for j in range(17):
                spread = jnp.where(gap == j, head_rows[j : j + 1], spread)
            spread = jnp.where(present, spread, ABSENT)
            for v in range(8):
                turned = spread if v == 0 else pltpu.roll(spread, 512 - 16 * v, 1)
                for u in range(3):
                    block = turned[:, 128 * u : 128 * u + 128]
                    for low, high, at in row_slots(23 - 8 * u - v):
                        table[pair, at : at + high - low, side * 128 : side * 128 + 128] = block[
                            low:high
                        ]
        return carry

    lax.fori_loop(0, 4, pair_step, 0)


def project(block, w, k, v, k_t, v_t, x_t, at):
    rows = slice(at, at + 256)
    keys = dot(block, w[:, 512:1024]).astype(BF16)
    values = dot(block, w[:, 1024:1536]).astype(BF16)
    k[rows] = keys
    v[rows] = values
    k_t[:, rows] = keys.T
    v_t[:, rows] = values.T
    x_t[:, rows] = block.T


def sides_kernel(left, right, upper, lower):
    for half, ref in enumerate((upper, lower)):
        ref[0:64] = left[half * 64 : half * 64 + 64]
        ref[64:128] = right[half * 64 : half * 64 + 64]


def middle_kernel(left, own, right, w, k, v, k_t, v_t, x_t):
    for half in range(2):
        side = slice(half * 64, half * 64 + 64)
        mine = slice(half * 128, half * 128 + 128)
        block = jnp.concatenate([left[side], own[mine], right[side]], axis=0)
        project(block, w, k, v, k_t, v_t, x_t, half * 256)


def by_range(block, rng):
    rows, cols = block.shape
    turned = jnp.transpose(block.reshape(rows // (rng * 8), rng, 8, cols), (1, 0, 2, 3))
    return turned.reshape(rows, cols)


def weight_terms(ref, who, rng, x_t, dkv, lhs, rhs):
    ref[:, 0:512] = by_range(dot(lhs[who], rhs[who]), rng).astype(BF16)
    for n in range(2):
        lanes = pl.ds(pl.multiple_of(who * 512 + n * 256, 256), 256)
        ref[:, 512 + n * 256 : 768 + n * 256] = by_range(dot(x_t[...], dkv[:, lanes]), rng).astype(
            BF16
        )


def attention_kernel(
    rng, core, top, above, bottom, below, q, q_t, da, da_t, table,
    k_mid, v_mid, kt_mid, vt_mid, xt_mid, w, cot,
    x_t, dkv, lhs, rhs, bsum, g_send,
    k, v, k_t, v_t, dq_t, dsum,
):
    for at, own, sides in ((0, top, above), (768, bottom, below)):
        block = jnp.concatenate([sides[0:64], own[...], sides[64:128]], axis=0)
        project(block, w, k, v, k_t, v_t, x_t, at)
    k[256:768] = k_mid[...]
    v[256:768] = v_mid[...]
    k_t[:, 256:768] = kt_mid[...]
    v_t[:, 256:768] = vt_mid[...]
    x_t[:, 256:768] = xt_mid[...]
    lhs[0, :, 0:128] = xt_mid[:, 64:192]
    lhs[0, :, 128:256] = xt_mid[:, 320:448]
    rhs[1] = cot[...]

    upper_rows = iota((128, 128), 0) < 64
    upper_lanes = iota((128, 128), 1) < 64
    corner = iota((16, 512), 0) == (iota((16, 512), 1) & 15)

    def split_lanes(block):
        zero = jnp.zeros_like(block)
        return jnp.concatenate(
            [jnp.where(upper_rows, block, zero), jnp.where(upper_rows, zero, block)], axis=1
        )

    def tall(ref, rows, cols, block):
        return dot(ref[rows, cols], block)

    def split_rows(block):
        zero = jnp.zeros_like(block)
        return jnp.concatenate(
            [jnp.where(upper_lanes, block, zero), jnp.where(upper_lanes, zero, block)], axis=0
        )

    def pair_step(pair, carry):
        at = pl.multiple_of(pair * 128, 128)
        cols = pl.ds(at, 128)
        keys = [slice(t * 256, t * 256 + 768) for t in range(2)]
        mine = [slice(t * 128, t * 128 + 128) for t in range(2)]
        da_block = [da_t[cols, mine[t]] for t in range(2)]
        score = [
            tall(k, keys[t], cols, split_lanes(q_t[cols, mine[t]])) + table[pair] for t in range(2)
        ]
        d_prob = [tall(v, keys[t], cols, split_lanes(da_block[t])) for t in range(2)]
        prob, delta, d_value, d_key = [], [], [], []
        for t in range(2):
            top_score = jnp.max(score[t], axis=0, keepdims=True)
            weight = jnp.exp(score[t] - top_score)
            prob.append(weight * (1.0 / jnp.sum(weight, axis=0, keepdims=True)))
        prob_low = [each.astype(BF16) for each in prob]
        for t in range(2):
            mixed = dot(v_t[cols, keys[t]], prob_low[t])
            att = jnp.where(upper_rows, mixed[:, :128], mixed[:, 128:]).astype(BF16)
            lhs[1, cols, mine[t]] = att
            product = att.astype(F32) * da_block[t].astype(F32)
            delta.append(
                jnp.concatenate(
                    [
                        jnp.sum(product[:64], axis=0, keepdims=True),
                        jnp.sum(product[64:], axis=0, keepdims=True),
                    ],
                    axis=1,
                )
            )
            d_value.append(dot(prob_low[t], split_rows(da[mine[t], cols])))
        d_score = [prob[t] * (d_prob[t] - delta[t]) for t in range(2)]
        dsum[...] = d_score[0] + d_score[1]
        for t in range(2):
            score_low = d_score[t].astype(BF16)
            d_q = dot(k_t[cols, keys[t]], score_low)
            dq_t[cols, mine[t]] = (
                jnp.where(upper_rows, d_q[:, :128], d_q[:, 128:]) * 0.125
            ).astype(BF16)
            d_key.append(dot(score_low, split_rows(q[mine[t], cols])))
        tails = ((d_key[0], d_value[0]), (d_key[1], d_value[1]))
        for which in range(2):
            early, late = tails[0][which], tails[1][which]
            to = pl.ds(pl.multiple_of(which * 512 + at, 128), 128)
            dkv[0:256, to] = early[0:256].astype(BF16)
            dkv[256:768, to] = (early[256:768] + late[0:512]).astype(BF16)
            dkv[768:1024, to] = late[512:768].astype(BF16)
        for side in range(2):
            lanes = slice(side * 128, side * 128 + 128)
            total = None
            for turn in range(8):
                parts = [
                    jnp.concatenate(
                        [
                            dsum[to : to + high - low, lanes]
                            for low, high, to in row_slots(23 - 8 * u - turn)
                        ],
                        axis=0,
                    )
                    for u in range(3)
                ]
                strip = jnp.concatenate(parts + [jnp.zeros((32, 128), F32)], axis=1)
                if turn:
                    strip = pltpu.roll(strip, 16 * turn, 1)
                total = strip if total is None else total + strip
            tail = total[16:32]
            last = jnp.where(corner, tail, 0.0)
            rest = jnp.where(corner, 0.0, tail)
            bsum[0, pair * 2 + side] = (
                total[0:8]
                + pltpu.roll(total[8:16], 504, 1)
                + pltpu.roll(rest[0:8], 496, 1)
                + pltpu.roll(rest[8:16], 488, 1)
            )
            bsum[1, pair * 2 + side] = pltpu.roll(last[0:8], 496, 1) + pltpu.roll(
                last[8:16], 488, 1
            )
        return carry

    lax.fori_loop(0, 4, pair_step, 0, unroll=True)

    rhs[0] = dq_t[...].T
    weight_terms(g_send, 1 - core[0], rng, x_t, dkv, lhs, rhs)


def terms_kernel(
    rng, core, x_t, dkv, lhs, rhs, bsum, w, g_keep, g_bias, g_above, g_upper, g_lower, g_below
):
    weight_terms(g_keep, core[0], rng, x_t, dkv, lhs, rhs)

    spot = iota((512, 384), 0)
    place = iota((512, 384), 1)
    i = (place * 241) >> 12
    j = place - i * 17
    inside = place < 289
    flat = None
    for which in range(2):
        lanes = None
        for b in range(8):
            row = bsum[which, :, b, :]
            row = pltpu.roll(row, 512 - b, 1) if b else row
            lanes = row if lanes is None else lanes + row
        from_lane = 368 - 16 * i - j
        choose = inside & (spot == from_lane) & ((j < 16) if which == 0 else (j == 16))
        part = dot(lanes.astype(BF16), choose.astype(F32).astype(BF16))
        flat = part if flat is None else flat + part
    g_bias[...] = flat

    for g, ref in enumerate((g_above, g_upper, g_lower, g_below)):
        block = dot(dkv[g * 256 : g * 256 + 256], w[:, 512:1536], NT)
        if g in (0, 3):
            ref[...] = block.astype(BF16)
        else:
            half = (g - 1) * 128
            ref[0:64] = block[0:64]
            ref[64:192] = block[64:192] + dot(rhs[0, half : half + 128], w[:, 0:512], NT)
            ref[192:256] = block[192:256]


def fold_kernel(g_upper, g_lower, up, down, west, own, east):
    for half, (ref, term) in enumerate(((g_upper, up), (g_lower, down))):
        total = ref[...] + term[...].astype(F32)
        west[half * 64 : half * 64 + 64] = total[0:64].astype(BF16)
        own[half * 128 : half * 128 + 128] = total[64:192]
        east[half * 64 : half * 64 + 64] = total[192:256].astype(BF16)


def after_kernel(own, west, east, out):
    out[:, 0:8] = (own[:, 0:8] + west[...].astype(F32)).astype(BF16)
    out[:, 8:16] = (own[:, 8:16] + east[...].astype(F32)).astype(BF16)


def pack_kernel(keep, came, bias, parcel):
    count = parcel.shape[0]
    rows = keep.shape[0] // count
    low = bias[...].astype(BF16)
    for r in range(count):
        at = slice(r * rows, r * rows + rows)
        both = (keep[at].astype(F32) + came[at].astype(F32)).astype(BF16)
        for n in range(8):
            parcel[r, n * rows : n * rows + rows] = both[:, n * 128 : n * 128 + 128]
        for n in range(3):
            to = 8 * rows + n * 8
            parcel[r, to : to + 8] = low[:, n * 128 : n * 128 + 128]


def regroup_kernel(came, _, parcel):
    total = came[0].astype(F32)
    for n in range(1, came.shape[0]):
        total += came[n].astype(F32)
    count = parcel.shape[0]
    for a in range(count):
        for n in range(8):
            at = (n * count + a) * 8
            parcel[a, :, n * 128 : n * 128 + 128] = total[at : at + 8].astype(BF16)
        for n in range(3):
            at = count * 64 + n * 8
            parcel[a, :, 1024 + n * 128 : 1152 + n * 128] = total[at : at + 8].astype(BF16)


def total_kernel(came, mine):
    total = came[0].astype(F32)
    for a in range(1, came.shape[0]):
        total += came[a].astype(F32)
    mine[...] = total


def add_kernel(mine, came, both):
    both[...] = mine[...] + came[...]


def finish_kernel(core, here, there, qkv, out, bias):
    is_first = core[0] == 0
    low = jnp.where(is_first, here[:, 0:1024], there[:, 0:1024])
    high = jnp.where(is_first, there[:, 0:1024], here[:, 0:1024])
    qkv[:, 0:1024] = low
    qkv[:, 1024:1536] = high[:, 512:1024]
    out[...] = high[:, 0:512]
    total = here[:, 1024:] + there[:, 1024:]
    for i in range(17):
        bias[i] = total[:, i * 17 : i * 17 + 17]


def whole(shape, dtype):
    return jax.ShapeDtypeStruct(shape, dtype)


def call(kernel, operands, outs, scratch=(), prefetch=0, flops=0, limit=16, untouched=0):
    spec = pl.BlockSpec(memory_space=pltpu.VMEM)
    scalar = pl.BlockSpec(memory_space=pltpu.SMEM)
    size = sum(leaf.size * leaf.dtype.itemsize for leaf in tuple(operands) + tuple(outs))
    return pl.pallas_call(
        kernel,
        out_shape=tuple(outs),
        in_specs=[scalar] * prefetch
        + [spec] * (len(operands) - prefetch - untouched)
        + [pl.BlockSpec(memory_space=pl.ANY)] * untouched,
        out_specs=tuple([spec] * len(outs)),
        scratch_shapes=list(scratch),
        compiler_params=pltpu.CompilerParams(vmem_limit_bytes=limit * MIB),
        cost_estimate=pl.CostEstimate(flops=flops, bytes_accessed=size, transcendentals=0),
        name=getattr(kernel, "func", kernel).__name__,
    )(*operands)


def shards(tokens, qkv_weight, out_weight, relative_bias, cotangent):
    az, rng = lax.axis_size("az"), lax.axis_size("rng")
    width = tokens.shape[3]
    cells = tokens[0]
    own = cells.reshape(256, width)
    cot = cotangent.reshape(256, width)

    def turn(leaf, step):
        return lax.ppermute(leaf, "az", [(i, (i + step) % az) for i in range(az)])

    def shift(leaf, step):
        pairs = [(i, i + step) for i in range(rng) if 0 <= i + step < rng]
        return lax.ppermute(leaf, "rng", pairs)

    def swap(leaf, axis="core"):
        return lax.ppermute(leaf, axis, [(0, 1), (1, 0)])

    left = shift(cells[:, 8:], 1).reshape(128, width)
    right = shift(cells[:, :8], -1).reshape(128, width)
    top = turn(own[128:], 1)
    bottom = turn(own[:128], -1)
    upper, lower = call(
        sides_kernel, (left, right), (whole((128, 512), BF16),) * 2, flops=1_000_000
    )
    above = turn(lower, 1)
    below = turn(upper, -1)

    core = lax.axis_index("core").astype(jnp.int32)[None]
    at_range = lax.axis_index("rng")
    edge = jnp.stack([at_range == 0, at_range == rng - 1]).astype(jnp.int32)

    q, q_t, da, da_t, table = call(
        before_kernel,
        (edge, own, cot, qkv_weight, out_weight, relative_bias),
        (
            whole((256, 512), BF16), whole((512, 256), BF16),
            whole((256, 512), BF16), whole((512, 256), BF16),
            whole((4, 768, 256), F32),
        ),
        prefetch=1,
        flops=600_000_000,
        limit=12,
    )
    middle = call(
        middle_kernel, (left, own, right, qkv_weight), (whole((512, 512), BF16),) * 5, flops=1_000_000_000, limit=12
    )
    x_t, dkv, lhs, rhs, bsum, g_send = call(
        functools.partial(attention_kernel, rng),
        (core, top, above, bottom, below, q, q_t, da, da_t, table, *middle, qkv_weight, cot),
        (
            whole((512, 1024), BF16), whole((1024, 1024), BF16),
            whole((2, 512, 256), BF16), whole((2, 256, 512), BF16),
            whole((2, 8, 8, 512), F32), whole((512, 1024), BF16),
        ),
        scratch=(
            pltpu.VMEM((1024, 512), BF16), pltpu.VMEM((1024, 512), BF16),
            pltpu.VMEM((512, 1024), BF16), pltpu.VMEM((512, 1024), BF16),
            pltpu.VMEM((512, 256), BF16), pltpu.VMEM((768, 256), F32),
        ),
        prefetch=1,
        flops=10_000_000_000,
        limit=20,
    )
    came = swap(g_send)
    g_keep, g_bias, g_above, g_upper, g_lower, g_below = call(
        functools.partial(terms_kernel, rng),
        (core, x_t, dkv, lhs, rhs, bsum, qkv_weight),
        (
            whole((512, 1024), BF16), whole((8, 384), F32),
            whole((256, 512), BF16), whole((256, 512), F32),
            whole((256, 512), F32), whole((256, 512), BF16),
        ),
        prefetch=1,
        flops=2_500_000_000,
        limit=12,
    )
    (parcel,) = call(
        pack_kernel,
        (g_keep, came, g_bias),
        (whole((rng, 64 * az + 24, 128), BF16),),
        flops=1_000_000,
    )
    parcel = lax.all_to_all(parcel, "rng", 0, 0, tiled=True)

    up = turn(g_below, 1)
    down = turn(g_above, -1)
    to_west, g_own, to_east = call(
        fold_kernel,
        (g_upper, g_lower, up, down),
        (whole((128, 512), BF16), whole((256, 512), F32), whole((128, 512), BF16)),
        flops=1_000_000,
    )
    east = shift(to_west.reshape(16, 8, width), -1)
    west = shift(to_east.reshape(16, 8, width), 1)
    (grad_tokens,) = call(
        after_kernel,
        (g_own.reshape(16, 16, width), west, east),
        (whole((16, 16, width), BF16),),
        flops=1_000_000,
    )

    (parcel,) = call(
        regroup_kernel,
        (parcel, g_own),
        (whole((az, 8, 1408), BF16),),
        flops=1_000_000,
        untouched=1,
    )
    parcel = lax.all_to_all(parcel, "az", 0, 0, tiled=True)
    (mine,) = call(total_kernel, (parcel,), (whole((8, 1408), F32),), flops=1_000_000)
    (mine,) = call(
        add_kernel, (mine, swap(mine, "half")), (whole((8, 1408), F32),), flops=1_000_000
    )
    rows_qkv, rows_out, total_bias = call(
        finish_kernel,
        (core, mine, swap(mine)),
        (whole((8, 1536), F32), whole((8, 512), F32), whole((17, 8, 17), F32)),
        prefetch=1,
        flops=1_000_000,
    )
    total_bias = jnp.transpose(total_bias, (1, 0, 2))
    return (grad_tokens[None], rows_qkv, rows_out, total_bias)


def solution(mesh):
    az, rng, dp = mesh.devices.shape
    split = Mesh(mesh.devices.reshape(az, rng, dp // 2, 2), ("az", "rng", "half", "core"))
    cells = P(("half", "core"), "az", "rng", None)
    rows = P(("az", "rng"), None)
    return jax.shard_map(
        shards,
        mesh=split,
        in_specs=(cells, P(), P(), P(), cells),
        out_specs=(cells, rows, rows, P()),
        check_vma=False,
    )
```

```python
import functools

import jax
import jax.numpy as jnp
from jax import lax
from jax.experimental import pallas as pl
from jax.experimental.pallas import tpu as pltpu
from jax.sharding import Mesh, PartitionSpec as P


F32 = jnp.float32
BF16 = jnp.bfloat16
ABSENT = -1e30
NT = (((1,), (1,)), ((), ()))
TN = (((0,), (0,)), ((), ()))
MIB = 1024 * 1024


def dot(a, b, dims=(((1,), (0,)), ((), ())), exact=False):
    precision = lax.Precision.HIGHEST if exact else None
    return lax.dot_general(a, b, dims, precision=precision, preferred_element_type=F32)


def iota(shape, axis):
    return lax.broadcasted_iota(jnp.int32, shape, axis)


def row_slots(row):
    base = row // 8 * 256
    at = row % 8
    return (
        (0, 8, base + at * 8),
        (8, 24, base + 64 + at * 16),
        (24, 32, base + 192 + at * 8),
    )


def slices_kernel(own, to_right, to_left, to_next, to_last, done):
    copies = [
        pltpu.make_async_copy(source, target, done.at[n])
        for n, (source, target) in enumerate(
            (
                (own.at[:, pl.ds(8, 8)], to_right),
                (own.at[:, pl.ds(0, 8)], to_left),
                (own.at[pl.ds(8, 8)], to_next),
                (own.at[pl.ds(0, 8)], to_last),
            )
        )
    ]
    for copy in copies:
        copy.start()
    for copy in copies:
        copy.wait()


def queries_kernel(x, cot, w, wo, q, q_t, da, da_t):
    queries = (dot(x[...], w[:, 0:512]).astype(BF16).astype(F32) * 0.125).astype(BF16)
    q[...] = queries
    q_t[...] = queries.T
    d_attended = dot(cot[...], wo[...], NT).astype(BF16)
    da[...] = d_attended
    da_t[...] = d_attended.T


def table_kernel(edge, bias, table):
    pick = (iota((17, 512), 0) == 23 - (iota((17, 512), 1) >> 4)).astype(F32)
    range_row = iota((32, 512), 0)
    lane = iota((32, 512), 1)
    gap = range_row - (lane & 15)
    first = jnp.where(edge[0] == 1, 8, 0)
    last = jnp.where(edge[1] == 1, 24, 32)
    present = (range_row >= first) & (range_row < last) & (lane >= 112) & (lane < 384)
    for head in range(8):
        pair, lanes = head // 2, slice(head % 2 * 128, head % 2 * 128 + 128)
        head_rows = dot(bias[:, head, :], pick, TN, exact=True)
        spread = jnp.full((32, 512), ABSENT, F32)
        for j in range(17):
            spread = jnp.where(gap == j, head_rows[j : j + 1], spread)
        spread = jnp.where(present, spread, ABSENT)
        for v in range(8):
            turned = spread if v == 0 else pltpu.roll(spread, 512 - 16 * v, 1)
            for u in range(3):
                block = turned[:, 128 * u : 128 * u + 128]
                for low, high, at in row_slots(23 - 8 * u - v):
                    table[pair, at : at + high - low, lanes] = block[low:high]


def project(block, w, k, v, k_t, v_t, x_t, at):
    rows = slice(at, at + 256)
    keys = dot(block, w[:, 512:1024]).astype(BF16)
    values = dot(block, w[:, 1024:1536]).astype(BF16)
    k[rows] = keys
    v[rows] = values
    k_t[:, rows] = keys.T
    v_t[:, rows] = values.T
    x_t[:, rows] = block.T


def sides_kernel(left, right, upper, lower):
    for half, ref in enumerate((upper, lower)):
        ref[0:64] = left[half * 64 : half * 64 + 64]
        ref[64:128] = right[half * 64 : half * 64 + 64]


def middle_kernel(left, own, right, w, k, v, k_t, v_t, x_t):
    for half in range(2):
        side = slice(half * 64, half * 64 + 64)
        mine = slice(half * 128, half * 128 + 128)
        block = jnp.concatenate([left[side], own[mine], right[side]], axis=0)
        project(block, w, k, v, k_t, v_t, x_t, half * 256)


def by_range(block, rng):
    rows, cols = block.shape
    turned = jnp.transpose(block.reshape(rows // (rng * 8), rng, 8, cols), (1, 0, 2, 3))
    return turned.reshape(rows, cols)


def weight_terms(ref, who, rng, x_t, dkv, lhs, rhs):
    ref[:, 0:512] = by_range(dot(lhs[who], rhs[who]), rng).astype(BF16)
    for n in range(2):
        lanes = pl.ds(pl.multiple_of(who * 512 + n * 256, 256), 256)
        ref[:, 512 + n * 256 : 768 + n * 256] = by_range(dot(x_t[...], dkv[:, lanes]), rng).astype(
            BF16
        )


def attention_kernel(
    rng, core, top, above, bottom, below, q, q_t, da, da_t, table,
    k_mid, v_mid, kt_mid, vt_mid, xt_mid, w, cot,
    x_t, dkv, lhs, rhs, bsum, g_send,
    k, v, k_t, v_t, dq_t, dsum,
):
    for at, own, sides in ((0, top, above), (768, bottom, below)):
        block = jnp.concatenate([sides[0:64], own[...], sides[64:128]], axis=0)
        project(block, w, k, v, k_t, v_t, x_t, at)
    k[256:768] = k_mid[...]
    v[256:768] = v_mid[...]
    k_t[:, 256:768] = kt_mid[...]
    v_t[:, 256:768] = vt_mid[...]
    x_t[:, 256:768] = xt_mid[...]
    lhs[0, :, 0:128] = xt_mid[:, 64:192]
    lhs[0, :, 128:256] = xt_mid[:, 320:448]
    rhs[1] = cot[...]

    upper_rows = iota((128, 128), 0) < 64
    upper_lanes = iota((128, 128), 1) < 64
    corner = iota((16, 512), 0) == (iota((16, 512), 1) & 15)

    def split_lanes(block):
        zero = jnp.zeros_like(block)
        return jnp.concatenate(
            [jnp.where(upper_rows, block, zero), jnp.where(upper_rows, zero, block)], axis=1
        )

    def tall(ref, rows, cols, block):
        return dot(ref[rows, cols], block)

    def split_rows(block):
        zero = jnp.zeros_like(block)
        return jnp.concatenate(
            [jnp.where(upper_lanes, block, zero), jnp.where(upper_lanes, zero, block)], axis=0
        )

    def pair_step(pair, carry):
        at = pl.multiple_of(pair * 128, 128)
        cols = pl.ds(at, 128)
        keys = [slice(t * 256, t * 256 + 768) for t in range(2)]
        mine = [slice(t * 128, t * 128 + 128) for t in range(2)]
        da_block = [da_t[cols, mine[t]] for t in range(2)]
        score = [
            tall(k, keys[t], cols, split_lanes(q_t[cols, mine[t]])) + table[pair] for t in range(2)
        ]
        d_prob = [tall(v, keys[t], cols, split_lanes(da_block[t])) for t in range(2)]
        prob, delta, d_value, d_key = [], [], [], []
        for t in range(2):
            top_score = jnp.max(score[t], axis=0, keepdims=True)
            weight = jnp.exp(score[t] - top_score)
            prob.append(weight * (1.0 / jnp.sum(weight, axis=0, keepdims=True)))
        prob_low = [each.astype(BF16) for each in prob]
        for t in range(2):
            mixed = dot(v_t[cols, keys[t]], prob_low[t])
            att = jnp.where(upper_rows, mixed[:, :128], mixed[:, 128:]).astype(BF16)
            lhs[1, cols, mine[t]] = att
            product = att.astype(F32) * da_block[t].astype(F32)
            delta.append(
                jnp.concatenate(
                    [
                        jnp.sum(product[:64], axis=0, keepdims=True),
                        jnp.sum(product[64:], axis=0, keepdims=True),
                    ],
                    axis=1,
                )
            )
            d_value.append(dot(prob_low[t], split_rows(da[mine[t], cols])))
        d_score = [prob[t] * (d_prob[t] - delta[t]) for t in range(2)]
        dsum[...] = d_score[0] + d_score[1]
        for t in range(2):
            score_low = d_score[t].astype(BF16)
            d_q = dot(k_t[cols, keys[t]], score_low)
            dq_t[cols, mine[t]] = (
                jnp.where(upper_rows, d_q[:, :128], d_q[:, 128:]) * 0.125
            ).astype(BF16)
            d_key.append(dot(score_low, split_rows(q[mine[t], cols])))
        tails = ((d_key[0], d_value[0]), (d_key[1], d_value[1]))
        for which in range(2):
            early, late = tails[0][which], tails[1][which]
            to = pl.ds(pl.multiple_of(which * 512 + at, 128), 128)
            dkv[0:256, to] = early[0:256].astype(BF16)
            dkv[256:768, to] = (early[256:768] + late[0:512]).astype(BF16)
            dkv[768:1024, to] = late[512:768].astype(BF16)
        for side in range(2):
            lanes = slice(side * 128, side * 128 + 128)
            total = None
            for turn in range(8):
                parts = [
                    jnp.concatenate(
                        [
                            dsum[to : to + high - low, lanes]
                            for low, high, to in row_slots(23 - 8 * u - turn)
                        ],
                        axis=0,
                    )
                    for u in range(3)
                ]
                strip = jnp.concatenate(parts + [jnp.zeros((32, 128), F32)], axis=1)
                if turn:
                    strip = pltpu.roll(strip, 16 * turn, 1)
                total = strip if total is None else total + strip
            tail = total[16:32]
            last = jnp.where(corner, tail, 0.0)
            rest = jnp.where(corner, 0.0, tail)
            bsum[0, pair * 2 + side] = (
                total[0:8]
                + pltpu.roll(total[8:16], 504, 1)
                + pltpu.roll(rest[0:8], 496, 1)
                + pltpu.roll(rest[8:16], 488, 1)
            )
            bsum[1, pair * 2 + side] = pltpu.roll(last[0:8], 496, 1) + pltpu.roll(
                last[8:16], 488, 1
            )
        return carry

    lax.fori_loop(0, 4, pair_step, 0, unroll=True)

    rhs[0] = dq_t[...].T
    weight_terms(g_send, 1 - core[0], rng, x_t, dkv, lhs, rhs)


def terms_kernel(
    rng, core, x_t, dkv, lhs, rhs, bsum, w, g_keep, g_bias, g_above, g_upper, g_lower, g_below
):
    weight_terms(g_keep, core[0], rng, x_t, dkv, lhs, rhs)

    spot = iota((512, 384), 0)
    place = iota((512, 384), 1)
    i = (place * 241) >> 12
    j = place - i * 17
    inside = place < 289
    flat = None
    for which in range(2):
        lanes = None
        for b in range(8):
            row = bsum[which, :, b, :]
            row = pltpu.roll(row, 512 - b, 1) if b else row
            lanes = row if lanes is None else lanes + row
        from_lane = 368 - 16 * i - j
        choose = inside & (spot == from_lane) & ((j < 16) if which == 0 else (j == 16))
        part = dot(lanes.astype(BF16), choose.astype(F32).astype(BF16))
        flat = part if flat is None else flat + part
    g_bias[...] = flat

    for g, ref in enumerate((g_above, g_upper, g_lower, g_below)):
        block = dot(dkv[g * 256 : g * 256 + 256], w[:, 512:1536], NT)
        if g in (0, 3):
            ref[...] = block.astype(BF16)
        else:
            half = (g - 1) * 128
            ref[0:64] = block[0:64]
            ref[64:192] = block[64:192] + dot(rhs[0, half : half + 128], w[:, 0:512], NT)
            ref[192:256] = block[192:256]


def fold_kernel(g_upper, g_lower, up, down, west, own, east):
    for half, (ref, term) in enumerate(((g_upper, up), (g_lower, down))):
        total = ref[...] + term[...].astype(F32)
        west[half * 64 : half * 64 + 64] = total[0:64].astype(BF16)
        own[half * 128 : half * 128 + 128] = total[64:192]
        east[half * 64 : half * 64 + 64] = total[192:256].astype(BF16)


def after_kernel(own, west, east, out):
    out[:, 0:8] = (own[:, 0:8] + west[...].astype(F32)).astype(BF16)
    out[:, 8:16] = (own[:, 8:16] + east[...].astype(F32)).astype(BF16)


def pack_kernel(keep, came, bias, parcel):
    count = parcel.shape[0]
    rows = keep.shape[0] // count
    low = bias[...].astype(BF16)
    for r in range(count):
        at = slice(r * rows, r * rows + rows)
        both = (keep[at].astype(F32) + came[at].astype(F32)).astype(BF16)
        for n in range(8):
            parcel[r, n * rows : n * rows + rows] = both[:, n * 128 : n * 128 + 128]
        for n in range(3):
            to = 8 * rows + n * 8
            parcel[r, to : to + 8] = low[:, n * 128 : n * 128 + 128]


def regroup_kernel(came, _, parcel):
    total = came[0].astype(F32)
    for n in range(1, came.shape[0]):
        total += came[n].astype(F32)
    count = parcel.shape[0]
    for a in range(count):
        for n in range(8):
            at = (n * count + a) * 8
            parcel[a, :, n * 128 : n * 128 + 128] = total[at : at + 8].astype(BF16)
        for n in range(3):
            at = count * 64 + n * 8
            parcel[a, :, 1024 + n * 128 : 1152 + n * 128] = total[at : at + 8].astype(BF16)


def total_kernel(came, mine):
    total = came[0].astype(F32)
    for a in range(1, came.shape[0]):
        total += came[a].astype(F32)
    mine[...] = total


def add_kernel(mine, came, both):
    both[...] = mine[...] + came[...]


def finish_kernel(core, here, there, qkv, out, bias):
    is_first = core[0] == 0
    low = jnp.where(is_first, here[:, 0:1024], there[:, 0:1024])
    high = jnp.where(is_first, there[:, 0:1024], here[:, 0:1024])
    qkv[:, 0:1024] = low
    qkv[:, 1024:1536] = high[:, 512:1024]
    out[...] = high[:, 0:512]
    total = here[:, 1024:] + there[:, 1024:]
    for i in range(17):
        bias[i] = total[:, i * 17 : i * 17 + 17]


def whole(shape, dtype):
    return jax.ShapeDtypeStruct(shape, dtype)


def call(kernel, operands, outs, scratch=(), prefetch=0, flops=0, limit=16, untouched=0, far=0):
    spec = pl.BlockSpec(memory_space=pltpu.VMEM)
    scalar = pl.BlockSpec(memory_space=pltpu.SMEM)
    size = sum(leaf.size * leaf.dtype.itemsize for leaf in tuple(operands) + tuple(outs))
    return pl.pallas_call(
        kernel,
        out_shape=tuple(outs),
        in_specs=[scalar] * prefetch
        + [spec] * (len(operands) - prefetch - untouched - far)
        + [pl.BlockSpec(memory_space=pl.ANY)] * untouched
        + [pl.BlockSpec(memory_space=pltpu.HBM)] * far,
        out_specs=tuple([spec] * len(outs)),
        scratch_shapes=list(scratch),
        compiler_params=pltpu.CompilerParams(vmem_limit_bytes=limit * MIB),
        cost_estimate=pl.CostEstimate(flops=flops, bytes_accessed=size, transcendentals=0),
    )(*operands)


def shards(tokens, qkv_weight, out_weight, relative_bias, cotangent):
    az, rng = lax.axis_size("az"), lax.axis_size("rng")
    width = tokens.shape[3]
    cells = tokens[0]
    own = cells.reshape(256, width)
    cot = cotangent.reshape(256, width)

    def turn(leaf, step):
        return lax.ppermute(leaf, "az", [(i, (i + step) % az) for i in range(az)])

    def shift(leaf, step):
        pairs = [(i, i + step) for i in range(rng) if 0 <= i + step < rng]
        return lax.ppermute(leaf, "rng", pairs)

    def swap(leaf, axis="core"):
        return lax.ppermute(leaf, axis, [(0, 1), (1, 0)])

    to_right, to_left, to_next, to_last = call(
        slices_kernel,
        (cells,),
        (whole((16, 8, width), BF16),) * 2 + (whole((8, 16, width), BF16),) * 2,
        scratch=(pltpu.SemaphoreType.DMA((4,)),),
        far=1,
        flops=1_000_000,
    )
    left = shift(to_right, 1).reshape(128, width)
    right = shift(to_left, -1).reshape(128, width)
    top = turn(to_next, 1).reshape(128, width)
    bottom = turn(to_last, -1).reshape(128, width)
    upper, lower = call(
        sides_kernel, (left, right), (whole((128, 512), BF16),) * 2, flops=1_000_000
    )
    above = turn(lower, 1)
    below = turn(upper, -1)

    core = lax.axis_index("core").astype(jnp.int32)[None]
    at_range = lax.axis_index("rng")
    edge = jnp.stack([at_range == 0, at_range == rng - 1]).astype(jnp.int32)

    (table,) = call(
        table_kernel,
        (edge, jnp.transpose(relative_bias, (1, 0, 2))),
        (whole((4, 768, 256), F32),),
        prefetch=1,
        flops=100_000_000,
        limit=12,
    )
    q, q_t, da, da_t = call(
        queries_kernel,
        (own, cot, qkv_weight, out_weight),
        (
            whole((256, 512), BF16), whole((512, 256), BF16),
            whole((256, 512), BF16), whole((512, 256), BF16),
        ),
        flops=300_000_000,
        limit=12,
    )
    middle = call(
        middle_kernel, (left, own, right, qkv_weight), (whole((512, 512), BF16),) * 5, flops=1_000_000_000, limit=12
    )
    x_t, dkv, lhs, rhs, bsum, g_send = call(
        functools.partial(attention_kernel, rng),
        (core, top, above, bottom, below, q, q_t, da, da_t, table, *middle, qkv_weight, cot),
        (
            whole((512, 1024), BF16), whole((1024, 1024), BF16),
            whole((2, 512, 256), BF16), whole((2, 256, 512), BF16),
            whole((2, 8, 8, 512), F32), whole((512, 1024), BF16),
        ),
        scratch=(
            pltpu.VMEM((1024, 512), BF16), pltpu.VMEM((1024, 512), BF16),
            pltpu.VMEM((512, 1024), BF16), pltpu.VMEM((512, 1024), BF16),
            pltpu.VMEM((512, 256), BF16), pltpu.VMEM((768, 256), F32),
        ),
        prefetch=1,
        flops=10_000_000_000,
        limit=20,
    )
    came = swap(g_send)
    g_keep, g_bias, g_above, g_upper, g_lower, g_below = call(
        functools.partial(terms_kernel, rng),
        (core, x_t, dkv, lhs, rhs, bsum, qkv_weight),
        (
            whole((512, 1024), BF16), whole((8, 384), F32),
            whole((256, 512), BF16), whole((256, 512), F32),
            whole((256, 512), F32), whole((256, 512), BF16),
        ),
        prefetch=1,
        flops=2_500_000_000,
        limit=12,
    )
    (parcel,) = call(
        pack_kernel,
        (g_keep, came, g_bias),
        (whole((rng, 64 * az + 24, 128), BF16),),
        flops=1_000_000,
    )
    parcel = lax.all_to_all(parcel, "rng", 0, 0, tiled=True)

    up = turn(g_below, 1)
    down = turn(g_above, -1)
    to_west, g_own, to_east = call(
        fold_kernel,
        (g_upper, g_lower, up, down),
        (whole((128, 512), BF16), whole((256, 512), F32), whole((128, 512), BF16)),
        flops=1_000_000,
    )
    east = shift(to_west.reshape(16, 8, width), -1)
    west = shift(to_east.reshape(16, 8, width), 1)
    (grad_tokens,) = call(
        after_kernel,
        (g_own.reshape(16, 16, width), west, east),
        (whole((16, 16, width), BF16),),
        flops=1_000_000,
    )

    (parcel,) = call(
        regroup_kernel,
        (parcel, g_own),
        (whole((az, 8, 1408), BF16),),
        flops=1_000_000,
        untouched=1,
    )
    parcel = lax.all_to_all(parcel, "az", 0, 0, tiled=True)
    (mine,) = call(total_kernel, (parcel,), (whole((8, 1408), F32),), flops=1_000_000)
    (mine,) = call(
        add_kernel, (mine, swap(mine, "half")), (whole((8, 1408), F32),), flops=1_000_000
    )
    rows_qkv, rows_out, total_bias = call(
        finish_kernel,
        (core, mine, swap(mine)),
        (whole((8, 1536), F32), whole((8, 512), F32), whole((17, 8, 17), F32)),
        prefetch=1,
        flops=1_000_000,
    )
    total_bias = jnp.transpose(total_bias, (1, 0, 2))
    return (grad_tokens[None], rows_qkv, rows_out, total_bias)


def solution(mesh):
    az, rng, dp = mesh.devices.shape
    split = Mesh(mesh.devices.reshape(az, rng, dp // 2, 2), ("az", "rng", "half", "core"))
    cells = P(("half", "core"), "az", "rng", None)
    rows = P(("az", "rng"), None)
    return jax.shard_map(
        shards,
        mesh=split,
        in_specs=(cells, P(), P(), P(), cells),
        out_specs=(cells, rows, rows, P()),
        check_vma=False,
    )
```

```python
import functools

import jax
import jax.numpy as jnp
from jax import lax
from jax.experimental import pallas as pl
from jax.experimental.pallas import tpu as pltpu
from jax.sharding import Mesh, PartitionSpec as P


F32 = jnp.float32
BF16 = jnp.bfloat16
ABSENT = -1e30
NT = (((1,), (1,)), ((), ()))
TN = (((0,), (0,)), ((), ()))
MIB = 1024 * 1024


def dot(a, b, dims=(((1,), (0,)), ((), ())), exact=False):
    precision = lax.Precision.HIGHEST if exact else None
    return lax.dot_general(a, b, dims, precision=precision, preferred_element_type=F32)


def iota(shape, axis):
    return lax.broadcasted_iota(jnp.int32, shape, axis)


def row_slots(row):
    base = row // 8 * 256
    at = row % 8
    return (
        (0, 8, base + at * 8),
        (8, 24, base + 64 + at * 16),
        (24, 32, base + 192 + at * 8),
    )


def slices_kernel(own, to_right, to_left, to_next, to_last, done):
    copies = [
        pltpu.make_async_copy(source, target, done.at[n])
        for n, (source, target) in enumerate(
            (
                (own.at[:, pl.ds(8, 8)], to_right),
                (own.at[:, pl.ds(0, 8)], to_left),
                (own.at[pl.ds(8, 8)], to_next),
                (own.at[pl.ds(0, 8)], to_last),
            )
        )
    ]
    for copy in copies:
        copy.start()
    for copy in copies:
        copy.wait()


def queries_kernel(x, cot, w, wo, q, q_t, da, da_t):
    queries = (dot(x[...], w[:, 0:512]).astype(BF16).astype(F32) * 0.125).astype(BF16)
    q[...] = queries
    q_t[...] = queries.T
    d_attended = dot(cot[...], wo[...], NT).astype(BF16)
    da[...] = d_attended
    da_t[...] = d_attended.T


def table_kernel(edge, bias, table):
    pick = (iota((17, 512), 0) == 23 - (iota((17, 512), 1) >> 4)).astype(F32)
    range_row = iota((32, 512), 0)
    lane = iota((32, 512), 1)
    gap = range_row - (lane & 15)
    first = jnp.where(edge[0] == 1, 8, 0)
    last = jnp.where(edge[1] == 1, 24, 32)
    present = (range_row >= first) & (range_row < last) & (lane >= 112) & (lane < 384)
    for head in range(8):
        pair, lanes = head // 2, slice(head % 2 * 128, head % 2 * 128 + 128)
        head_rows = dot(bias[:, head, :], pick, TN, exact=True)
        spread = jnp.full((32, 512), ABSENT, F32)
        for j in range(17):
            spread = jnp.where(gap == j, head_rows[j : j + 1], spread)
        spread = jnp.where(present, spread, ABSENT)
        for v in range(8):
            turned = spread if v == 0 else pltpu.roll(spread, 512 - 16 * v, 1)
            for u in range(3):
                block = turned[:, 128 * u : 128 * u + 128]
                for low, high, at in row_slots(23 - 8 * u - v):
                    table[pair, at : at + high - low, lanes] = block[low:high]


def project(block, w, k, v, k_t, v_t, x_t, at):
    rows = slice(at, at + 256)
    keys = dot(block, w[:, 512:1024]).astype(BF16)
    values = dot(block, w[:, 1024:1536]).astype(BF16)
    k[rows] = keys
    v[rows] = values
    k_t[:, rows] = keys.T
    v_t[:, rows] = values.T
    x_t[:, rows] = block.T


def sides_kernel(left, right, upper, lower):
    for half, ref in enumerate((upper, lower)):
        ref[0:64] = left[half * 64 : half * 64 + 64]
        ref[64:128] = right[half * 64 : half * 64 + 64]


def middle_kernel(left, own, right, w, k, v, k_t, v_t, x_t):
    for half in range(2):
        side = slice(half * 64, half * 64 + 64)
        mine = slice(half * 128, half * 128 + 128)
        block = jnp.concatenate([left[side], own[mine], right[side]], axis=0)
        project(block, w, k, v, k_t, v_t, x_t, half * 256)


def by_range(block, rng):
    rows, cols = block.shape
    turned = jnp.transpose(block.reshape(rows // (rng * 8), rng, 8, cols), (1, 0, 2, 3))
    return turned.reshape(rows, cols)


def weight_terms(ref, who, rng, x_t, dkv, lhs, rhs):
    ref[:, 0:512] = by_range(dot(lhs[who], rhs[who]), rng).astype(BF16)
    for n in range(2):
        lanes = pl.ds(pl.multiple_of(who * 512 + n * 256, 256), 256)
        ref[:, 512 + n * 256 : 768 + n * 256] = by_range(dot(x_t[...], dkv[:, lanes]), rng).astype(
            BF16
        )


def attention_kernel(
    rng, core, top, above, bottom, below, q, q_t, da, da_t, table,
    k_mid, v_mid, kt_mid, vt_mid, xt_mid, w, cot,
    x_t, dkv, lhs, rhs, bsum, g_send,
    k, v, k_t, v_t, dq_t, dsum,
):
    for at, own, sides in ((0, top, above), (768, bottom, below)):
        block = jnp.concatenate([sides[0:64], own[...], sides[64:128]], axis=0)
        project(block, w, k, v, k_t, v_t, x_t, at)
    k[256:768] = k_mid[...]
    v[256:768] = v_mid[...]
    k_t[:, 256:768] = kt_mid[...]
    v_t[:, 256:768] = vt_mid[...]
    x_t[:, 256:768] = xt_mid[...]
    lhs[0, :, 0:128] = xt_mid[:, 64:192]
    lhs[0, :, 128:256] = xt_mid[:, 320:448]
    rhs[1] = cot[...]

    upper_rows = iota((128, 128), 0) < 64
    upper_lanes = iota((128, 128), 1) < 64
    corner = iota((16, 512), 0) == (iota((16, 512), 1) & 15)

    def split_lanes(block):
        zero = jnp.zeros_like(block)
        return jnp.concatenate(
            [jnp.where(upper_rows, block, zero), jnp.where(upper_rows, zero, block)], axis=1
        )

    def tall(ref, rows, cols, block):
        return dot(ref[rows, cols], block)

    def split_rows(block):
        zero = jnp.zeros_like(block)
        return jnp.concatenate(
            [jnp.where(upper_lanes, block, zero), jnp.where(upper_lanes, zero, block)], axis=0
        )

    def pair_step(pair, carry):
        at = pl.multiple_of(pair * 128, 128)
        cols = pl.ds(at, 128)
        keys = [slice(t * 256, t * 256 + 768) for t in range(2)]
        mine = [slice(t * 128, t * 128 + 128) for t in range(2)]
        da_block = [da_t[cols, mine[t]] for t in range(2)]
        score = [
            tall(k, keys[t], cols, split_lanes(q_t[cols, mine[t]])) + table[pair] for t in range(2)
        ]
        d_prob = [tall(v, keys[t], cols, split_lanes(da_block[t])) for t in range(2)]
        prob, delta, d_value, d_key = [], [], [], []
        for t in range(2):
            top_score = jnp.max(score[t], axis=0, keepdims=True)
            weight = jnp.exp(score[t] - top_score)
            prob.append(weight * (1.0 / jnp.sum(weight, axis=0, keepdims=True)))
        prob_low = [each.astype(BF16) for each in prob]
        for t in range(2):
            mixed = dot(v_t[cols, keys[t]], prob_low[t])
            att = jnp.where(upper_rows, mixed[:, :128], mixed[:, 128:]).astype(BF16)
            lhs[1, cols, mine[t]] = att
            product = att.astype(F32) * da_block[t].astype(F32)
            delta.append(
                jnp.concatenate(
                    [
                        jnp.sum(product[:64], axis=0, keepdims=True),
                        jnp.sum(product[64:], axis=0, keepdims=True),
                    ],
                    axis=1,
                )
            )
            d_value.append(dot(prob_low[t], split_rows(da[mine[t], cols])))
        d_score = [prob[t] * (d_prob[t] - delta[t]) for t in range(2)]
        dsum[...] = d_score[0] + d_score[1]
        for t in range(2):
            score_low = d_score[t].astype(BF16)
            d_q = dot(k_t[cols, keys[t]], score_low)
            dq_t[cols, mine[t]] = (
                jnp.where(upper_rows, d_q[:, :128], d_q[:, 128:]) * 0.125
            ).astype(BF16)
            d_key.append(dot(score_low, split_rows(q[mine[t], cols])))
        tails = ((d_key[0], d_value[0]), (d_key[1], d_value[1]))
        for which in range(2):
            early, late = tails[0][which], tails[1][which]
            to = pl.ds(pl.multiple_of(which * 512 + at, 128), 128)
            dkv[0:256, to] = early[0:256].astype(BF16)
            dkv[256:768, to] = (early[256:768] + late[0:512]).astype(BF16)
            dkv[768:1024, to] = late[512:768].astype(BF16)
        for side in range(2):
            lanes = slice(side * 128, side * 128 + 128)
            total = None
            for turn in range(8):
                parts = [
                    jnp.concatenate(
                        [
                            dsum[to : to + high - low, lanes]
                            for low, high, to in row_slots(23 - 8 * u - turn)
                        ],
                        axis=0,
                    )
                    for u in range(3)
                ]
                strip = jnp.concatenate(parts + [jnp.zeros((32, 128), F32)], axis=1)
                if turn:
                    strip = pltpu.roll(strip, 16 * turn, 1)
                total = strip if total is None else total + strip
            tail = total[16:32]
            last = jnp.where(corner, tail, 0.0)
            rest = jnp.where(corner, 0.0, tail)
            bsum[0, pair * 2 + side] = (
                total[0:8]
                + pltpu.roll(total[8:16], 504, 1)
                + pltpu.roll(rest[0:8], 496, 1)
                + pltpu.roll(rest[8:16], 488, 1)
            )
            bsum[1, pair * 2 + side] = pltpu.roll(last[0:8], 496, 1) + pltpu.roll(
                last[8:16], 488, 1
            )
        return carry

    lax.fori_loop(0, 4, pair_step, 0, unroll=True)

    rhs[0] = dq_t[...].T
    weight_terms(g_send, 1 - core[0], rng, x_t, dkv, lhs, rhs)


def terms_kernel(
    rng, core, x_t, dkv, lhs, rhs, bsum, w, g_keep, g_bias, g_above, g_upper, g_lower, g_below
):
    weight_terms(g_keep, core[0], rng, x_t, dkv, lhs, rhs)

    spot = iota((512, 384), 0)
    place = iota((512, 384), 1)
    i = (place * 241) >> 12
    j = place - i * 17
    inside = place < 289
    flat = None
    for which in range(2):
        lanes = None
        for b in range(8):
            row = bsum[which, :, b, :]
            row = pltpu.roll(row, 512 - b, 1) if b else row
            lanes = row if lanes is None else lanes + row
        from_lane = 368 - 16 * i - j
        choose = inside & (spot == from_lane) & ((j < 16) if which == 0 else (j == 16))
        part = dot(lanes.astype(BF16), choose.astype(F32).astype(BF16))
        flat = part if flat is None else flat + part
    g_bias[...] = flat

    for g, ref in enumerate((g_above, g_upper, g_lower, g_below)):
        block = dot(dkv[g * 256 : g * 256 + 256], w[:, 512:1536], NT)
        if g in (0, 3):
            ref[...] = block.astype(BF16)
        else:
            half = (g - 1) * 128
            ref[0:64] = block[0:64]
            ref[64:192] = block[64:192] + dot(rhs[0, half : half + 128], w[:, 0:512], NT)
            ref[192:256] = block[192:256]


def fold_kernel(g_upper, g_lower, up, down, west, own, east):
    for half, (ref, term) in enumerate(((g_upper, up), (g_lower, down))):
        total = ref[...] + term[...].astype(F32)
        west[half * 64 : half * 64 + 64] = total[0:64].astype(BF16)
        own[half * 128 : half * 128 + 128] = total[64:192]
        east[half * 64 : half * 64 + 64] = total[192:256].astype(BF16)


def after_kernel(own, west, east, out):
    out[:, 0:8] = (own[:, 0:8] + west[...].astype(F32)).astype(BF16)
    out[:, 8:16] = (own[:, 8:16] + east[...].astype(F32)).astype(BF16)


def pack_kernel(keep, came, bias, parcel):
    count = parcel.shape[0]
    rows = keep.shape[0] // count
    low = bias[...].astype(BF16)
    for r in range(count):
        at = slice(r * rows, r * rows + rows)
        both = (keep[at].astype(F32) + came[at].astype(F32)).astype(BF16)
        for n in range(8):
            parcel[r, n * rows : n * rows + rows] = both[:, n * 128 : n * 128 + 128]
        for n in range(3):
            to = 8 * rows + n * 8
            parcel[r, to : to + 8] = low[:, n * 128 : n * 128 + 128]


def regroup_kernel(came, _, parcel):
    total = came[0].astype(F32)
    for n in range(1, came.shape[0]):
        total += came[n].astype(F32)
    count = parcel.shape[0]
    for a in range(count):
        for n in range(8):
            at = (n * count + a) * 8
            parcel[a, :, n * 128 : n * 128 + 128] = total[at : at + 8].astype(BF16)
        for n in range(3):
            at = count * 64 + n * 8
            parcel[a, :, 1024 + n * 128 : 1152 + n * 128] = total[at : at + 8].astype(BF16)


def total_kernel(came, mine):
    total = came[0].astype(F32)
    for a in range(1, came.shape[0]):
        total += came[a].astype(F32)
    mine[...] = total


def add_kernel(mine, came, both):
    both[...] = mine[...] + came[...]


def finish_kernel(core, here, there, qkv, out, bias):
    is_first = core[0] == 0
    low = jnp.where(is_first, here[:, 0:1024], there[:, 0:1024])
    high = jnp.where(is_first, there[:, 0:1024], here[:, 0:1024])
    qkv[:, 0:1024] = low
    qkv[:, 1024:1536] = high[:, 512:1024]
    out[...] = high[:, 0:512]
    total = here[:, 1024:] + there[:, 1024:]
    for i in range(17):
        bias[i] = total[:, i * 17 : i * 17 + 17]


def whole(shape, dtype):
    return jax.ShapeDtypeStruct(shape, dtype)


def call(kernel, operands, outs, scratch=(), prefetch=0, flops=0, limit=16, untouched=0, far=0):
    spec = pl.BlockSpec(memory_space=pltpu.VMEM)
    scalar = pl.BlockSpec(memory_space=pltpu.SMEM)
    size = sum(leaf.size * leaf.dtype.itemsize for leaf in tuple(operands) + tuple(outs))
    return pl.pallas_call(
        kernel,
        out_shape=tuple(outs),
        in_specs=[scalar] * prefetch
        + [spec] * (len(operands) - prefetch - untouched - far)
        + [pl.BlockSpec(memory_space=pl.ANY)] * untouched
        + [pl.BlockSpec(memory_space=pltpu.HBM)] * far,
        out_specs=tuple([spec] * len(outs)),
        scratch_shapes=list(scratch),
        compiler_params=pltpu.CompilerParams(vmem_limit_bytes=limit * MIB),
        cost_estimate=pl.CostEstimate(flops=flops, bytes_accessed=size, transcendentals=0),
    )(*operands)


def shards(tokens, qkv_weight, out_weight, relative_bias, cotangent):
    az, rng = lax.axis_size("az"), lax.axis_size("rng")
    width = tokens.shape[3]
    cells = tokens[0]
    own = cells.reshape(256, width)
    cot = cotangent.reshape(256, width)

    def turn(leaf, step):
        return lax.ppermute(leaf, "az", [(i, (i + step) % az) for i in range(az)])

    def shift(leaf, step):
        pairs = [(i, i + step) for i in range(rng) if 0 <= i + step < rng]
        return lax.ppermute(leaf, "rng", pairs)

    def swap(leaf, axis="core"):
        return lax.ppermute(leaf, axis, [(0, 1), (1, 0)])

    to_right, to_left, to_next, to_last = call(
        slices_kernel,
        (cells,),
        (whole((16, 8, width), BF16),) * 2 + (whole((8, 16, width), BF16),) * 2,
        scratch=(pltpu.SemaphoreType.DMA((4,)),),
        far=1,
        flops=1_000_000,
    )
    left = shift(to_right, 1).reshape(128, width)
    right = shift(to_left, -1).reshape(128, width)
    top = turn(to_next, 1).reshape(128, width)
    bottom = turn(to_last, -1).reshape(128, width)
    upper, lower = call(
        sides_kernel, (left, right), (whole((128, 512), BF16),) * 2, flops=1_000_000
    )
    above = turn(lower, 1)
    below = turn(upper, -1)

    core = lax.axis_index("core").astype(jnp.int32)[None]
    at_range = lax.axis_index("rng")
    edge = jnp.stack([at_range == 0, at_range == rng - 1]).astype(jnp.int32)

    (table,) = call(
        table_kernel,
        (edge, jnp.transpose(relative_bias, (1, 0, 2))),
        (whole((4, 768, 256), F32),),
        prefetch=1,
        flops=100_000_000,
        limit=12,
    )
    q, q_t, da, da_t = call(
        queries_kernel,
        (own, cot, qkv_weight, out_weight),
        (
            whole((256, 512), BF16), whole((512, 256), BF16),
            whole((256, 512), BF16), whole((512, 256), BF16),
        ),
        flops=300_000_000,
        limit=12,
    )
    middle = call(
        middle_kernel, (left, own, right, qkv_weight), (whole((512, 512), BF16),) * 5, flops=1_000_000_000, limit=12
    )
    x_t, dkv, lhs, rhs, bsum, g_send = call(
        functools.partial(attention_kernel, rng),
        (core, top, above, bottom, below, q, q_t, da, da_t, table, *middle, qkv_weight, cot),
        (
            whole((512, 1024), BF16), whole((1024, 1024), BF16),
            whole((2, 512, 256), BF16), whole((2, 256, 512), BF16),
            whole((2, 8, 8, 512), F32), whole((512, 1024), BF16),
        ),
        scratch=(
            pltpu.VMEM((1024, 512), BF16), pltpu.VMEM((1024, 512), BF16),
            pltpu.VMEM((512, 1024), BF16), pltpu.VMEM((512, 1024), BF16),
            pltpu.VMEM((512, 256), BF16), pltpu.VMEM((768, 256), F32),
        ),
        prefetch=1,
        flops=10_000_000_000,
        limit=20,
    )
    came = swap(g_send)
    g_keep, g_bias, g_above, g_upper, g_lower, g_below = call(
        functools.partial(terms_kernel, rng),
        (core, x_t, dkv, lhs, rhs, bsum, qkv_weight),
        (
            whole((512, 1024), BF16), whole((8, 384), F32),
            whole((256, 512), BF16), whole((256, 512), F32),
            whole((256, 512), F32), whole((256, 512), BF16),
        ),
        prefetch=1,
        flops=2_500_000_000,
        limit=12,
    )
    (parcel,) = call(
        pack_kernel,
        (g_keep, came, g_bias),
        (whole((rng, 64 * az + 24, 128), BF16),),
        flops=1_000_000,
    )
    parcel = lax.all_to_all(parcel, "rng", 0, 0, tiled=True)

    up = turn(g_below, 1)
    down = turn(g_above, -1)
    to_west, g_own, to_east = call(
        fold_kernel,
        (g_upper, g_lower, up, down),
        (whole((128, 512), BF16), whole((256, 512), F32), whole((128, 512), BF16)),
        flops=1_000_000,
    )
    east = shift(to_west.reshape(16, 8, width), -1)
    west = shift(to_east.reshape(16, 8, width), 1)
    (grad_tokens,) = call(
        after_kernel,
        (g_own.reshape(16, 16, width), west, east),
        (whole((16, 16, width), BF16),),
        flops=1_000_000,
    )

    (parcel,) = call(
        regroup_kernel,
        (parcel, g_own),
        (whole((az, 8, 1408), BF16),),
        flops=1_000_000,
        untouched=1,
    )
    parcel = lax.all_to_all(parcel, "az", 0, 0, tiled=True)
    (mine,) = call(total_kernel, (parcel,), (whole((8, 1408), F32),), flops=1_000_000)
    near = swap(mine, "half")
    (mine,) = call(add_kernel, (mine, near), (whole((8, 1408), F32),), flops=1_000_000)
    rows_qkv, rows_out, total_bias = call(
        finish_kernel,
        (core, mine, swap(mine)),
        (whole((8, 1536), F32), whole((8, 512), F32), whole((17, 8, 17), F32)),
        prefetch=1,
        flops=1_000_000,
    )
    total_bias = jnp.transpose(total_bias, (1, 0, 2))
    return (grad_tokens[None], rows_qkv, rows_out, total_bias)


def solution(mesh):
    az, rng, dp = mesh.devices.shape
    split = Mesh(mesh.devices.reshape(az, rng, dp // 2, 2), ("az", "rng", "half", "core"))
    cells = P(("half", "core"), "az", "rng", None)
    rows = P(("az", "rng"), None)
    return jax.shard_map(
        shards,
        mesh=split,
        in_specs=(cells, P(), P(), P(), cells),
        out_specs=(cells, rows, rows, P()),
        check_vma=False,
    )
```

```python
import functools

import jax
import jax.numpy as jnp
from jax import lax
from jax.experimental import pallas as pl
from jax.experimental.pallas import tpu as pltpu
from jax.sharding import Mesh, PartitionSpec as P


F32 = jnp.float32
BF16 = jnp.bfloat16
ABSENT = -1e30
NT = (((1,), (1,)), ((), ()))
TN = (((0,), (0,)), ((), ()))
MIB = 1024 * 1024


def dot(a, b, dims=(((1,), (0,)), ((), ())), exact=False):
    precision = lax.Precision.HIGHEST if exact else None
    return lax.dot_general(a, b, dims, precision=precision, preferred_element_type=F32)


def iota(shape, axis):
    return lax.broadcasted_iota(jnp.int32, shape, axis)


def row_slots(row):
    base = row // 8 * 256
    at = row % 8
    return (
        (0, 8, base + at * 8),
        (8, 24, base + 64 + at * 16),
        (24, 32, base + 192 + at * 8),
    )


def slices_kernel(own, to_right, to_left, to_next, to_last, done):
    copies = [
        pltpu.make_async_copy(source, target, done.at[n])
        for n, (source, target) in enumerate(
            (
                (own.at[:, pl.ds(8, 8)], to_right),
                (own.at[:, pl.ds(0, 8)], to_left),
                (own.at[pl.ds(8, 8)], to_next),
                (own.at[pl.ds(0, 8)], to_last),
            )
        )
    ]
    for copy in copies:
        copy.start()
    for copy in copies:
        copy.wait()


def queries_kernel(x, cot, w, wo, q, q_t, da, da_t):
    queries = (dot(x[...], w[:, 0:512]).astype(BF16).astype(F32) * 0.125).astype(BF16)
    q[...] = queries
    q_t[...] = queries.T
    d_attended = dot(cot[...], wo[...], NT).astype(BF16)
    da[...] = d_attended
    da_t[...] = d_attended.T


def table_kernel(edge, bias_far, table, bias, done):
    copy = pltpu.make_async_copy(bias_far, bias, done)
    copy.start()
    pick = (iota((17, 512), 0) == 23 - (iota((17, 512), 1) >> 4)).astype(F32)
    range_row = iota((32, 512), 0)
    lane = iota((32, 512), 1)
    gap = range_row - (lane & 15)
    first = jnp.where(edge[0] == 1, 8, 0)
    last = jnp.where(edge[1] == 1, 24, 32)
    present = (range_row >= first) & (range_row < last) & (lane >= 112) & (lane < 384)
    copy.wait()
    for head in range(8):
        pair, lanes = head // 2, slice(head % 2 * 128, head % 2 * 128 + 128)
        head_rows = dot(bias[:, head, :], pick, TN, exact=True)
        spread = jnp.full((32, 512), ABSENT, F32)
        for j in range(17):
            spread = jnp.where(gap == j, head_rows[j : j + 1], spread)
        spread = jnp.where(present, spread, ABSENT)
        for v in range(8):
            turned = spread if v == 0 else pltpu.roll(spread, 512 - 16 * v, 1)
            for u in range(3):
                block = turned[:, 128 * u : 128 * u + 128]
                for low, high, at in row_slots(23 - 8 * u - v):
                    table[pair, at : at + high - low, lanes] = block[low:high]


def project(block, w, k, v, k_t, v_t, x_t, at):
    rows = slice(at, at + 256)
    keys = dot(block, w[:, 512:1024]).astype(BF16)
    values = dot(block, w[:, 1024:1536]).astype(BF16)
    k[rows] = keys
    v[rows] = values
    k_t[:, rows] = keys.T
    v_t[:, rows] = values.T
    x_t[:, rows] = block.T


def sides_kernel(left, right, upper, lower):
    for half, ref in enumerate((upper, lower)):
        ref[0:64] = left[half * 64 : half * 64 + 64]
        ref[64:128] = right[half * 64 : half * 64 + 64]


def middle_kernel(left, own, right, w, k, v, k_t, v_t, x_t):
    for half in range(2):
        side = slice(half * 64, half * 64 + 64)
        mine = slice(half * 128, half * 128 + 128)
        block = jnp.concatenate([left[side], own[mine], right[side]], axis=0)
        project(block, w, k, v, k_t, v_t, x_t, half * 256)


def by_range(block, rng):
    rows, cols = block.shape
    turned = jnp.transpose(block.reshape(rows // (rng * 8), rng, 8, cols), (1, 0, 2, 3))
    return turned.reshape(rows, cols)


def weight_terms(ref, who, rng, x_t, dkv, lhs, rhs):
    ref[:, 0:512] = by_range(dot(lhs[who], rhs[who]), rng).astype(BF16)
    for n in range(2):
        lanes = pl.ds(pl.multiple_of(who * 512 + n * 256, 256), 256)
        ref[:, 512 + n * 256 : 768 + n * 256] = by_range(dot(x_t[...], dkv[:, lanes]), rng).astype(
            BF16
        )


def attention_kernel(
    rng, core, top, above, bottom, below, q, q_t, da, da_t, table,
    k_mid, v_mid, kt_mid, vt_mid, xt_mid, w, cot,
    x_t, dkv, lhs, rhs, bsum, g_send,
    k, v, k_t, v_t, dq_t, dsum,
):
    for at, own, sides in ((0, top, above), (768, bottom, below)):
        block = jnp.concatenate([sides[0:64], own[...], sides[64:128]], axis=0)
        project(block, w, k, v, k_t, v_t, x_t, at)
    k[256:768] = k_mid[...]
    v[256:768] = v_mid[...]
    k_t[:, 256:768] = kt_mid[...]
    v_t[:, 256:768] = vt_mid[...]
    x_t[:, 256:768] = xt_mid[...]
    lhs[0, :, 0:128] = xt_mid[:, 64:192]
    lhs[0, :, 128:256] = xt_mid[:, 320:448]
    rhs[1] = cot[...]

    upper_rows = iota((128, 128), 0) < 64
    upper_lanes = iota((128, 128), 1) < 64
    corner = iota((16, 512), 0) == (iota((16, 512), 1) & 15)

    def split_lanes(block):
        zero = jnp.zeros_like(block)
        return jnp.concatenate(
            [jnp.where(upper_rows, block, zero), jnp.where(upper_rows, zero, block)], axis=1
        )

    def tall(ref, rows, cols, block):
        return dot(ref[rows, cols], block)

    def split_rows(block):
        zero = jnp.zeros_like(block)
        return jnp.concatenate(
            [jnp.where(upper_lanes, block, zero), jnp.where(upper_lanes, zero, block)], axis=0
        )

    def pair_step(pair, carry):
        at = pl.multiple_of(pair * 128, 128)
        cols = pl.ds(at, 128)
        keys = [slice(t * 256, t * 256 + 768) for t in range(2)]
        mine = [slice(t * 128, t * 128 + 128) for t in range(2)]
        da_block = [da_t[cols, mine[t]] for t in range(2)]
        score = [
            tall(k, keys[t], cols, split_lanes(q_t[cols, mine[t]])) + table[pair] for t in range(2)
        ]
        d_prob = [tall(v, keys[t], cols, split_lanes(da_block[t])) for t in range(2)]
        prob, delta, d_value, d_key = [], [], [], []
        for t in range(2):
            top_score = jnp.max(score[t], axis=0, keepdims=True)
            weight = jnp.exp(score[t] - top_score)
            prob.append(weight * (1.0 / jnp.sum(weight, axis=0, keepdims=True)))
        prob_low = [each.astype(BF16) for each in prob]
        for t in range(2):
            mixed = dot(v_t[cols, keys[t]], prob_low[t])
            att = jnp.where(upper_rows, mixed[:, :128], mixed[:, 128:]).astype(BF16)
            lhs[1, cols, mine[t]] = att
            product = att.astype(F32) * da_block[t].astype(F32)
            delta.append(
                jnp.concatenate(
                    [
                        jnp.sum(product[:64], axis=0, keepdims=True),
                        jnp.sum(product[64:], axis=0, keepdims=True),
                    ],
                    axis=1,
                )
            )
            d_value.append(dot(prob_low[t], split_rows(da[mine[t], cols])))
        d_score = [prob[t] * (d_prob[t] - delta[t]) for t in range(2)]
        dsum[...] = d_score[0] + d_score[1]
        for t in range(2):
            score_low = d_score[t].astype(BF16)
            d_q = dot(k_t[cols, keys[t]], score_low)
            dq_t[cols, mine[t]] = (
                jnp.where(upper_rows, d_q[:, :128], d_q[:, 128:]) * 0.125
            ).astype(BF16)
            d_key.append(dot(score_low, split_rows(q[mine[t], cols])))
        tails = ((d_key[0], d_value[0]), (d_key[1], d_value[1]))
        for which in range(2):
            early, late = tails[0][which], tails[1][which]
            to = pl.ds(pl.multiple_of(which * 512 + at, 128), 128)
            dkv[0:256, to] = early[0:256].astype(BF16)
            dkv[256:768, to] = (early[256:768] + late[0:512]).astype(BF16)
            dkv[768:1024, to] = late[512:768].astype(BF16)
        for side in range(2):
            lanes = slice(side * 128, side * 128 + 128)
            total = None
            for turn in range(8):
                parts = [
                    jnp.concatenate(
                        [
                            dsum[to : to + high - low, lanes]
                            for low, high, to in row_slots(23 - 8 * u - turn)
                        ],
                        axis=0,
                    )
                    for u in range(3)
                ]
                strip = jnp.concatenate(parts + [jnp.zeros((32, 128), F32)], axis=1)
                if turn:
                    strip = pltpu.roll(strip, 16 * turn, 1)
                total = strip if total is None else total + strip
            tail = total[16:32]
            last = jnp.where(corner, tail, 0.0)
            rest = jnp.where(corner, 0.0, tail)
            bsum[0, pair * 2 + side] = (
                total[0:8]
                + pltpu.roll(total[8:16], 504, 1)
                + pltpu.roll(rest[0:8], 496, 1)
                + pltpu.roll(rest[8:16], 488, 1)
            )
            bsum[1, pair * 2 + side] = pltpu.roll(last[0:8], 496, 1) + pltpu.roll(
                last[8:16], 488, 1
            )
        return carry

    lax.fori_loop(0, 4, pair_step, 0, unroll=True)

    rhs[0] = dq_t[...].T
    weight_terms(g_send, 1 - core[0], rng, x_t, dkv, lhs, rhs)


def terms_kernel(
    rng, core, x_t, dkv, lhs, rhs, bsum, w, g_keep, g_bias, g_above, g_upper, g_lower, g_below
):
    weight_terms(g_keep, core[0], rng, x_t, dkv, lhs, rhs)

    spot = iota((512, 384), 0)
    place = iota((512, 384), 1)
    i = (place * 241) >> 12
    j = place - i * 17
    inside = place < 289
    flat = None
    for which in range(2):
        lanes = None
        for b in range(8):
            row = bsum[which, :, b, :]
            row = pltpu.roll(row, 512 - b, 1) if b else row
            lanes = row if lanes is None else lanes + row
        from_lane = 368 - 16 * i - j
        choose = inside & (spot == from_lane) & ((j < 16) if which == 0 else (j == 16))
        part = dot(lanes.astype(BF16), choose.astype(F32).astype(BF16))
        flat = part if flat is None else flat + part
    g_bias[...] = flat

    for g, ref in enumerate((g_above, g_upper, g_lower, g_below)):
        block = dot(dkv[g * 256 : g * 256 + 256], w[:, 512:1536], NT)
        if g in (0, 3):
            ref[...] = block.astype(BF16)
        else:
            half = (g - 1) * 128
            ref[0:64] = block[0:64]
            ref[64:192] = block[64:192] + dot(rhs[0, half : half + 128], w[:, 0:512], NT)
            ref[192:256] = block[192:256]


def fold_kernel(g_upper, g_lower, up, down, west, own, east):
    for half, (ref, term) in enumerate(((g_upper, up), (g_lower, down))):
        total = ref[...] + term[...].astype(F32)
        west[half * 64 : half * 64 + 64] = total[0:64].astype(BF16)
        own[half * 128 : half * 128 + 128] = total[64:192]
        east[half * 64 : half * 64 + 64] = total[192:256].astype(BF16)


def after_kernel(own, west, east, out):
    out[:, 0:8] = (own[:, 0:8] + west[...].astype(F32)).astype(BF16)
    out[:, 8:16] = (own[:, 8:16] + east[...].astype(F32)).astype(BF16)


def pack_kernel(keep, came, bias, parcel, block, done):
    count = parcel.shape[0]
    rows = keep.shape[0] // count
    low = bias[...].astype(BF16)
    copies = []
    for r in range(count):
        at = slice(r * rows, r * rows + rows)
        both = (keep[at].astype(F32) + came[at].astype(F32)).astype(BF16)
        for n in range(8):
            block[r, n * rows : n * rows + rows] = both[:, n * 128 : n * 128 + 128]
        for n in range(3):
            to = 8 * rows + n * 8
            block[r, to : to + 8] = low[:, n * 128 : n * 128 + 128]
        copies.append(pltpu.make_async_copy(block.at[r], parcel.at[r], done.at[r]))
        copies[-1].start()
    for copy in copies:
        copy.wait()


def regroup_kernel(came, _, parcel):
    total = came[0].astype(F32)
    for n in range(1, came.shape[0]):
        total += came[n].astype(F32)
    count = parcel.shape[0]
    for a in range(count):
        for n in range(8):
            at = (n * count + a) * 8
            parcel[a, :, n * 128 : n * 128 + 128] = total[at : at + 8].astype(BF16)
        for n in range(3):
            at = count * 64 + n * 8
            parcel[a, :, 1024 + n * 128 : 1152 + n * 128] = total[at : at + 8].astype(BF16)


def total_kernel(came, mine):
    total = came[0].astype(F32)
    for a in range(1, came.shape[0]):
        total += came[a].astype(F32)
    mine[...] = total


def add_kernel(mine, came, both):
    both[...] = mine[...] + came[...]


def finish_kernel(core, here, there, qkv, out, bias):
    is_first = core[0] == 0
    low = jnp.where(is_first, here[:, 0:1024], there[:, 0:1024])
    high = jnp.where(is_first, there[:, 0:1024], here[:, 0:1024])
    qkv[:, 0:1024] = low
    qkv[:, 1024:1536] = high[:, 512:1024]
    out[...] = high[:, 0:512]
    total = here[:, 1024:] + there[:, 1024:]
    for i in range(17):
        bias[i] = total[:, i * 17 : i * 17 + 17]


def whole(shape, dtype):
    return jax.ShapeDtypeStruct(shape, dtype)


def call(kernel, operands, outs, scratch=(), prefetch=0, flops=0, limit=16, untouched=0, far=0, outside=False):
    spec = pl.BlockSpec(memory_space=pltpu.VMEM)
    scalar = pl.BlockSpec(memory_space=pltpu.SMEM)
    size = sum(leaf.size * leaf.dtype.itemsize for leaf in tuple(operands) + tuple(outs))
    return pl.pallas_call(
        kernel,
        out_shape=tuple(outs),
        in_specs=[scalar] * prefetch
        + [spec] * (len(operands) - prefetch - untouched - far)
        + [pl.BlockSpec(memory_space=pl.ANY)] * untouched
        + [pl.BlockSpec(memory_space=pltpu.HBM)] * far,
        out_specs=tuple([pl.BlockSpec(memory_space=pl.ANY) if outside else spec] * len(outs)),
        scratch_shapes=list(scratch),
        compiler_params=pltpu.CompilerParams(vmem_limit_bytes=limit * MIB),
        cost_estimate=pl.CostEstimate(flops=flops, bytes_accessed=size, transcendentals=0),
    )(*operands)


def shards(tokens, qkv_weight, out_weight, relative_bias, cotangent):
    az, rng = lax.axis_size("az"), lax.axis_size("rng")
    width = tokens.shape[3]
    cells = tokens[0]
    own = cells.reshape(256, width)
    cot = cotangent.reshape(256, width)

    def turn(leaf, step):
        return lax.ppermute(leaf, "az", [(i, (i + step) % az) for i in range(az)])

    def shift(leaf, step):
        pairs = [(i, i + step) for i in range(rng) if 0 <= i + step < rng]
        return lax.ppermute(leaf, "rng", pairs)

    def swap(leaf, axis="core"):
        return lax.ppermute(leaf, axis, [(0, 1), (1, 0)])

    to_right, to_left, to_next, to_last = call(
        slices_kernel,
        (pltpu.with_memory_space_constraint(cells, pltpu.HBM),),
        (whole((16, 8, width), BF16),) * 2 + (whole((8, 16, width), BF16),) * 2,
        scratch=(pltpu.SemaphoreType.DMA((4,)),),
        far=1,
        flops=1_000_000,
    )
    left = shift(to_right, 1).reshape(128, width)
    right = shift(to_left, -1).reshape(128, width)
    top = turn(to_next, 1).reshape(128, width)
    bottom = turn(to_last, -1).reshape(128, width)
    upper, lower = call(
        sides_kernel, (left, right), (whole((128, 512), BF16),) * 2, flops=1_000_000
    )
    above = turn(lower, 1)
    below = turn(upper, -1)

    core = lax.axis_index("core").astype(jnp.int32)[None]
    at_range = lax.axis_index("rng")
    edge = jnp.stack([at_range == 0, at_range == rng - 1]).astype(jnp.int32)

    (table,) = call(
        table_kernel,
        (
            edge,
            pltpu.with_memory_space_constraint(
                jnp.transpose(relative_bias, (1, 0, 2)), pltpu.HBM
            ),
        ),
        (whole((4, 768, 256), F32),),
        scratch=(pltpu.VMEM((17, 8, 17), F32), pltpu.SemaphoreType.DMA(())),
        prefetch=1,
        far=1,
        flops=100_000_000,
        limit=12,
    )
    q, q_t, da, da_t = call(
        queries_kernel,
        (own, cot, qkv_weight, out_weight),
        (
            whole((256, 512), BF16), whole((512, 256), BF16),
            whole((256, 512), BF16), whole((512, 256), BF16),
        ),
        flops=300_000_000,
        limit=12,
    )
    middle = call(
        middle_kernel, (left, own, right, qkv_weight), (whole((512, 512), BF16),) * 5, flops=1_000_000_000, limit=12
    )
    x_t, dkv, lhs, rhs, bsum, g_send = call(
        functools.partial(attention_kernel, rng),
        (core, top, above, bottom, below, q, q_t, da, da_t, table, *middle, qkv_weight, cot),
        (
            whole((512, 1024), BF16), whole((1024, 1024), BF16),
            whole((2, 512, 256), BF16), whole((2, 256, 512), BF16),
            whole((2, 8, 8, 512), F32), whole((512, 1024), BF16),
        ),
        scratch=(
            pltpu.VMEM((1024, 512), BF16), pltpu.VMEM((1024, 512), BF16),
            pltpu.VMEM((512, 1024), BF16), pltpu.VMEM((512, 1024), BF16),
            pltpu.VMEM((512, 256), BF16), pltpu.VMEM((768, 256), F32),
        ),
        prefetch=1,
        flops=10_000_000_000,
        limit=20,
    )
    came = swap(g_send)
    g_keep, g_bias, g_above, g_upper, g_lower, g_below = call(
        functools.partial(terms_kernel, rng),
        (core, x_t, dkv, lhs, rhs, bsum, qkv_weight),
        (
            whole((512, 1024), BF16), whole((8, 384), F32),
            whole((256, 512), BF16), whole((256, 512), F32),
            whole((256, 512), F32), whole((256, 512), BF16),
        ),
        prefetch=1,
        flops=2_500_000_000,
        limit=12,
    )
    (parcel,) = call(
        pack_kernel,
        (g_keep, came, g_bias),
        (whole((rng, 64 * az + 24, 128), BF16),),
        scratch=(
            pltpu.VMEM((rng, 64 * az + 24, 128), BF16), pltpu.SemaphoreType.DMA((rng,)),
        ),
        outside=True,
        flops=1_000_000,
    )
    parcel = lax.all_to_all(parcel, "rng", 0, 0, tiled=True)

    up = turn(g_below, 1)
    down = turn(g_above, -1)
    to_west, g_own, to_east = call(
        fold_kernel,
        (g_upper, g_lower, up, down),
        (whole((128, 512), BF16), whole((256, 512), F32), whole((128, 512), BF16)),
        flops=1_000_000,
    )
    east = shift(to_west.reshape(16, 8, width), -1)
    west = shift(to_east.reshape(16, 8, width), 1)
    (grad_tokens,) = call(
        after_kernel,
        (g_own.reshape(16, 16, width), west, east),
        (whole((16, 16, width), BF16),),
        flops=1_000_000,
    )

    (parcel,) = call(
        regroup_kernel,
        (parcel, g_own),
        (whole((az, 8, 1408), BF16),),
        flops=1_000_000,
        untouched=1,
    )
    parcel = lax.all_to_all(parcel, "az", 0, 0, tiled=True)
    (mine,) = call(total_kernel, (parcel,), (whole((8, 1408), F32),), flops=1_000_000)
    near = swap(mine, "half")
    (mine,) = call(add_kernel, (mine, near), (whole((8, 1408), F32),), flops=1_000_000)
    rows_qkv, rows_out, total_bias = call(
        finish_kernel,
        (core, mine, swap(mine)),
        (whole((8, 1536), F32), whole((8, 512), F32), whole((17, 8, 17), F32)),
        prefetch=1,
        flops=1_000_000,
    )
    total_bias = jnp.transpose(total_bias, (1, 0, 2))
    return (grad_tokens[None], rows_qkv, rows_out, total_bias)


def solution(mesh):
    az, rng, dp = mesh.devices.shape
    split = Mesh(mesh.devices.reshape(az, rng, dp // 2, 2), ("az", "rng", "half", "core"))
    cells = P(("half", "core"), "az", "rng", None)
    rows = P(("az", "rng"), None)
    return jax.shard_map(
        shards,
        mesh=split,
        in_specs=(cells, P(), P(), P(), cells),
        out_specs=(cells, rows, rows, P()),
        check_vma=False,
    )
```

```python
import functools

import jax
import jax.numpy as jnp
from jax import lax
from jax.experimental import pallas as pl
from jax.experimental.pallas import tpu as pltpu
from jax.sharding import Mesh, PartitionSpec as P


F32 = jnp.float32
BF16 = jnp.bfloat16
ABSENT = -1e30
NT = (((1,), (1,)), ((), ()))
TN = (((0,), (0,)), ((), ()))
MIB = 1024 * 1024


def dot(a, b, dims=(((1,), (0,)), ((), ())), exact=False):
    precision = lax.Precision.HIGHEST if exact else None
    return lax.dot_general(a, b, dims, precision=precision, preferred_element_type=F32)


def iota(shape, axis):
    return lax.broadcasted_iota(jnp.int32, shape, axis)


def row_slots(row):
    base = row // 8 * 256
    at = row % 8
    return (
        (0, 8, base + at * 8),
        (8, 24, base + 64 + at * 16),
        (24, 32, base + 192 + at * 8),
    )


def slices_kernel(own, bias, to_right, to_left, to_next, to_last, bias_near, done):
    copies = [
        pltpu.make_async_copy(source, target, done.at[n])
        for n, (source, target) in enumerate(
            (
                (bias, bias_near),
                (own.at[:, pl.ds(8, 8)], to_right),
                (own.at[:, pl.ds(0, 8)], to_left),
                (own.at[pl.ds(8, 8)], to_next),
                (own.at[pl.ds(0, 8)], to_last),
            )
        )
    ]
    for copy in copies:
        copy.start()
    for copy in copies:
        copy.wait()


def queries_kernel(x, cot, w, wo, q, q_t, da, da_t):
    queries = (dot(x[...], w[:, 0:512]).astype(BF16).astype(F32) * 0.125).astype(BF16)
    q[...] = queries
    q_t[...] = queries.T
    d_attended = dot(cot[...], wo[...], NT).astype(BF16)
    da[...] = d_attended
    da_t[...] = d_attended.T


def table_kernel(edge, bias, table):
    pick = (iota((17, 512), 0) == 23 - (iota((17, 512), 1) >> 4)).astype(F32)
    range_row = iota((32, 512), 0)
    lane = iota((32, 512), 1)
    gap = range_row - (lane & 15)
    first = jnp.where(edge[0] == 1, 8, 0)
    last = jnp.where(edge[1] == 1, 24, 32)
    present = (range_row >= first) & (range_row < last) & (lane >= 112) & (lane < 384)
    for head in range(8):
        pair, lanes = head // 2, slice(head % 2 * 128, head % 2 * 128 + 128)
        head_rows = dot(bias[:, head, :], pick, TN, exact=True)
        spread = jnp.full((32, 512), ABSENT, F32)
        for j in range(17):
            spread = jnp.where(gap == j, head_rows[j : j + 1], spread)
        spread = jnp.where(present, spread, ABSENT)
        for v in range(8):
            turned = spread if v == 0 else pltpu.roll(spread, 512 - 16 * v, 1)
            for u in range(3):
                block = turned[:, 128 * u : 128 * u + 128]
                for low, high, at in row_slots(23 - 8 * u - v):
                    table[pair, at : at + high - low, lanes] = block[low:high]


def project(block, w, k, v, k_t, v_t, x_t, at):
    rows = slice(at, at + 256)
    keys = dot(block, w[:, 512:1024]).astype(BF16)
    values = dot(block, w[:, 1024:1536]).astype(BF16)
    k[rows] = keys
    v[rows] = values
    k_t[:, rows] = keys.T
    v_t[:, rows] = values.T
    x_t[:, rows] = block.T


def sides_kernel(left, right, upper, lower):
    for half, ref in enumerate((upper, lower)):
        ref[0:64] = left[half * 64 : half * 64 + 64]
        ref[64:128] = right[half * 64 : half * 64 + 64]


def middle_kernel(left, own, right, w, k, v, k_t, v_t, x_t):
    for half in range(2):
        side = slice(half * 64, half * 64 + 64)
        mine = slice(half * 128, half * 128 + 128)
        block = jnp.concatenate([left[side], own[mine], right[side]], axis=0)
        project(block, w, k, v, k_t, v_t, x_t, half * 256)


def by_range(block, rng):
    rows, cols = block.shape
    turned = jnp.transpose(block.reshape(rows // (rng * 8), rng, 8, cols), (1, 0, 2, 3))
    return turned.reshape(rows, cols)


def weight_terms(ref, who, rng, x_t, dkv, lhs, rhs):
    ref[:, 0:512] = by_range(dot(lhs[who], rhs[who]), rng).astype(BF16)
    for n in range(2):
        lanes = pl.ds(pl.multiple_of(who * 512 + n * 256, 256), 256)
        ref[:, 512 + n * 256 : 768 + n * 256] = by_range(dot(x_t[...], dkv[:, lanes]), rng).astype(
            BF16
        )


def attention_kernel(
    rng, core, top, above, bottom, below, q, q_t, da, da_t, table,
    k_mid, v_mid, kt_mid, vt_mid, xt_mid, w, cot,
    x_t, dkv, lhs, rhs, bsum, g_send,
    k, v, k_t, v_t, dq_t, dsum,
):
    for at, own, sides in ((0, top, above), (768, bottom, below)):
        block = jnp.concatenate([sides[0:64], own[...], sides[64:128]], axis=0)
        project(block, w, k, v, k_t, v_t, x_t, at)
    k[256:768] = k_mid[...]
    v[256:768] = v_mid[...]
    k_t[:, 256:768] = kt_mid[...]
    v_t[:, 256:768] = vt_mid[...]
    x_t[:, 256:768] = xt_mid[...]
    lhs[0, :, 0:128] = xt_mid[:, 64:192]
    lhs[0, :, 128:256] = xt_mid[:, 320:448]
    rhs[1] = cot[...]

    upper_rows = iota((128, 128), 0) < 64
    upper_lanes = iota((128, 128), 1) < 64
    corner = iota((16, 512), 0) == (iota((16, 512), 1) & 15)

    def split_lanes(block):
        zero = jnp.zeros_like(block)
        return jnp.concatenate(
            [jnp.where(upper_rows, block, zero), jnp.where(upper_rows, zero, block)], axis=1
        )

    def tall(ref, rows, cols, block):
        return dot(ref[rows, cols], block)

    def split_rows(block):
        zero = jnp.zeros_like(block)
        return jnp.concatenate(
            [jnp.where(upper_lanes, block, zero), jnp.where(upper_lanes, zero, block)], axis=0
        )

    def pair_step(pair, carry):
        at = pl.multiple_of(pair * 128, 128)
        cols = pl.ds(at, 128)
        keys = [slice(t * 256, t * 256 + 768) for t in range(2)]
        mine = [slice(t * 128, t * 128 + 128) for t in range(2)]
        da_block = [da_t[cols, mine[t]] for t in range(2)]
        score = [
            tall(k, keys[t], cols, split_lanes(q_t[cols, mine[t]])) + table[pair] for t in range(2)
        ]
        d_prob = [tall(v, keys[t], cols, split_lanes(da_block[t])) for t in range(2)]
        prob, delta, d_value, d_key = [], [], [], []
        for t in range(2):
            top_score = jnp.max(score[t], axis=0, keepdims=True)
            weight = jnp.exp(score[t] - top_score)
            prob.append(weight * (1.0 / jnp.sum(weight, axis=0, keepdims=True)))
        prob_low = [each.astype(BF16) for each in prob]
        for t in range(2):
            mixed = dot(v_t[cols, keys[t]], prob_low[t])
            att = jnp.where(upper_rows, mixed[:, :128], mixed[:, 128:]).astype(BF16)
            lhs[1, cols, mine[t]] = att
            product = att.astype(F32) * da_block[t].astype(F32)
            delta.append(
                jnp.concatenate(
                    [
                        jnp.sum(product[:64], axis=0, keepdims=True),
                        jnp.sum(product[64:], axis=0, keepdims=True),
                    ],
                    axis=1,
                )
            )
            d_value.append(dot(prob_low[t], split_rows(da[mine[t], cols])))
        d_score = [prob[t] * (d_prob[t] - delta[t]) for t in range(2)]
        dsum[...] = d_score[0] + d_score[1]
        for t in range(2):
            score_low = d_score[t].astype(BF16)
            d_q = dot(k_t[cols, keys[t]], score_low)
            dq_t[cols, mine[t]] = (
                jnp.where(upper_rows, d_q[:, :128], d_q[:, 128:]) * 0.125
            ).astype(BF16)
            d_key.append(dot(score_low, split_rows(q[mine[t], cols])))
        tails = ((d_key[0], d_value[0]), (d_key[1], d_value[1]))
        for which in range(2):
            early, late = tails[0][which], tails[1][which]
            to = pl.ds(pl.multiple_of(which * 512 + at, 128), 128)
            dkv[0:256, to] = early[0:256].astype(BF16)
            dkv[256:768, to] = (early[256:768] + late[0:512]).astype(BF16)
            dkv[768:1024, to] = late[512:768].astype(BF16)
        for side in range(2):
            lanes = slice(side * 128, side * 128 + 128)
            total = None
            for turn in range(8):
                parts = [
                    jnp.concatenate(
                        [
                            dsum[to : to + high - low, lanes]
                            for low, high, to in row_slots(23 - 8 * u - turn)
                        ],
                        axis=0,
                    )
                    for u in range(3)
                ]
                strip = jnp.concatenate(parts + [jnp.zeros((32, 128), F32)], axis=1)
                if turn:
                    strip = pltpu.roll(strip, 16 * turn, 1)
                total = strip if total is None else total + strip
            tail = total[16:32]
            last = jnp.where(corner, tail, 0.0)
            rest = jnp.where(corner, 0.0, tail)
            bsum[0, pair * 2 + side] = (
                total[0:8]
                + pltpu.roll(total[8:16], 504, 1)
                + pltpu.roll(rest[0:8], 496, 1)
                + pltpu.roll(rest[8:16], 488, 1)
            )
            bsum[1, pair * 2 + side] = pltpu.roll(last[0:8], 496, 1) + pltpu.roll(
                last[8:16], 488, 1
            )
        return carry

    lax.fori_loop(0, 4, pair_step, 0, unroll=True)

    rhs[0] = dq_t[...].T
    weight_terms(g_send, 1 - core[0], rng, x_t, dkv, lhs, rhs)


def terms_kernel(
    rng, core, x_t, dkv, lhs, rhs, bsum, w, g_keep, g_bias, g_above, g_upper, g_lower, g_below
):
    weight_terms(g_keep, core[0], rng, x_t, dkv, lhs, rhs)

    spot = iota((512, 384), 0)
    place = iota((512, 384), 1)
    i = (place * 241) >> 12
    j = place - i * 17
    inside = place < 289
    flat = None
    for which in range(2):
        lanes = None
        for b in range(8):
            row = bsum[which, :, b, :]
            row = pltpu.roll(row, 512 - b, 1) if b else row
            lanes = row if lanes is None else lanes + row
        from_lane = 368 - 16 * i - j
        choose = inside & (spot == from_lane) & ((j < 16) if which == 0 else (j == 16))
        part = dot(lanes.astype(BF16), choose.astype(F32).astype(BF16))
        flat = part if flat is None else flat + part
    g_bias[...] = flat

    for g, ref in enumerate((g_above, g_upper, g_lower, g_below)):
        block = dot(dkv[g * 256 : g * 256 + 256], w[:, 512:1536], NT)
        if g in (0, 3):
            ref[...] = block.astype(BF16)
        else:
            half = (g - 1) * 128
            ref[0:64] = block[0:64]
            ref[64:192] = block[64:192] + dot(rhs[0, half : half + 128], w[:, 0:512], NT)
            ref[192:256] = block[192:256]


def fold_kernel(g_upper, g_lower, up, down, west, own, east):
    for half, (ref, term) in enumerate(((g_upper, up), (g_lower, down))):
        total = ref[...] + term[...].astype(F32)
        west[half * 64 : half * 64 + 64] = total[0:64].astype(BF16)
        own[half * 128 : half * 128 + 128] = total[64:192]
        east[half * 64 : half * 64 + 64] = total[192:256].astype(BF16)


def after_kernel(own, west, east, out):
    out[:, 0:8] = (own[:, 0:8] + west[...].astype(F32)).astype(BF16)
    out[:, 8:16] = (own[:, 8:16] + east[...].astype(F32)).astype(BF16)


def pack_kernel(keep, came, bias, parcel, block, done):
    count = parcel.shape[0]
    rows = keep.shape[0] // count
    low = bias[...].astype(BF16)
    copies = []
    for r in range(count):
        at = slice(r * rows, r * rows + rows)
        both = (keep[at].astype(F32) + came[at].astype(F32)).astype(BF16)
        for n in range(8):
            block[r, n * rows : n * rows + rows] = both[:, n * 128 : n * 128 + 128]
        for n in range(3):
            to = 8 * rows + n * 8
            block[r, to : to + 8] = low[:, n * 128 : n * 128 + 128]
        copies.append(pltpu.make_async_copy(block.at[r], parcel.at[r], done.at[r]))
        copies[-1].start()
    for copy in copies:
        copy.wait()


def regroup_kernel(came, _, parcel):
    total = came[0].astype(F32)
    for n in range(1, came.shape[0]):
        total += came[n].astype(F32)
    count = parcel.shape[0]
    for a in range(count):
        for n in range(8):
            at = (n * count + a) * 8
            parcel[a, :, n * 128 : n * 128 + 128] = total[at : at + 8].astype(BF16)
        for n in range(3):
            at = count * 64 + n * 8
            parcel[a, :, 1024 + n * 128 : 1152 + n * 128] = total[at : at + 8].astype(BF16)


def total_kernel(came, mine):
    total = came[0].astype(F32)
    for a in range(1, came.shape[0]):
        total += came[a].astype(F32)
    mine[...] = total


def add_kernel(mine, came, both):
    both[...] = mine[...] + came[...]


def finish_kernel(core, here, there, qkv, out, bias):
    is_first = core[0] == 0
    low = jnp.where(is_first, here[:, 0:1024], there[:, 0:1024])
    high = jnp.where(is_first, there[:, 0:1024], here[:, 0:1024])
    qkv[:, 0:1024] = low
    qkv[:, 1024:1536] = high[:, 512:1024]
    out[...] = high[:, 0:512]
    total = here[:, 1024:] + there[:, 1024:]
    for i in range(17):
        bias[i] = total[:, i * 17 : i * 17 + 17]


def whole(shape, dtype):
    return jax.ShapeDtypeStruct(shape, dtype)


def call(kernel, operands, outs, scratch=(), prefetch=0, flops=0, limit=16, untouched=0, far=0, outside=False):
    spec = pl.BlockSpec(memory_space=pltpu.VMEM)
    scalar = pl.BlockSpec(memory_space=pltpu.SMEM)
    size = sum(leaf.size * leaf.dtype.itemsize for leaf in tuple(operands) + tuple(outs))
    return pl.pallas_call(
        kernel,
        out_shape=tuple(outs),
        in_specs=[scalar] * prefetch
        + [spec] * (len(operands) - prefetch - untouched - far)
        + [pl.BlockSpec(memory_space=pl.ANY)] * untouched
        + [pl.BlockSpec(memory_space=pltpu.HBM)] * far,
        out_specs=tuple([pl.BlockSpec(memory_space=pl.ANY) if outside else spec] * len(outs)),
        scratch_shapes=list(scratch),
        compiler_params=pltpu.CompilerParams(vmem_limit_bytes=limit * MIB),
        cost_estimate=pl.CostEstimate(flops=flops, bytes_accessed=size, transcendentals=0),
    )(*operands)


def shards(tokens, qkv_weight, out_weight, relative_bias, cotangent):
    az, rng = lax.axis_size("az"), lax.axis_size("rng")
    width = tokens.shape[3]
    cells = tokens[0]
    own = cells.reshape(256, width)
    cot = cotangent.reshape(256, width)

    def turn(leaf, step):
        return lax.ppermute(leaf, "az", [(i, (i + step) % az) for i in range(az)])

    def shift(leaf, step):
        pairs = [(i, i + step) for i in range(rng) if 0 <= i + step < rng]
        return lax.ppermute(leaf, "rng", pairs)

    def swap(leaf, axis="core"):
        return lax.ppermute(leaf, axis, [(0, 1), (1, 0)])

    bias = jnp.transpose(relative_bias, (1, 0, 2))
    to_right, to_left, to_next, to_last, bias = call(
        slices_kernel,
        (
            pltpu.with_memory_space_constraint(cells, pltpu.HBM),
            pltpu.with_memory_space_constraint(bias, pltpu.HBM),
        ),
        (whole((16, 8, width), BF16),) * 2
        + (whole((8, 16, width), BF16),) * 2
        + (whole(bias.shape, F32),),
        scratch=(pltpu.SemaphoreType.DMA((5,)),),
        far=2,
        flops=1_000_000,
    )
    left = shift(to_right, 1).reshape(128, width)
    right = shift(to_left, -1).reshape(128, width)
    top = turn(to_next, 1).reshape(128, width)
    bottom = turn(to_last, -1).reshape(128, width)
    upper, lower = call(
        sides_kernel, (left, right), (whole((128, 512), BF16),) * 2, flops=1_000_000
    )
    above = turn(lower, 1)
    below = turn(upper, -1)

    core = lax.axis_index("core").astype(jnp.int32)[None]
    at_range = lax.axis_index("rng")
    edge = jnp.stack([at_range == 0, at_range == rng - 1]).astype(jnp.int32)

    (table,) = call(
        table_kernel,
        (edge, bias),
        (whole((4, 768, 256), F32),),
        prefetch=1,
        flops=100_000_000,
        limit=12,
    )
    q, q_t, da, da_t = call(
        queries_kernel,
        (own, cot, qkv_weight, out_weight),
        (
            whole((256, 512), BF16), whole((512, 256), BF16),
            whole((256, 512), BF16), whole((512, 256), BF16),
        ),
        flops=300_000_000,
        limit=12,
    )
    middle = call(
        middle_kernel, (left, own, right, qkv_weight), (whole((512, 512), BF16),) * 5, flops=1_000_000_000, limit=12
    )
    x_t, dkv, lhs, rhs, bsum, g_send = call(
        functools.partial(attention_kernel, rng),
        (core, top, above, bottom, below, q, q_t, da, da_t, table, *middle, qkv_weight, cot),
        (
            whole((512, 1024), BF16), whole((1024, 1024), BF16),
            whole((2, 512, 256), BF16), whole((2, 256, 512), BF16),
            whole((2, 8, 8, 512), F32), whole((512, 1024), BF16),
        ),
        scratch=(
            pltpu.VMEM((1024, 512), BF16), pltpu.VMEM((1024, 512), BF16),
            pltpu.VMEM((512, 1024), BF16), pltpu.VMEM((512, 1024), BF16),
            pltpu.VMEM((512, 256), BF16), pltpu.VMEM((768, 256), F32),
        ),
        prefetch=1,
        flops=10_000_000_000,
        limit=20,
    )
    came = swap(g_send)
    g_keep, g_bias, g_above, g_upper, g_lower, g_below = call(
        functools.partial(terms_kernel, rng),
        (core, x_t, dkv, lhs, rhs, bsum, qkv_weight),
        (
            whole((512, 1024), BF16), whole((8, 384), F32),
            whole((256, 512), BF16), whole((256, 512), F32),
            whole((256, 512), F32), whole((256, 512), BF16),
        ),
        prefetch=1,
        flops=2_500_000_000,
        limit=12,
    )
    (parcel,) = call(
        pack_kernel,
        (g_keep, came, g_bias),
        (whole((rng, 64 * az + 24, 128), BF16),),
        scratch=(
            pltpu.VMEM((rng, 64 * az + 24, 128), BF16), pltpu.SemaphoreType.DMA((rng,)),
        ),
        outside=True,
        flops=1_000_000,
    )
    parcel = lax.all_to_all(parcel, "rng", 0, 0, tiled=True)

    up = turn(g_below, 1)
    down = turn(g_above, -1)
    to_west, g_own, to_east = call(
        fold_kernel,
        (g_upper, g_lower, up, down),
        (whole((128, 512), BF16), whole((256, 512), F32), whole((128, 512), BF16)),
        flops=1_000_000,
    )
    east = shift(to_west.reshape(16, 8, width), -1)
    west = shift(to_east.reshape(16, 8, width), 1)
    (grad_tokens,) = call(
        after_kernel,
        (g_own.reshape(16, 16, width), west, east),
        (whole((16, 16, width), BF16),),
        flops=1_000_000,
    )

    (parcel,) = call(
        regroup_kernel,
        (parcel, g_own),
        (whole((az, 8, 1408), BF16),),
        flops=1_000_000,
        untouched=1,
    )
    parcel = lax.all_to_all(parcel, "az", 0, 0, tiled=True)
    (mine,) = call(total_kernel, (parcel,), (whole((8, 1408), F32),), flops=1_000_000)
    near = swap(mine, "half")
    (mine,) = call(add_kernel, (mine, near), (whole((8, 1408), F32),), flops=1_000_000)
    rows_qkv, rows_out, total_bias = call(
        finish_kernel,
        (core, mine, swap(mine)),
        (whole((8, 1536), F32), whole((8, 512), F32), whole((17, 8, 17), F32)),
        prefetch=1,
        flops=1_000_000,
    )
    total_bias = jnp.transpose(total_bias, (1, 0, 2))
    return (grad_tokens[None], rows_qkv, rows_out, total_bias)


def solution(mesh):
    az, rng, dp = mesh.devices.shape
    split = Mesh(mesh.devices.reshape(az, rng, dp // 2, 2), ("az", "rng", "half", "core"))
    cells = P(("half", "core"), "az", "rng", None)
    rows = P(("az", "rng"), None)
    return jax.shard_map(
        shards,
        mesh=split,
        in_specs=(cells, P(), P(), P(), cells),
        out_specs=(cells, rows, rows, P()),
        check_vma=False,
    )
```

```python
import functools

import jax
import jax.numpy as jnp
from jax import lax
from jax.experimental import pallas as pl
from jax.experimental.pallas import tpu as pltpu
from jax.sharding import Mesh, PartitionSpec as P


F32 = jnp.float32
BF16 = jnp.bfloat16
ABSENT = -1e30
NT = (((1,), (1,)), ((), ()))
TN = (((0,), (0,)), ((), ()))
MIB = 1024 * 1024


def dot(a, b, dims=(((1,), (0,)), ((), ())), exact=False):
    precision = lax.Precision.HIGHEST if exact else None
    return lax.dot_general(a, b, dims, precision=precision, preferred_element_type=F32)


def iota(shape, axis):
    return lax.broadcasted_iota(jnp.int32, shape, axis)


def row_slots(row):
    base = row // 8 * 256
    at = row % 8
    return (
        (0, 8, base + at * 8),
        (8, 24, base + 64 + at * 16),
        (24, 32, base + 192 + at * 8),
    )


def slices_kernel(own, bias, to_right, to_left, to_next, to_last, bias_near, done):
    copies = [
        pltpu.make_async_copy(source, target, done.at[n])
        for n, (source, target) in enumerate(
            (
                (bias, bias_near),
                (own.at[:, pl.ds(8, 8)], to_right),
                (own.at[:, pl.ds(0, 8)], to_left),
                (own.at[pl.ds(8, 8)], to_next),
                (own.at[pl.ds(0, 8)], to_last),
            )
        )
    ]
    for copy in copies:
        copy.start()
    for copy in copies:
        copy.wait()


def queries_kernel(x, cot, w, wo, q, q_t, da, da_t):
    queries = (dot(x[...], w[:, 0:512]).astype(BF16).astype(F32) * 0.125).astype(BF16)
    q[...] = queries
    q_t[...] = queries.T
    d_attended = dot(cot[...], wo[...], NT).astype(BF16)
    da[...] = d_attended
    da_t[...] = d_attended.T


def table_kernel(edge, bias, table):
    pick = (iota((17, 512), 0) == 23 - (iota((17, 512), 1) >> 4)).astype(F32)
    range_row = iota((32, 512), 0)
    lane = iota((32, 512), 1)
    gap = range_row - (lane & 15)
    first = jnp.where(edge[0] == 1, 8, 0)
    last = jnp.where(edge[1] == 1, 24, 32)
    present = (range_row >= first) & (range_row < last) & (lane >= 112) & (lane < 384)
    for head in range(8):
        pair, lanes = head // 2, slice(head % 2 * 128, head % 2 * 128 + 128)
        head_rows = dot(bias[:, head, :], pick, TN, exact=True)
        spread = jnp.full((32, 512), ABSENT, F32)
        for j in range(17):
            spread = jnp.where(gap == j, head_rows[j : j + 1], spread)
        spread = jnp.where(present, spread, ABSENT)
        for v in range(8):
            turned = spread if v == 0 else pltpu.roll(spread, 512 - 16 * v, 1)
            for u in range(3):
                block = turned[:, 128 * u : 128 * u + 128]
                for low, high, at in row_slots(23 - 8 * u - v):
                    table[pair, at : at + high - low, lanes] = block[low:high]


def project(block, w, k, v, k_t, v_t, x_t, at):
    rows = slice(at, at + 256)
    keys = dot(block, w[:, 512:1024]).astype(BF16)
    values = dot(block, w[:, 1024:1536]).astype(BF16)
    k[rows] = keys
    v[rows] = values
    k_t[:, rows] = keys.T
    v_t[:, rows] = values.T
    x_t[:, rows] = block.T


def sides_kernel(left, right, upper, lower):
    for half, ref in enumerate((upper, lower)):
        ref[0:64] = left[half * 64 : half * 64 + 64]
        ref[64:128] = right[half * 64 : half * 64 + 64]


def middle_kernel(left, own, right, w, k, v, k_t, v_t, x_t):
    for half in range(2):
        side = slice(half * 64, half * 64 + 64)
        mine = slice(half * 128, half * 128 + 128)
        block = jnp.concatenate([left[side], own[mine], right[side]], axis=0)
        project(block, w, k, v, k_t, v_t, x_t, half * 256)


def by_range(block, rng):
    rows, cols = block.shape
    turned = jnp.transpose(block.reshape(rows // (rng * 8), rng, 8, cols), (1, 0, 2, 3))
    return turned.reshape(rows, cols)


def weight_terms(ref, who, rng, x_t, dkv, lhs, rhs):
    ref[:, 0:512] = by_range(dot(lhs[who], rhs[who]), rng).astype(BF16)
    for n in range(2):
        lanes = pl.ds(pl.multiple_of(who * 512 + n * 256, 256), 256)
        ref[:, 512 + n * 256 : 768 + n * 256] = by_range(dot(x_t[...], dkv[:, lanes]), rng).astype(
            BF16
        )


def attention_kernel(
    rng, core, top, above, bottom, below, q, q_t, da, da_t, table,
    k_mid, v_mid, kt_mid, vt_mid, xt_mid, w, cot,
    x_t, dkv, lhs, rhs, bsum, g_send,
    k, v, k_t, v_t, dq_t, dsum,
):
    for at, own, sides in ((0, top, above), (768, bottom, below)):
        block = jnp.concatenate([sides[0:64], own[...], sides[64:128]], axis=0)
        project(block, w, k, v, k_t, v_t, x_t, at)
    k[256:768] = k_mid[...]
    v[256:768] = v_mid[...]
    k_t[:, 256:768] = kt_mid[...]
    v_t[:, 256:768] = vt_mid[...]
    x_t[:, 256:768] = xt_mid[...]
    lhs[0, :, 0:128] = xt_mid[:, 64:192]
    lhs[0, :, 128:256] = xt_mid[:, 320:448]
    rhs[1] = cot[...]

    upper_rows = iota((128, 128), 0) < 64
    upper_lanes = iota((128, 128), 1) < 64
    corner = iota((16, 512), 0) == (iota((16, 512), 1) & 15)

    def split_lanes(block):
        zero = jnp.zeros_like(block)
        return jnp.concatenate(
            [jnp.where(upper_rows, block, zero), jnp.where(upper_rows, zero, block)], axis=1
        )

    def tall(ref, rows, cols, block):
        return dot(ref[rows, cols], block)

    def split_rows(block):
        zero = jnp.zeros_like(block)
        return jnp.concatenate(
            [jnp.where(upper_lanes, block, zero), jnp.where(upper_lanes, zero, block)], axis=0
        )

    def pair_step(pair, carry):
        at = pl.multiple_of(pair * 128, 128)
        cols = pl.ds(at, 128)
        keys = [slice(t * 256, t * 256 + 768) for t in range(2)]
        mine = [slice(t * 128, t * 128 + 128) for t in range(2)]
        da_block = [da_t[cols, mine[t]] for t in range(2)]
        score = [
            tall(k, keys[t], cols, split_lanes(q_t[cols, mine[t]])) + table[pair] for t in range(2)
        ]
        d_prob = [tall(v, keys[t], cols, split_lanes(da_block[t])) for t in range(2)]
        prob, delta, d_value, d_key = [], [], [], []
        for t in range(2):
            top_score = jnp.max(score[t], axis=0, keepdims=True)
            weight = jnp.exp(score[t] - top_score)
            prob.append(weight * (1.0 / jnp.sum(weight, axis=0, keepdims=True)))
        prob_low = [each.astype(BF16) for each in prob]
        for t in range(2):
            mixed = dot(v_t[cols, keys[t]], prob_low[t])
            att = jnp.where(upper_rows, mixed[:, :128], mixed[:, 128:]).astype(BF16)
            lhs[1, cols, mine[t]] = att
            product = att.astype(F32) * da_block[t].astype(F32)
            delta.append(
                jnp.concatenate(
                    [
                        jnp.sum(product[:64], axis=0, keepdims=True),
                        jnp.sum(product[64:], axis=0, keepdims=True),
                    ],
                    axis=1,
                )
            )
            d_value.append(dot(prob_low[t], split_rows(da[mine[t], cols])))
        d_score = [prob[t] * (d_prob[t] - delta[t]) for t in range(2)]
        dsum[...] = d_score[0] + d_score[1]
        for t in range(2):
            score_low = d_score[t].astype(BF16)
            d_q = dot(k_t[cols, keys[t]], score_low)
            dq_t[cols, mine[t]] = (
                jnp.where(upper_rows, d_q[:, :128], d_q[:, 128:]) * 0.125
            ).astype(BF16)
            d_key.append(dot(score_low, split_rows(q[mine[t], cols])))
        tails = ((d_key[0], d_value[0]), (d_key[1], d_value[1]))
        for which in range(2):
            early, late = tails[0][which], tails[1][which]
            to = pl.ds(pl.multiple_of(which * 512 + at, 128), 128)
            dkv[0:256, to] = early[0:256].astype(BF16)
            dkv[256:768, to] = (early[256:768] + late[0:512]).astype(BF16)
            dkv[768:1024, to] = late[512:768].astype(BF16)
        for side in range(2):
            lanes = slice(side * 128, side * 128 + 128)
            total = None
            for turn in range(8):
                parts = [
                    jnp.concatenate(
                        [
                            dsum[to : to + high - low, lanes]
                            for low, high, to in row_slots(23 - 8 * u - turn)
                        ],
                        axis=0,
                    )
                    for u in range(3)
                ]
                strip = jnp.concatenate(parts + [jnp.zeros((32, 128), F32)], axis=1)
                if turn:
                    strip = pltpu.roll(strip, 16 * turn, 1)
                total = strip if total is None else total + strip
            tail = total[16:32]
            last = jnp.where(corner, tail, 0.0)
            rest = jnp.where(corner, 0.0, tail)
            bsum[0, pair * 2 + side] = (
                total[0:8]
                + pltpu.roll(total[8:16], 504, 1)
                + pltpu.roll(rest[0:8], 496, 1)
                + pltpu.roll(rest[8:16], 488, 1)
            )
            bsum[1, pair * 2 + side] = pltpu.roll(last[0:8], 496, 1) + pltpu.roll(
                last[8:16], 488, 1
            )
        return carry

    lax.fori_loop(0, 4, pair_step, 0, unroll=True)

    rhs[0] = dq_t[...].T
    weight_terms(g_send, 1 - core[0], rng, x_t, dkv, lhs, rhs)


def terms_kernel(
    rng, core, x_t, dkv, lhs, rhs, bsum, w, g_keep, g_bias, g_above, g_upper, g_lower, g_below
):
    weight_terms(g_keep, core[0], rng, x_t, dkv, lhs, rhs)

    spot = iota((512, 384), 0)
    place = iota((512, 384), 1)
    i = (place * 241) >> 12
    j = place - i * 17
    inside = place < 289
    flat = None
    for which in range(2):
        lanes = None
        for b in range(8):
            row = bsum[which, :, b, :]
            row = pltpu.roll(row, 512 - b, 1) if b else row
            lanes = row if lanes is None else lanes + row
        from_lane = 368 - 16 * i - j
        choose = inside & (spot == from_lane) & ((j < 16) if which == 0 else (j == 16))
        part = dot(lanes.astype(BF16), choose.astype(F32).astype(BF16))
        flat = part if flat is None else flat + part
    g_bias[...] = flat

    for g, ref in enumerate((g_above, g_upper, g_lower, g_below)):
        block = dot(dkv[g * 256 : g * 256 + 256], w[:, 512:1536], NT)
        if g in (0, 3):
            ref[...] = block.astype(BF16)
        else:
            half = (g - 1) * 128
            ref[0:64] = block[0:64]
            ref[64:192] = block[64:192] + dot(rhs[0, half : half + 128], w[:, 0:512], NT)
            ref[192:256] = block[192:256]


def fold_kernel(g_upper, g_lower, up, down, west, own, east):
    for half, (ref, term) in enumerate(((g_upper, up), (g_lower, down))):
        total = ref[...] + term[...].astype(F32)
        west[half * 64 : half * 64 + 64] = total[0:64].astype(BF16)
        own[half * 128 : half * 128 + 128] = total[64:192]
        east[half * 64 : half * 64 + 64] = total[192:256].astype(BF16)


def after_kernel(own, west, east, out):
    out[:, 0:8] = (own[:, 0:8] + west[...].astype(F32)).astype(BF16)
    out[:, 8:16] = (own[:, 8:16] + east[...].astype(F32)).astype(BF16)


def pack_kernel(keep, came, bias, parcel, block, done):
    count = parcel.shape[0]
    rows = keep.shape[0] // count
    low = bias[...].astype(BF16)
    copies = []
    for r in range(count):
        at = slice(r * rows, r * rows + rows)
        both = (keep[at].astype(F32) + came[at].astype(F32)).astype(BF16)
        for n in range(8):
            block[r, n * rows : n * rows + rows] = both[:, n * 128 : n * 128 + 128]
        for n in range(3):
            to = 8 * rows + n * 8
            block[r, to : to + 8] = low[:, n * 128 : n * 128 + 128]
        copies.append(pltpu.make_async_copy(block.at[r], parcel.at[r], done.at[r]))
        copies[-1].start()
    for copy in copies:
        copy.wait()


def regroup_kernel(came, _, parcel):
    total = came[0].astype(F32)
    for n in range(1, came.shape[0]):
        total += came[n].astype(F32)
    count = parcel.shape[0]
    for a in range(count):
        for n in range(8):
            at = (n * count + a) * 8
            parcel[a, :, n * 128 : n * 128 + 128] = total[at : at + 8].astype(BF16)
        for n in range(3):
            at = count * 64 + n * 8
            parcel[a, :, 1024 + n * 128 : 1152 + n * 128] = total[at : at + 8].astype(BF16)


def total_kernel(came, mine):
    total = came[0].astype(F32)
    for a in range(1, came.shape[0]):
        total += came[a].astype(F32)
    mine[...] = total


def finish_kernel(parts, qkv, out, bias):
    first = parts[0] + parts[2]
    second = parts[1] + parts[3]
    low, high = first[:, 0:1024], second[:, 0:1024]
    qkv[:, 0:1024] = low
    qkv[:, 1024:1536] = high[:, 512:1024]
    out[...] = high[:, 0:512]
    total = first[:, 1024:] + second[:, 1024:]
    for i in range(17):
        bias[i] = total[:, i * 17 : i * 17 + 17]


def whole(shape, dtype):
    return jax.ShapeDtypeStruct(shape, dtype)


def call(kernel, operands, outs, scratch=(), prefetch=0, flops=0, limit=16, untouched=0, far=0, outside=False):
    spec = pl.BlockSpec(memory_space=pltpu.VMEM)
    scalar = pl.BlockSpec(memory_space=pltpu.SMEM)
    size = sum(leaf.size * leaf.dtype.itemsize for leaf in tuple(operands) + tuple(outs))
    return pl.pallas_call(
        kernel,
        out_shape=tuple(outs),
        in_specs=[scalar] * prefetch
        + [spec] * (len(operands) - prefetch - untouched - far)
        + [pl.BlockSpec(memory_space=pl.ANY)] * untouched
        + [pl.BlockSpec(memory_space=pltpu.HBM)] * far,
        out_specs=tuple([pl.BlockSpec(memory_space=pl.ANY) if outside else spec] * len(outs)),
        scratch_shapes=list(scratch),
        compiler_params=pltpu.CompilerParams(vmem_limit_bytes=limit * MIB),
        cost_estimate=pl.CostEstimate(flops=flops, bytes_accessed=size, transcendentals=0),
    )(*operands)


def shards(tokens, qkv_weight, out_weight, relative_bias, cotangent):
    az, rng = lax.axis_size("az"), lax.axis_size("rng")
    width = tokens.shape[3]
    cells = tokens[0]
    own = cells.reshape(256, width)
    cot = cotangent.reshape(256, width)

    def turn(leaf, step):
        return lax.ppermute(leaf, "az", [(i, (i + step) % az) for i in range(az)])

    def shift(leaf, step):
        pairs = [(i, i + step) for i in range(rng) if 0 <= i + step < rng]
        return lax.ppermute(leaf, "rng", pairs)

    def swap(leaf, axis="core"):
        return lax.ppermute(leaf, axis, [(0, 1), (1, 0)])

    bias = jnp.transpose(relative_bias, (1, 0, 2))
    to_right, to_left, to_next, to_last, bias = call(
        slices_kernel,
        (
            pltpu.with_memory_space_constraint(cells, pltpu.HBM),
            pltpu.with_memory_space_constraint(bias, pltpu.HBM),
        ),
        (whole((16, 8, width), BF16),) * 2
        + (whole((8, 16, width), BF16),) * 2
        + (whole(bias.shape, F32),),
        scratch=(pltpu.SemaphoreType.DMA((5,)),),
        far=2,
        flops=1_000_000,
    )
    left = shift(to_right, 1).reshape(128, width)
    right = shift(to_left, -1).reshape(128, width)
    top = turn(to_next, 1).reshape(128, width)
    bottom = turn(to_last, -1).reshape(128, width)
    upper, lower = call(
        sides_kernel, (left, right), (whole((128, 512), BF16),) * 2, flops=1_000_000
    )
    above = turn(lower, 1)
    below = turn(upper, -1)

    core = lax.axis_index("core").astype(jnp.int32)[None]
    at_range = lax.axis_index("rng")
    edge = jnp.stack([at_range == 0, at_range == rng - 1]).astype(jnp.int32)

    (table,) = call(
        table_kernel,
        (edge, bias),
        (whole((4, 768, 256), F32),),
        prefetch=1,
        flops=100_000_000,
        limit=12,
    )
    q, q_t, da, da_t = call(
        queries_kernel,
        (own, cot, qkv_weight, out_weight),
        (
            whole((256, 512), BF16), whole((512, 256), BF16),
            whole((256, 512), BF16), whole((512, 256), BF16),
        ),
        flops=300_000_000,
        limit=12,
    )
    middle = call(
        middle_kernel, (left, own, right, qkv_weight), (whole((512, 512), BF16),) * 5, flops=1_000_000_000, limit=12
    )
    x_t, dkv, lhs, rhs, bsum, g_send = call(
        functools.partial(attention_kernel, rng),
        (core, top, above, bottom, below, q, q_t, da, da_t, table, *middle, qkv_weight, cot),
        (
            whole((512, 1024), BF16), whole((1024, 1024), BF16),
            whole((2, 512, 256), BF16), whole((2, 256, 512), BF16),
            whole((2, 8, 8, 512), F32), whole((512, 1024), BF16),
        ),
        scratch=(
            pltpu.VMEM((1024, 512), BF16), pltpu.VMEM((1024, 512), BF16),
            pltpu.VMEM((512, 1024), BF16), pltpu.VMEM((512, 1024), BF16),
            pltpu.VMEM((512, 256), BF16), pltpu.VMEM((768, 256), F32),
        ),
        prefetch=1,
        flops=10_000_000_000,
        limit=20,
    )
    came = swap(g_send)
    g_keep, g_bias, g_above, g_upper, g_lower, g_below = call(
        functools.partial(terms_kernel, rng),
        (core, x_t, dkv, lhs, rhs, bsum, qkv_weight),
        (
            whole((512, 1024), BF16), whole((8, 384), F32),
            whole((256, 512), BF16), whole((256, 512), F32),
            whole((256, 512), F32), whole((256, 512), BF16),
        ),
        prefetch=1,
        flops=2_500_000_000,
        limit=12,
    )
    (parcel,) = call(
        pack_kernel,
        (g_keep, came, g_bias),
        (whole((rng, 64 * az + 24, 128), BF16),),
        scratch=(
            pltpu.VMEM((rng, 64 * az + 24, 128), BF16), pltpu.SemaphoreType.DMA((rng,)),
        ),
        outside=True,
        flops=1_000_000,
    )
    parcel = lax.all_to_all(parcel, "rng", 0, 0, tiled=True)

    up = turn(g_below, 1)
    down = turn(g_above, -1)
    to_west, g_own, to_east = call(
        fold_kernel,
        (g_upper, g_lower, up, down),
        (whole((128, 512), BF16), whole((256, 512), F32), whole((128, 512), BF16)),
        flops=1_000_000,
    )
    east = shift(to_west.reshape(16, 8, width), -1)
    west = shift(to_east.reshape(16, 8, width), 1)
    (grad_tokens,) = call(
        after_kernel,
        (g_own.reshape(16, 16, width), west, east),
        (whole((16, 16, width), BF16),),
        flops=1_000_000,
    )

    (parcel,) = call(
        regroup_kernel,
        (parcel, g_own),
        (whole((az, 8, 1408), BF16),),
        flops=1_000_000,
        untouched=1,
    )
    parcel = lax.all_to_all(parcel, "az", 0, 0, tiled=True)
    (mine,) = call(total_kernel, (parcel,), (whole((8, 1408), F32),), flops=1_000_000)
    parts = lax.all_gather(mine, ("half", "core"))
    rows_qkv, rows_out, total_bias = call(
        finish_kernel,
        (parts,),
        (whole((8, 1536), F32), whole((8, 512), F32), whole((17, 8, 17), F32)),
        flops=1_000_000,
    )
    total_bias = jnp.transpose(total_bias, (1, 0, 2))
    return (grad_tokens[None], rows_qkv, rows_out, total_bias)


def solution(mesh):
    az, rng, dp = mesh.devices.shape
    split = Mesh(mesh.devices.reshape(az, rng, dp // 2, 2), ("az", "rng", "half", "core"))
    cells = P(("half", "core"), "az", "rng", None)
    rows = P(("az", "rng"), None)
    return jax.shard_map(
        shards,
        mesh=split,
        in_specs=(cells, P(), P(), P(), cells),
        out_specs=(cells, rows, rows, P()),
        check_vma=False,
    )
```
